32 devices in a mesh: row: 8 (over y, x, core), col: 4 (over z).
Axes of the slice: x: 2, y: 2, z: 4, core: 2. Of those that a mesh axis runs over, the one named last changes fastest.
Arguments:
- grid_obs: float32 [32, 2048, 512], P(None, 'row', 'col'), may hold values from -6 to 6
- grid_noise: float32 [2048, 512], P('row', 'col'), may hold values from 0.25 to 2
- station_obs: float32 [32, 8, 4, 1024], P(None, 'row', 'col'), may hold values from -6 to 6
- station_noise: float32 [8, 4, 1024], P('row', 'col'), may hold values from 0.25 to 2
- station_offset: float32 [2, 8, 4, 1024], P(None, 'row', 'col'), may hold values from 0 to 1
- station_cell: int32 [8, 4, 1024], P('row', 'col'), may hold values from 0 to 32638, as said below
- station_count: int32 [8, 4], P('row', 'col'), may hold values from 128 to 1024, as said below
- time_cov: float32 [32, 32], replicated, as said below
Outputs:
- solution_grid: float32 [32, 2048, 512], P(None, 'row', 'col')
- solution_stations: float32 [32, 8, 4, 1024], P(None, 'row', 'col')
- residual_grid: float32 [32, 2048, 512], P(None, 'row', 'col')
The draws below stay inside these ranges and needn't reach their ends.
Inputs may be any that keep to these rules, and one draw needn't show every extreme that they name: `station_cell`: cell r * 128 + c with r < 255 and c < 127, so the footprint lies in the station's tile. `station_count`: each tile holds 1024, 512, 256 or 128 stations. `time_cov`: symmetric; each diagonal entry exceeds the sum of the magnitudes of the other entries of its row.
All inputs are finite; a program needn't handle non-finite values.
Results may differ from the reference program's by a relative error of at most 0.00019.
Values sent between devices are 32-bit elements; how exact they have to be, the bound alone decides.
No kernel may reach another device: no remote copies, remote signals or barrier semaphores. Data moves between devices by JAX's collectives and lax.ppermute only.
A program may use at most 128 MiB of HBM per device.

```python
import math
import jax
import jax.numpy as jnp
from jax import lax

CX = 256
CY = 128
STEPS = 32
SLOT = 1024
REACH = 8
ITERS = 2
NX = 2048
NY = 512
N_ROW = 8
N_COL = 4


def draw_station_cell(key, part):
    first_key = jax.random.fold_in(key, 11)
    second_key = jax.random.fold_in(key, 12)
    rows_drawn = jax.random.randint(first_key, (N_ROW, N_COL, SLOT), 0, CX - 1, dtype=jnp.int32)
    cols_drawn = jax.random.randint(second_key, (N_ROW, N_COL, SLOT), 0, CY - 1, dtype=jnp.int32)
    cells = rows_drawn * CY + cols_drawn
    cells = cells.at[0, 0, 0].set(0)
    cells = cells.at[N_ROW - 1, N_COL - 1, SLOT - 1].set((CX - 2) * CY + CY - 2)
    return cells.astype(jnp.int32)


def draw_station_count(key, part):
    level_key = jax.random.fold_in(key, 21)
    pick_key = jax.random.fold_in(key, 22)
    levels = jax.random.randint(level_key, (N_ROW * N_COL,), 0, 4, dtype=jnp.int32)
    counts = SLOT // jnp.left_shift(jnp.ones_like(levels), levels)
    chosen = jax.random.randint(pick_key, (), 0, N_ROW * N_COL, dtype=jnp.int32)
    counts = counts.at[chosen].set(SLOT)
    counts = counts.at[(chosen + 1) % (N_ROW * N_COL)].set(SLOT // 8)
    return counts.reshape(N_ROW, N_COL).astype(jnp.int32)


def draw_time_cov(key, part):
    off_key = jax.random.fold_in(key, 31)
    diag_key = jax.random.fold_in(key, 32)
    spread = jax.random.uniform(off_key, (STEPS, STEPS), jnp.float32, -1.0, 1.0) / STEPS
    diagonal = jax.random.uniform(diag_key, (STEPS,), jnp.float32, 1.0, 1.5)
    symmetric = 0.5 * (spread + spread.T)
    symmetric = symmetric * (1.0 - jnp.eye(STEPS, dtype=jnp.float32))
    return (symmetric + jnp.diag(diagonal)).astype(jnp.float32)


def steps_of(key, shape, pieces, low, top_value):
    level, own = 1.0, jax.random.fold_in(key, 6)
    for dim, blocks in pieces:
        draws = jnp.exp(jax.random.uniform(jax.random.fold_in(own, dim), (blocks,), jnp.float32, low / len(pieces), top_value / len(pieces)))
        level = level * jnp.repeat(draws, shape[dim] // blocks).reshape([-1 if axis == dim else 1 for axis in range(len(shape))])
    return level


def scatter_about(own_key, dims, width, most, split=(), kind=jnp.bfloat16):
    array = width * jax.random.normal(own_key, dims, jnp.float32)
    if split:
        array = array * steps_of(own_key, dims, split, -0.22, 0.18)
    return jnp.clip(array, -most, most).astype(kind)


def setup_inputs(seed: int = 0) -> dict:
    splits = jax.random.split(jax.random.key(seed), 9)
    grid_obs = scatter_about(splits[0], (STEPS, NX, NY), 1.0, 6.0, ((1, 8), (2, 4)), jnp.float32)
    grid_noise = jnp.clip(jnp.exp(math.log(2.0) - 2.0794415 * jax.random.uniform(splits[1], (NX, NY), jnp.float32) ** steps_of(splits[1], (NX, NY), ((0, 8), (1, 4)), -0.2, 0.2)), 0.25, 2.0)
    station_obs = scatter_about(splits[2], (STEPS, N_ROW, N_COL, SLOT), 1.0, 6.0, ((1, 8), (2, 4)), jnp.float32)
    station_noise = jnp.clip(jnp.exp(math.log(2.0) - 2.0794415 * jax.random.uniform(splits[3], (N_ROW, N_COL, SLOT), jnp.float32) ** steps_of(splits[3], (N_ROW, N_COL, SLOT), ((0, 8), (1, 4)), -0.2, 0.2)), 0.25, 2.0)
    station_offset = jnp.clip(1.0 * jax.random.uniform(splits[4], (2, N_ROW, N_COL, SLOT), jnp.float32) ** steps_of(splits[4], (2, N_ROW, N_COL, SLOT), ((1, 8), (2, 4)), -0.2, 0.2), 0.0, 1.0)
    station_cell = draw_station_cell(jax.random.fold_in(splits[8], 71), 0)
    station_count = draw_station_count(jax.random.fold_in(splits[8], 71), 0)
    time_cov = draw_time_cov(jax.random.fold_in(splits[8], 71), 0)
    return dict(grid_obs=grid_obs, grid_noise=grid_noise, station_obs=station_obs, station_noise=station_noise, station_offset=station_offset, station_cell=station_cell, station_count=station_count, time_cov=time_cov)


def taper(reach):
    spread = jnp.abs(jnp.arange(-reach, reach + 1, dtype=jnp.int32)).astype(jnp.float32)
    return (1.0 - spread / (reach + 1)) * jnp.exp(-spread / 3.0)


def smooth_axis(field, weights, axis, length):
    padding = [(0, 0), (0, 0), (0, 0)]
    padding[axis] = (REACH, REACH)
    padded = jnp.pad(field, padding)
    total = jnp.zeros_like(field)
    for offset in range(2 * REACH + 1):
        total = total + weights[offset] * lax.slice_in_dim(padded, offset, offset + length, axis=1 if axis == 1 else 2)
    return total


def reference(grid_obs, grid_noise, station_obs, station_noise, station_offset, station_cell, station_count, time_cov):
    weights = taper(REACH)
    tile_row = (jnp.arange(N_ROW, dtype=jnp.int32) * CX)[:, None, None]
    tile_col = (jnp.arange(N_COL, dtype=jnp.int32) * CY)[None, :, None]
    cell_row = station_cell // CY
    cell_col = station_cell % CY
    base = ((tile_row + cell_row) * NY + tile_col + cell_col).astype(jnp.int32)
    station_indices = jnp.stack([base, base + NY, base + 1, base + NY + 1]).reshape(-1).astype(jnp.int32)
    along_row = station_offset[0]
    along_col = station_offset[1]
    footprint = jnp.stack([(1.0 - along_row) * (1.0 - along_col), along_row * (1.0 - along_col),
                           (1.0 - along_row) * along_col, along_row * along_col])
    live = (jnp.arange(SLOT, dtype=jnp.int32)[None, None, :] < station_count[:, :, None]).astype(jnp.float32)[None]

    def operate(grid_part, site_part):
        scattered = (footprint[None] * (live * site_part)[:, None]).reshape(STEPS, -1)
        merged = grid_part.reshape(STEPS, -1).at[:, station_indices].add(scattered).reshape(STEPS, NX, NY)
        temporal_shift = jnp.einsum("st,tij->sij", time_cov, merged, precision=lax.Precision.HIGHEST)
        smooth = smooth_axis(smooth_axis(temporal_shift, weights, 1, NX), weights, 2, NY)
        picked = smooth.reshape(STEPS, -1)[:, station_indices].reshape((STEPS, 4) + site_part.shape[1:])
        sampled = jnp.sum(footprint[None] * picked, axis=1)
        grid_out = 0.25 * smooth + grid_noise[None] * grid_part
        site_out = live * (0.25 * sampled + station_noise[None] * site_part) + (1.0 - live) * site_part
        return grid_out, site_out

    def inner(first, second):
        return jnp.sum(first[0] * second[0]) + jnp.sum(first[1] * second[1])

    def combine(scale, first, second):
        return (first[0] + scale * second[0], first[1] + scale * second[1])

    residual_vector = (grid_obs, live * station_obs)
    solution = (jnp.zeros_like(grid_obs), jnp.zeros_like(station_obs))
    direction = residual_vector
    norm_now = inner(residual_vector, residual_vector)
    for iteration in range(ITERS):
        image = operate(direction[0], direction[1])
        alpha = norm_now / inner(direction, image)
        solution = combine(alpha, solution, direction)
        residual_vector = combine(-alpha, residual_vector, image)
        norm_next = inner(residual_vector, residual_vector)
        direction = combine(norm_next / norm_now, residual_vector, direction)
        norm_now = norm_next
    return solution[0], solution[1], residual_vector[0]
```

```python
import functools

import jax
import jax.numpy as jnp
from jax import lax
from jax.experimental import pallas as pl
from jax.experimental.pallas import tpu as pltpu
from jax.sharding import PartitionSpec as P

REACH = 8
LANES = 128
GROUP = 8
F32 = jnp.float32
BF16 = jnp.bfloat16
HIGHEST = lax.Precision.HIGHEST


def iota(shape, dim):
    return lax.broadcasted_iota(jnp.int32, shape, dim)


def taper(distance):
    spread = jnp.abs(distance).astype(F32)
    value = (1.0 - spread / (REACH + 1)) * jnp.exp(-spread / 3.0)
    return jnp.where(jnp.abs(distance) <= REACH, value, 0.0)


def split(x):
    high = x.astype(BF16)
    return high, (x - high.astype(F32)).astype(BF16)


def pair(x):
    high, low = split(x)
    return jnp.concatenate([high, low], axis=1)


def dot(a, b):
    return jnp.dot(a, b, preferred_element_type=F32)


def dot_nt(a, b):
    return lax.dot_general(a, b, (((1,), (1,)), ((), ())), preferred_element_type=F32)


def halves(x):
    width = x.shape[1] // 2
    return x[:, :width] + x[:, width:]


def three(x):
    high = x.astype(BF16)
    rest = x - high.astype(F32)
    middle = rest.astype(BF16)
    low = (rest - middle.astype(F32)).astype(BF16)
    return jnp.concatenate([high, middle, low], axis=0)


def cut(x, axis):
    return [
        lax.slice_in_dim(x, start, start + LANES, axis=axis)
        for start in range(0, x.shape[axis], LANES)
    ]


def rows_of(g):
    return pl.ds(pl.multiple_of(g * GROUP, GROUP), GROUP)


def prepare_kernel(
    count, cell, offset, noise, obs, cov,
    sb, info, rank_out, sv, gv, ut, bounds, mix, mat, band_rows, band_cols, edge,
    table, sorted_rows,
):
    steps, slots = obs.shape
    tiles = slots // LANES
    rows = band_rows.shape[1]
    groups = rows // GROUP
    wide = steps * GROUP
    slot = iota((1, slots), 1)
    live = slot < count[0, 0]
    where_row = cell[...] // LANES
    where_col = cell[...] - where_row * LANES
    key = jnp.where(live, where_row, rows) * slots + slot
    key = key.astype(F32)
    total = jnp.zeros((1, slots), F32)
    for block in range(tiles):
        piece = key[:, block * LANES : (block + 1) * LANES]
        column = jnp.transpose(jnp.broadcast_to(piece, (LANES, LANES)))
        column = jnp.concatenate([column] * tiles, axis=1)
        less = jnp.where(column < key, 1.0, 0.0)
        total = total + jnp.sum(less, axis=0, keepdims=True)
    rank = total.astype(jnp.int32)
    rank_out[...] = rank
    lived = jnp.where(live, 1.0, 0.0)
    table[pl.ds(0, steps), :] = obs[...] * lived
    table[pl.ds(steps, 1), :] = where_row.astype(F32)
    table[pl.ds(steps + 1, 1), :] = where_col.astype(F32)
    table[pl.ds(steps + 2, 1), :] = offset[0:1, :]
    table[pl.ds(steps + 3, 1), :] = offset[1:2, :]
    table[pl.ds(steps + 4, 1), :] = noise[...]
    table[pl.ds(steps + 5, 1), :] = lived
    table[pl.ds(steps + 6, 2), :] = jnp.zeros((2, slots), F32)
    pieces = three(table[...])
    height = table.shape[0]

    def sort_block(block, carry):
        start = pl.multiple_of(block * LANES, LANES)
        order = (iota((LANES, slots), 0) + start == rank).astype(F32).astype(BF16)
        out = dot_nt(pieces, order)
        sorted_rows[:, pl.ds(start, LANES)] = (
            out[:height] + out[height : 2 * height] + out[2 * height :]
        )
        return carry

    lax.fori_loop(0, tiles, sort_block, 0)
    ordered_row = sorted_rows[pl.ds(steps, 1), :]
    ordered_live = sorted_rows[pl.ds(steps + 5, 1), :]
    first_row = (iota((groups, slots), 0) * GROUP).astype(F32)
    before = jnp.where(ordered_row < first_row - 1.0, ordered_live, 0.0)
    until = jnp.where(ordered_row < first_row + GROUP, ordered_live, 0.0)
    low = jnp.sum(before, axis=1, keepdims=True)
    high = jnp.sum(until, axis=1, keepdims=True)
    start_tile = jnp.where(high > low, jnp.floor(low * (1.0 / LANES)), float(tiles))
    stop_tile = jnp.where(high > low, jnp.floor((high - 1.0) * (1.0 / LANES)) + 1.0, 0.0)
    lane = iota((groups, LANES), 1)
    bounds[...] = jnp.where(lane == 0, start_tile, stop_tile).astype(jnp.int32)
    for block in range(tiles + 2):
        if block >= tiles:
            sb[block] = jnp.zeros((steps, GROUP, LANES), F32)
            info[:, block] = jnp.zeros((2, GROUP, LANES), F32)
            sv[block] = jnp.zeros((2 * LANES, 2 * LANES), BF16)
            gv[block] = jnp.zeros((2 * LANES, 2 * LANES), BF16)
            ut[block] = jnp.zeros((rows, LANES), F32)
            continue
        lanes = pl.ds(block * LANES, LANES)
        at_row = sorted_rows[pl.ds(steps, 1), lanes].astype(jnp.int32)
        at_col = sorted_rows[pl.ds(steps + 1, 1), lanes].astype(jnp.int32)
        along_row = sorted_rows[pl.ds(steps + 2, 1), lanes]
        along_col = sorted_rows[pl.ds(steps + 3, 1), lanes]
        row = iota((rows, LANES), 0)
        ut[block] = jnp.where(row == at_row, 1.0 - along_row, 0.0) + jnp.where(
            row == at_row + 1, along_row, 0.0
        )
        col = iota((LANES, LANES), 0)
        across = jnp.where(col == at_col, 1.0 - along_col, 0.0) + jnp.where(
            col == at_col + 1, along_col, 0.0
        )
        for target, weight in ((gv, across), (sv, jnp.transpose(across))):
            high_part, low_part = split(weight)
            target[block] = jnp.concatenate(
                [
                    jnp.concatenate([high_part, low_part], axis=1),
                    jnp.concatenate([high_part, jnp.zeros_like(low_part)], axis=1),
                ],
                axis=0,
            )
        info[0, block] = jnp.broadcast_to(
            sorted_rows[pl.ds(steps + 4, 1), lanes], (GROUP, LANES)
        )
        info[1, block] = jnp.broadcast_to(
            sorted_rows[pl.ds(steps + 5, 1), lanes], (GROUP, LANES)
        )
        for step in range(steps):
            sb[block, step] = jnp.broadcast_to(
                sorted_rows[pl.ds(step, 1), lanes], (GROUP, LANES)
            )
    spread = (iota((wide, steps), 0) // GROUP == iota((wide, steps), 1)).astype(F32)
    spread_t = (iota((steps, wide), 1) // GROUP == iota((steps, wide), 0)).astype(F32)
    expanded = jnp.dot(
        jnp.dot(spread, cov[...], precision=HIGHEST, preferred_element_type=F32),
        spread_t,
        precision=HIGHEST,
        preferred_element_type=F32,
    )
    a = iota((wide, wide), 0)
    b = iota((wide, wide), 1)
    same = (a % GROUP) == (b % GROUP)
    mix[0], mix[1] = split(jnp.where(same, expanded, 0.0))
    near = taper((b % GROUP) + REACH - (a % GROUP)) * expanded
    near = jnp.concatenate(
        [jnp.concatenate([x[GROUP:], x[:GROUP]], axis=0) for x in cut(near, 0)], axis=0
    )
    mat[0], mat[1] = split(near)
    far = taper(REACH + (a % GROUP) - (b % GROUP)) * expanded
    far = jnp.concatenate(
        [pltpu.roll(x, LANES - GROUP, 1) for x in cut(far, 1)], axis=1
    )
    mat[2], mat[3] = split(far)
    ra = iota((rows, rows), 0)
    rb = iota((rows, rows), 1)
    band_rows[0], band_rows[1] = split(0.25 * taper(ra - rb))
    ca = iota((LANES, LANES), 0)
    cb = iota((LANES, LANES), 1)
    high_part, low_part = split(taper(ca - cb))
    band_cols[...] = jnp.concatenate(
        [
            jnp.concatenate([high_part, low_part], axis=1),
            jnp.concatenate([high_part, jnp.zeros_like(low_part)], axis=1),
        ],
        axis=0,
    )
    block_same = (a // GROUP) == (b // GROUP)
    above = 0.25 * taper((a % GROUP) + REACH - (b % GROUP))
    below = 0.25 * taper(REACH + (b % GROUP) - (a % GROUP))
    edge[0], edge[1] = split(jnp.where(block_same, above, 0.0))
    edge[2], edge[3] = split(jnp.where(block_same, below, 0.0))


def scatter_group(g, base, z, sb, ut, sv, bounds):
    steps = base.shape[0]
    flat = (steps * GROUP, LANES)
    first = bounds[g, 0]

    def tile(index):
        scaled = (sb[index] * ut[index, rows_of(g), :][None]).reshape(flat)
        return dot(pair(scaled), sv[index])

    out = halves(tile(first) + tile(first + 1))
    z[:, rows_of(g), :] = base[:, rows_of(g), :] + out.reshape(steps, GROUP, LANES)

    @pl.when(bounds[g, 1] > first + 2)
    def _():
        def more(index, carry):
            z[:, rows_of(g), :] += halves(tile(index)).reshape(steps, GROUP, LANES)
            return carry

        lax.fori_loop(first + 2, bounds[g, 1], more, 0)


def pack_group(g, z, strips):
    steps = z.shape[0]
    per = LANES // GROUP
    slot = iota((GROUP, LANES), 1) // GROUP
    for half in range(steps // per):
        left = jnp.zeros((GROUP, LANES), F32)
        right = jnp.zeros((GROUP, LANES), F32)
        for local in range(per):
            value = z[half * per + local, rows_of(g), :]
            if local:
                value = pltpu.roll(value, local * GROUP, 1)
            left = jnp.where(slot == local, value, left)
            right = jnp.where(slot == (local - 1) % per, value, right)
        lanes = pl.ds(half * LANES, LANES)
        strips[0, rows_of(g), lanes] = left
        strips[1, rows_of(g), lanes] = right


def unpack(left, right, step):
    per = LANES // GROUP
    half, local = step // per, step % per
    lane = iota((GROUP, LANES), 1)
    slot = lane // GROUP
    lanes = slice(half * LANES, (half + 1) * LANES)
    both = jnp.where(slot == local, left[:, lanes], right[:, lanes])
    if local:
        both = pltpu.roll(both, LANES - local * GROUP, 1)
    return jnp.where((lane < GROUP) | (lane >= LANES - GROUP), both, 0.0)


def scatter_all(base, z, strips, sb, ut, sv, bounds):
    groups = base.shape[1] // GROUP

    def run(g, carry):
        scatter_group(g, base, z, sb, ut, sv, bounds)
        pack_group(g, z, strips)
        return carry

    lax.fori_loop(0, groups, run, 0)


def scatter_kernel(bounds, base, sb, ut, sv, z, strips):
    scatter_all(base, z, strips, sb, ut, sv, bounds)


def filter_kernel(z, mix, band_rows, band_cols, w, u_edges, u):
    steps, rows, cols = z.shape
    groups = rows // GROUP
    flat = (steps * GROUP, LANES)

    def first(g, carry):
        value = z[:, rows_of(g), :].reshape(flat)
        across = halves(dot(pair(value), band_cols[...]))
        both = pair(across)
        mixed = halves(dot(mix[0], both)) + dot(mix[1], both[:, :LANES])
        u[:, rows_of(g), :] = mixed.reshape(steps, GROUP, LANES)
        return carry

    lax.fori_loop(0, groups, first, 0, unroll=2)
    u_edges[0] = u[:, pl.ds(0, GROUP), :]
    u_edges[1] = u[:, pl.ds(rows - GROUP, GROUP), :]

    def second(pairs, carry):
        one = pair(u[2 * pairs])
        two = pair(u[2 * pairs + 1])
        low = dot(band_rows[1], jnp.concatenate([one[:, :LANES], two[:, :LANES]], axis=1))
        w[2 * pairs] = halves(dot(band_rows[0], one)) + low[:, :LANES]
        w[2 * pairs + 1] = halves(dot(band_rows[0], two)) + low[:, LANES:]
        return carry

    lax.fori_loop(0, steps // 2, second, 0)


def edge_kernel(from_left, from_right, u_edges, mat, band_rows, sides, full_edges):
    steps = u_edges.shape[1]
    rows = from_left.shape[0]
    for side, source in ((0, from_left), (1, from_right)):
        high, low = split(source[...])
        value = dot(high, mat[2 * side]) + dot(low, mat[2 * side])
        value = value + dot(high, mat[2 * side + 1])
        sides[side] = value
    for which, start in ((0, 0), (1, rows - GROUP)):
        left = sides[0, pl.ds(start, GROUP), :]
        right = sides[1, pl.ds(start, GROUP), :]
        for step in range(steps):
            full_edges[which, step] = u_edges[which, step] + unpack(left, right, step)
    for side in range(2):
        high, low = split(sides[side])
        sides[side] = (
            dot(band_rows[0], high) + dot(band_rows[0], low) + dot(band_rows[1], high)
        )


def add_sides_kernel(w_in, sides, w):
    steps, rows, _ = w.shape

    def run(g, carry):
        left = sides[0, rows_of(g), :]
        right = sides[1, rows_of(g), :]
        for step in range(steps):
            w[step, rows_of(g), :] = w_in[step, rows_of(g), :] + unpack(left, right, step)
        return carry

    lax.fori_loop(0, rows // GROUP, run, 0)


def fill_extra(extra, above, below, edge):
    steps = above.shape[0]
    flat = (steps * GROUP, LANES)
    for which, source in ((0, above), (1, below)):
        both = pair(source[...].reshape(flat))
        value = halves(dot(edge[2 * which], both)) + dot(edge[2 * which + 1], both[:, :LANES])
        extra[which] = value.reshape(steps, GROUP, LANES)
    extra[2] = jnp.zeros((steps, GROUP, LANES), F32)


def gather_group(g, value, acc, ut, gv, bounds):
    steps = value.shape[0]
    both = pair(value.reshape(steps * GROUP, LANES))
    first = bounds[g, 0]

    def add(index):
        out = halves(dot(both, gv[index])).reshape(steps, GROUP, LANES)
        acc[index] += out * ut[index, rows_of(g), :][None]

    add(first)
    add(first + 1)

    @pl.when(bounds[g, 1] > first + 2)
    def _():
        def more(index, carry):
            add(index)
            return carry

        lax.fori_loop(first + 2, bounds[g, 1], more, 0)


def whole(x):
    return jnp.sum(jnp.sum(x, axis=1, keepdims=True), axis=0, keepdims=True)


def image_pass(w, extra, noise, field, out, acc, ut, gv, bounds, terms, sums):
    steps, rows, _ = w.shape
    groups = rows // GROUP
    acc[...] = jnp.zeros_like(acc)

    def run(g, carry):
        which = jnp.where(g == 0, 0, jnp.where(g == groups - 1, 1, 2))
        value = w[:, rows_of(g), :] + extra[which]
        mine = field[:, rows_of(g), :]
        image = value + noise[rows_of(g), :][None] * mine
        out[:, rows_of(g), :] = image
        gather_group(g, value, acc, ut, gv, bounds)
        return tuple(c + t for c, t in zip(carry, terms(g, mine, image)))

    return lax.fori_loop(0, groups, run, sums)


def image_stations(index, acc, info, field):
    sampled = jnp.sum(acc[index], axis=1, keepdims=True)
    mine = field[index]
    live = info[1, index][None]
    return live * (sampled + info[0, index][None] * mine) + (1.0 - live) * mine


def image_one_kernel(
    bounds, w, above, below, edge, noise, b, sb, info, ut, gv, sv, rank,
    p, ps, z, strips, sums, unsorted, acc, extra, flat_rows,
):
    steps, rows, _ = w.shape
    tiles = sb.shape[0] - 2
    slots = tiles * LANES
    fill_extra(extra, above, below, edge)

    def fold(x, y):
        return jnp.sum(x * y, axis=0)

    def terms(g, mine, image):
        return fold(mine, mine), fold(mine, image), fold(image, image)

    zero = jnp.zeros((GROUP, LANES), F32)
    grid_sums = image_pass(w, extra, noise, b, p, acc, ut, gv, bounds, terms, (zero,) * 3)

    def stations(index, carry):
        image = image_stations(index, acc, info, sb)
        ps[index] = image
        for step in range(steps):
            flat_rows[pl.ds(step, 1), pl.ds(pl.multiple_of(index * LANES, LANES), LANES)] = image[step, 0:1]
        mine = sb[index]
        return tuple(c + (1.0 / GROUP) * t for c, t in zip(carry, terms(0, mine, image)))

    both = lax.fori_loop(0, tiles, stations, grid_sums)
    ps[tiles] = jnp.zeros((steps, GROUP, LANES), F32)
    ps[tiles + 1] = jnp.zeros((steps, GROUP, LANES), F32)
    bb, bp, pp = (whole(x) for x in both)
    lane = iota((GROUP, LANES), 1)
    value = jnp.where(lane == 0, bb / bp, 0.0)
    value = jnp.where(lane == 1, bb, value)
    value = jnp.where(lane == 2, bp, value)
    value = jnp.where(lane == 3, pp, value)
    sums[...] = value
    scatter_all(p, z, strips, ps, ut, sv, bounds)
    pieces = three(flat_rows[...])

    def unsort_block(block, carry):
        start = pl.multiple_of(block * LANES, LANES)
        order = (iota((slots, LANES), 0) == rank[:, pl.ds(start, LANES)]).astype(F32).astype(BF16)
        out = dot(pieces, order)
        unsorted[:, pl.ds(start, LANES)] = (
            out[:steps] + out[steps : 2 * steps] + out[2 * steps :]
        )
        return carry

    lax.fori_loop(0, tiles, unsort_block, 0)


def image_two_kernel(
    bounds, w, above, below, edge, noise, b, p, sb, ps, info, ut, gv, sums,
    q, message, acc, extra,
):
    steps, rows, _ = w.shape
    tiles = sb.shape[0] - 2
    fill_extra(extra, above, below, edge)
    shift = sums[0:1, 0:1]

    def fold(x, y):
        return jnp.sum(x * y, axis=0)

    def products(first, mine, image):
        residual = first - shift[None] * mine
        moved = mine - shift[None] * image
        return fold(residual, residual), fold(residual, moved), fold(mine, image), fold(residual, image)

    def terms(g, mine, image):
        return products(b[:, rows_of(g), :], mine, image)

    zero = jnp.zeros((GROUP, LANES), F32)
    grid_sums = image_pass(w, extra, noise, p, q, acc, ut, gv, bounds, terms, (zero,) * 4)

    def stations(index, carry):
        image = image_stations(index, acc, info, ps)
        new = products(sb[index], ps[index], image)
        return tuple(c + (1.0 / GROUP) * t for c, t in zip(carry, new))

    both = lax.fori_loop(0, tiles, stations, grid_sums)
    lane = iota((1, LANES), 1)
    value = jnp.where(lane < 4, sums[0:1, :], 0.0)
    for place, x in enumerate(both):
        value = jnp.where(lane == 4 + place, whole(x), value)
    message[...] = jnp.broadcast_to(value, message.shape)


def final_kernel(received, b, p, q, obs, unsorted, count, solution_out, residual_out, station_out):
    everything = received[...]

    def column(index):
        return everything[:, index : index + 1]

    def total(x):
        return jnp.sum(x, axis=0, keepdims=True)

    shift, bb, bp, pp = (column(i) for i in range(4))
    rr, ru, pq, rq = (column(i) for i in range(4, 8))
    norm = total(bb)
    alpha = norm / total(bp)
    delta = shift - alpha
    rp = bp - shift * pp
    pu = pp - shift * pq
    norm_next = total(rr + 2.0 * delta * rp + delta * delta * pp)
    energy = total(ru + delta * (rq + pu) + delta * delta * pq)
    beta = norm_next / norm
    alpha_next = norm_next / (energy - beta * norm_next / alpha)
    along = alpha + alpha_next * (1.0 + beta)
    twice = alpha_next * alpha
    first = b[...]
    second = p[...]
    solution_out[...] = along[None] * first - twice[None] * second
    residual_out[...] = first - along[None] * second + twice[None] * q[...]

    @pl.when(pl.program_id(0) == 0)
    def _():
        steps, slots = obs.shape
        live = iota((steps, slots), 1) < count[0, 0]
        own = jnp.where(live, obs[...], 0.0)
        station_out[...] = along * own - twice * unsorted[...]


VMEM = pl.BlockSpec(memory_space=pltpu.VMEM)
SMEM = pl.BlockSpec(memory_space=pltpu.SMEM)


def call(kernel, outs, ins, operands, scratch=(), flops=10**9, moved=10**7, limit=40, **extra):
    return pl.pallas_call(
        kernel,
        out_shape=outs,
        in_specs=ins,
        out_specs=[VMEM] * len(outs),
        scratch_shapes=list(scratch),
        compiler_params=pltpu.CompilerParams(vmem_limit_bytes=limit * 2**20),
        cost_estimate=pl.CostEstimate(flops=flops, bytes_accessed=moved, transcendentals=0),
        **extra,
    )(*operands)


def exchange(first, second, axis):
    count = lax.axis_size(axis)
    forward = [(i, i + 1) for i in range(count - 1)]
    backward = [(target, source) for source, target in forward]
    return lax.ppermute(first, axis, forward), lax.ppermute(second, axis, backward)


def body(
    grid_obs, grid_noise, station_obs, station_noise, station_offset, station_cell,
    station_count, time_cov,
):
    steps, rows, cols = grid_obs.shape
    slots = station_obs.shape[3]
    tiles = slots // LANES
    wide = steps * GROUP
    groups = rows // GROUP
    devices = lax.axis_size("row") * lax.axis_size("col")
    obs = station_obs.reshape(steps, slots)
    shape = jax.ShapeDtypeStruct
    field = shape((steps, rows, cols), F32)
    rim = shape((2, steps, GROUP, cols), F32)
    strips_shape = shape((2, rows, wide), F32)
    sb, info, rank, sv, gv, ut, bounds, mix, mat, band_rows, band_cols, edge = call(
        prepare_kernel,
        [
            shape((tiles + 2, steps, GROUP, LANES), F32),
            shape((2, tiles + 2, GROUP, LANES), F32),
            shape((1, slots), jnp.int32),
            shape((tiles + 2, 2 * LANES, 2 * LANES), BF16),
            shape((tiles + 2, 2 * LANES, 2 * LANES), BF16),
            shape((tiles + 2, rows, LANES), F32),
            shape((groups, LANES), jnp.int32),
            shape((2, wide, wide), BF16),
            shape((4, wide, wide), BF16),
            shape((2, rows, rows), BF16),
            shape((2 * LANES, 2 * LANES), BF16),
            shape((4, wide, wide), BF16),
        ],
        [SMEM] + [VMEM] * 5,
        (
            station_count,
            station_cell.reshape(1, slots),
            station_offset.reshape(2, slots),
            station_noise.reshape(1, slots),
            obs,
            time_cov,
        ),
        [pltpu.VMEM((steps + 8, slots), F32), pltpu.VMEM((steps + 8, slots), F32)],
    )
    z, strips = call(
        scatter_kernel,
        [field, strips_shape],
        [SMEM] + [VMEM] * 4,
        (bounds, grid_obs, sb, ut, sv),
    )

    def smooth(z, strips):
        from_left, from_right = exchange(strips[1], strips[0], "col")
        w, u_edges = call(
            filter_kernel,
            [field, rim],
            [VMEM] * 4,
            (z, mix, band_rows, band_cols),
            [pltpu.VMEM((steps, rows, cols), F32)],
        )
        sides, full_edges = call(
            edge_kernel,
            [strips_shape, rim],
            [VMEM] * 5,
            (from_left, from_right, u_edges, mat, band_rows),
        )
        above, below = exchange(full_edges[1], full_edges[0], "row")
        (w,) = call(add_sides_kernel, [field], [VMEM] * 2, (w, sides), input_output_aliases={0: 0})
        return w, above, below

    w, above, below = smooth(z, strips)
    station_field = shape((tiles + 2, steps, GROUP, LANES), F32)
    p, ps, z, strips, sums, unsorted = call(
        image_one_kernel,
        [field, station_field, field, strips_shape, shape((GROUP, LANES), F32), shape((steps, slots), F32)],
        [SMEM] + [VMEM] * 12,
        (bounds, w, above, below, edge, grid_noise, grid_obs, sb, info, ut, gv, sv, rank),
        [
            pltpu.VMEM((tiles + 2, steps, GROUP, LANES), F32),
            pltpu.VMEM((3, steps, GROUP, LANES), F32),
            pltpu.VMEM((steps, slots), F32),
        ],
    )
    w, above, below = smooth(z, strips)
    q, message = call(
        image_two_kernel,
        [field, shape((devices, LANES), F32)],
        [SMEM] + [VMEM] * 13,
        (bounds, w, above, below, edge, grid_noise, grid_obs, p, sb, ps, info, ut, gv, sums),
        [
            pltpu.VMEM((tiles + 2, steps, GROUP, LANES), F32),
            pltpu.VMEM((3, steps, GROUP, LANES), F32),
        ],
    )
    received = lax.all_to_all(message, ("row", "col"), 0, 0, tiled=True)
    parts = 8
    block = pl.BlockSpec((steps // parts, rows, cols), lambda i: (i, 0, 0))
    fixed = lambda dims: pl.BlockSpec(dims, lambda i: (0,) * len(dims))
    solution_grid, residual_grid, solution_stations = pl.pallas_call(
        final_kernel,
        grid=(parts,),
        out_shape=[field, field, shape((steps, slots), F32)],
        in_specs=[
            fixed((devices, LANES)), block, block, block, fixed((steps, slots)), fixed((steps, slots)), SMEM,
        ],
        out_specs=[block, block, fixed((steps, slots))],
        compiler_params=pltpu.CompilerParams(vmem_limit_bytes=20 * 2**20),
    )(received, grid_obs, p, q, obs, unsorted, station_count)
    return solution_grid, solution_stations.reshape(steps, 1, 1, slots), residual_grid


def solution(mesh):
    placed = (
        P(None, "row", "col"),
        P("row", "col"),
        P(None, "row", "col", None),
        P("row", "col", None),
        P(None, "row", "col", None),
        P("row", "col", None),
        P("row", "col"),
        P(),
    )
    return jax.shard_map(
        body,
        mesh=mesh,
        in_specs=placed,
        out_specs=(P(None, "row", "col"), P(None, "row", "col", None), P(None, "row", "col")),
        check_vma=False,
    )
```

```python
import functools

import jax
import jax.numpy as jnp
from jax import lax
from jax.experimental import pallas as pl
from jax.experimental.pallas import tpu as pltpu
from jax.sharding import PartitionSpec as P

REACH = 8
LANES = 128
GROUP = 8
F32 = jnp.float32
BF16 = jnp.bfloat16
HIGHEST = lax.Precision.HIGHEST


def iota(shape, dim):
    return lax.broadcasted_iota(jnp.int32, shape, dim)


def taper(distance):
    spread = jnp.abs(distance).astype(F32)
    value = (1.0 - spread / (REACH + 1)) * jnp.exp(-spread / 3.0)
    return jnp.where(jnp.abs(distance) <= REACH, value, 0.0)


def split(x):
    high = x.astype(BF16)
    return high, (x - high.astype(F32)).astype(BF16)


def pair(x):
    high, low = split(x)
    return jnp.concatenate([high, low], axis=1)


def dot(a, b):
    return jnp.dot(a, b, preferred_element_type=F32)


def dot_nt(a, b):
    return lax.dot_general(a, b, (((1,), (1,)), ((), ())), preferred_element_type=F32)


def halves(x):
    width = x.shape[1] // 2
    return x[:, :width] + x[:, width:]


def three(x):
    high = x.astype(BF16)
    rest = x - high.astype(F32)
    middle = rest.astype(BF16)
    low = (rest - middle.astype(F32)).astype(BF16)
    return jnp.concatenate([high, middle, low], axis=0)


def cut(x, axis):
    return [
        lax.slice_in_dim(x, start, start + LANES, axis=axis)
        for start in range(0, x.shape[axis], LANES)
    ]


def rows_of(g):
    return pl.ds(pl.multiple_of(g * GROUP, GROUP), GROUP)


def prepare_kernel(
    count, cell, offset, noise, obs, cov,
    sb, info, rank_out, sv, gv, ut, bounds, mix, mat, band_rows, band_cols, edge,
    table, sorted_rows,
):
    steps, slots = obs.shape
    tiles = slots // LANES
    rows = band_rows.shape[0]
    groups = rows // GROUP
    wide = steps * GROUP
    slot = iota((1, slots), 1)
    live = slot < count[0, 0]
    where_row = cell[...] // LANES
    where_col = cell[...] - where_row * LANES
    key = jnp.where(live, where_row, rows) * slots + slot
    key = key.astype(F32)
    total = jnp.zeros((1, slots), F32)
    for block in range(tiles):
        piece = key[:, block * LANES : (block + 1) * LANES]
        column = jnp.transpose(jnp.broadcast_to(piece, (LANES, LANES)))
        column = jnp.concatenate([column] * tiles, axis=1)
        less = jnp.where(column < key, 1.0, 0.0)
        total = total + jnp.sum(less, axis=0, keepdims=True)
    rank = total.astype(jnp.int32)
    rank_out[...] = rank
    lived = jnp.where(live, 1.0, 0.0)
    table[pl.ds(0, steps), :] = obs[...] * lived
    table[pl.ds(steps, 1), :] = where_row.astype(F32)
    table[pl.ds(steps + 1, 1), :] = where_col.astype(F32)
    table[pl.ds(steps + 2, 1), :] = offset[0:1, :]
    table[pl.ds(steps + 3, 1), :] = offset[1:2, :]
    table[pl.ds(steps + 4, 1), :] = noise[...]
    table[pl.ds(steps + 5, 1), :] = lived
    table[pl.ds(steps + 6, 2), :] = jnp.zeros((2, slots), F32)
    pieces = three(table[...])
    height = table.shape[0]

    def sort_block(block, carry):
        start = pl.multiple_of(block * LANES, LANES)
        order = (iota((LANES, slots), 0) + start == rank).astype(F32).astype(BF16)
        out = dot_nt(pieces, order)
        sorted_rows[:, pl.ds(start, LANES)] = (
            out[:height] + out[height : 2 * height] + out[2 * height :]
        )
        return carry

    lax.fori_loop(0, tiles, sort_block, 0)
    ordered_row = sorted_rows[pl.ds(steps, 1), :]
    ordered_live = sorted_rows[pl.ds(steps + 5, 1), :]
    first_row = (iota((groups, slots), 0) * GROUP).astype(F32)
    before = jnp.where(ordered_row < first_row - 1.0, ordered_live, 0.0)
    until = jnp.where(ordered_row < first_row + GROUP, ordered_live, 0.0)
    low = jnp.sum(before, axis=1, keepdims=True)
    high = jnp.sum(until, axis=1, keepdims=True)
    start_tile = jnp.where(high > low, jnp.floor(low * (1.0 / LANES)), float(tiles))
    stop_tile = jnp.where(high > low, jnp.floor((high - 1.0) * (1.0 / LANES)) + 1.0, 0.0)
    lane = iota((groups, LANES), 1)
    span = jnp.max(stop_tile - start_tile, axis=0, keepdims=True)
    bounds[...] = jnp.where(
        lane == 0, start_tile, jnp.where(lane == 1, stop_tile, span)
    ).astype(jnp.int32)
    extra = pl.ds(slots, 2 * LANES)
    sb[:, :, extra] = jnp.zeros((steps, GROUP, 2 * LANES), F32)
    info[:, :, extra] = jnp.zeros((2, GROUP, 2 * LANES), F32)
    sv[:, extra, :] = jnp.zeros((2, 2 * LANES, 2 * LANES), BF16)
    gv[:, extra] = jnp.zeros((3 * LANES, 2 * LANES), BF16)
    ut[:, extra] = jnp.zeros((rows, 2 * LANES), F32)
    for block in range(tiles):
        lanes = pl.ds(block * LANES, LANES)
        at_row = sorted_rows[pl.ds(steps, 1), lanes].astype(jnp.int32)
        at_col = sorted_rows[pl.ds(steps + 1, 1), lanes].astype(jnp.int32)
        along_row = sorted_rows[pl.ds(steps + 2, 1), lanes]
        along_col = sorted_rows[pl.ds(steps + 3, 1), lanes]
        row = iota((rows, LANES), 0)
        ut[:, lanes] = jnp.where(row == at_row, 1.0 - along_row, 0.0) + jnp.where(
            row == at_row + 1, along_row, 0.0
        )
        col = iota((LANES, LANES), 0)
        across = jnp.where(col == at_col, 1.0 - along_col, 0.0) + jnp.where(
            col == at_col + 1, along_col, 0.0
        )
        high_part, low_part = split(across)
        gv[:, lanes] = jnp.concatenate([high_part, high_part, low_part], axis=0)
        high_part, low_part = split(jnp.transpose(across))
        sv[0, lanes, :] = jnp.concatenate([high_part, low_part], axis=1)
        sv[1, lanes, :] = jnp.concatenate([high_part, jnp.zeros_like(low_part)], axis=1)
        for place in range(2):
            info[place, :, lanes] = jnp.broadcast_to(
                sorted_rows[pl.ds(steps + 4 + place, 1), lanes], (GROUP, LANES)
            )
        for step in range(steps):
            sb[step, :, lanes] = jnp.broadcast_to(
                sorted_rows[pl.ds(step, 1), lanes], (GROUP, LANES)
            )
    spread = (iota((wide, steps), 0) // GROUP == iota((wide, steps), 1)).astype(F32)
    spread_t = (iota((steps, wide), 1) // GROUP == iota((steps, wide), 0)).astype(F32)
    expanded = jnp.dot(
        jnp.dot(spread, cov[...], precision=HIGHEST, preferred_element_type=F32),
        spread_t,
        precision=HIGHEST,
        preferred_element_type=F32,
    )
    a = iota((wide, wide), 0)
    b = iota((wide, wide), 1)
    same = (a % GROUP) == (b % GROUP)
    high_part, low_part = split(jnp.where(same, expanded, 0.0))
    mix[...] = jnp.concatenate([high_part, high_part, low_part], axis=1)
    near = taper((b % GROUP) + REACH - (a % GROUP)) * expanded
    near = jnp.concatenate(
        [jnp.concatenate([x[GROUP:], x[:GROUP]], axis=0) for x in cut(near, 0)], axis=0
    )
    mat[0], mat[1] = split(near)
    far = taper(REACH + (a % GROUP) - (b % GROUP)) * expanded
    far = jnp.concatenate(
        [pltpu.roll(x, LANES - GROUP, 1) for x in cut(far, 1)], axis=1
    )
    mat[2], mat[3] = split(far)
    ra = iota((rows, rows), 0)
    rb = iota((rows, rows), 1)
    high_part, low_part = split(0.25 * taper(ra - rb))
    band_rows[...] = jnp.concatenate([high_part, high_part, low_part], axis=1)
    ca = iota((LANES, LANES), 0)
    cb = iota((LANES, LANES), 1)
    high_part, low_part = split(taper(ca - cb))
    band_cols[...] = jnp.concatenate(
        [
            jnp.concatenate([high_part, low_part], axis=1),
            jnp.concatenate([high_part, jnp.zeros_like(low_part)], axis=1),
        ],
        axis=0,
    )
    block_same = (a // GROUP) == (b // GROUP)
    above = 0.25 * taper((a % GROUP) + REACH - (b % GROUP))
    below = 0.25 * taper(REACH + (b % GROUP) - (a % GROUP))
    edge[0], edge[1] = split(jnp.where(block_same, above, 0.0))
    edge[2], edge[3] = split(jnp.where(block_same, below, 0.0))


def tile_lanes(index, count):
    return pl.ds(pl.multiple_of(index * LANES, LANES), count * LANES)


def spread_tiles(g, first, count, sb, ut, sv):
    steps = sb.shape[0]
    lanes = tile_lanes(first, count)
    scaled = sb[:, :, lanes] * ut[rows_of(g), lanes][None]
    left = pair(scaled.reshape(steps * GROUP, count * LANES))
    right = jnp.concatenate([sv[0, lanes, :], sv[1, lanes, :]], axis=0)
    return halves(dot(left, right)).reshape(steps, GROUP, LANES)


def scatter_all(base, z, strips, sb, ut, sv, bounds):
    groups = base.shape[1] // GROUP

    def run(g, carry):
        z[:, rows_of(g), :] = base[:, rows_of(g), :] + spread_tiles(g, bounds[g, 0], 2, sb, ut, sv)
        return carry

    lax.fori_loop(0, groups, run, 0, unroll=2)

    @pl.when(bounds[0, 2] > 2)
    def _():
        def crowded(g, carry):
            def more(index, inner):
                z[:, rows_of(g), :] += spread_tiles(g, index, 1, sb, ut, sv)
                return inner

            return lax.fori_loop(bounds[g, 0] + 2, bounds[g, 1], more, carry)

        lax.fori_loop(0, groups, crowded, 0)

    def pack(g, carry):
        pack_group(g, z, strips)
        return carry

    lax.fori_loop(0, groups, pack, 0, unroll=2)


def pack_group(g, z, strips):
    steps = z.shape[0]
    per = LANES // GROUP
    slot = iota((GROUP, LANES), 1) // GROUP
    for half in range(steps // per):
        left = jnp.zeros((GROUP, LANES), F32)
        right = jnp.zeros((GROUP, LANES), F32)
        for local in range(per):
            value = z[half * per + local, rows_of(g), :]
            if local:
                value = pltpu.roll(value, local * GROUP, 1)
            left = jnp.where(slot == local, value, left)
            right = jnp.where(slot == (local - 1) % per, value, right)
        lanes = pl.ds(half * LANES, LANES)
        strips[0, rows_of(g), lanes] = left
        strips[1, rows_of(g), lanes] = right


def unpack(sides, where_rows, count, step):
    per = LANES // GROUP
    half, local = step // per, step % per
    lane = iota((count, LANES), 1)
    lanes = pl.ds(half * LANES, LANES) if isinstance(step, int) else tile_lanes(half, 1)
    both = jnp.where(lane // GROUP == local, sides[0, where_rows, lanes], sides[1, where_rows, lanes])
    both = pltpu.roll(both, (LANES - local * GROUP) % LANES, 1)
    return jnp.where((lane < GROUP) | (lane >= LANES - GROUP), both, 0.0)


def scatter_kernel(bounds, base, sb, ut, sv, z, strips):
    scatter_all(base, z, strips, sb, ut, sv, bounds)


def first_filter_kernel(z, mix, band_cols, u, u_edges, y):
    steps, rows, cols = z.shape
    groups = rows // GROUP
    flat = (steps * GROUP, LANES)

    def across(quad, carry):
        parts = [z[:, rows_of(4 * quad + i), :].reshape(flat) for i in range(4)]
        value = halves(dot(pair(jnp.concatenate(parts, axis=0)), band_cols[...]))
        both = split(value)
        for i in range(4):
            for part in range(2):
                y[2 * quad + i // 2, part, :, pl.ds((i % 2) * LANES, LANES)] = both[part][
                    i * flat[0] : (i + 1) * flat[0]
                ]
        return carry

    lax.fori_loop(0, groups // 4, across, 0)

    def mixing(two, carry):
        right = jnp.concatenate([y[two, 0], y[two, 1], y[two, 0]], axis=0)
        out = dot(mix[...], right)
        u[:, rows_of(2 * two), :] = out[:, :LANES].reshape(steps, GROUP, LANES)
        u[:, rows_of(2 * two + 1), :] = out[:, LANES:].reshape(steps, GROUP, LANES)
        return carry

    lax.fori_loop(0, groups // 2, mixing, 0, unroll=2)
    u_edges[0] = u[:, pl.ds(0, GROUP), :]
    u_edges[1] = u[:, pl.ds(rows - GROUP, GROUP), :]


def second_filter_kernel(u, sides, band_rows, w):
    steps, rows, cols = u.shape

    def along(two, carry):
        one = split(u[2 * two])
        other = split(u[2 * two + 1])
        high = jnp.concatenate([one[0], other[0]], axis=1)
        low = jnp.concatenate([one[1], other[1]], axis=1)
        out = dot(band_rows[...], jnp.concatenate([high, low, high], axis=0))
        everything = pl.ds(0, rows)
        w[2 * two] = out[:, :LANES] + unpack(sides, everything, rows, 2 * two)
        w[2 * two + 1] = out[:, LANES:] + unpack(sides, everything, rows, 2 * two + 1)
        return carry

    lax.fori_loop(0, steps // 2, along, 0, unroll=2)


def edge_kernel(from_left, from_right, u_edges, mat, band_rows, sides, full_edges):
    steps = u_edges.shape[1]
    rows = from_left.shape[0]
    for side, source in ((0, from_left), (1, from_right)):
        high, low = split(source[...])
        value = dot(high, mat[2 * side]) + dot(low, mat[2 * side])
        value = value + dot(high, mat[2 * side + 1])
        sides[side] = value
    for which, start in ((0, 0), (1, rows - GROUP)):
        for step in range(steps):
            full_edges[which, step] = u_edges[which, step] + unpack(
                sides, pl.ds(start, GROUP), GROUP, step
            )
    for side in range(2):
        high, low = split(sides[side])
        sides[side] = dot(band_rows[...], jnp.concatenate([high, low, high], axis=0))


def fill_extra(extra, above, below, edge):
    steps = above.shape[0]
    flat = (steps * GROUP, LANES)
    for which, source in ((0, above), (1, below)):
        both = pair(source[...].reshape(flat))
        value = halves(dot(edge[2 * which], both)) + dot(edge[2 * which + 1], both[:, :LANES])
        extra[which] = value.reshape(steps, GROUP, LANES)
    extra[2] = jnp.zeros((steps, GROUP, LANES), F32)


def which_extra(g, groups):
    return jnp.where(g == 0, 0, jnp.where(g == groups - 1, 1, 2))


def gather_tiles(g, both, first, count, acc, ut, gv):
    steps = acc.shape[0]
    lanes = tile_lanes(first, count)
    out = dot(both, gv[:, lanes]).reshape(steps, GROUP, count * LANES)
    acc[:, :, lanes] += out * ut[rows_of(g), lanes][None]


def left_of(value):
    steps = value.shape[0]
    high, low = split(value.reshape(steps * GROUP, LANES))
    return jnp.concatenate([high, low, high], axis=1)


def whole(x):
    return jnp.sum(jnp.sum(x, axis=1, keepdims=True), axis=0, keepdims=True)


def fold(x):
    return jnp.sum(x, axis=0)


def image_one_kernel(
    bounds, w, above, below, edge, noise, b, sb, info, ut, gv, sv, rank,
    p, ps, z, strips, sums, unsorted, acc, extra, flat_rows,
):
    steps, rows, _ = w.shape
    groups = rows // GROUP
    slots = rank.shape[1]
    tiles = slots // LANES
    fill_extra(extra, above, below, edge)
    acc[...] = jnp.zeros_like(acc)

    def run(g, carry):
        value = w[:, rows_of(g), :] + extra[which_extra(g, groups)]
        mine = b[:, rows_of(g), :]
        image = value + noise[rows_of(g), :][None] * mine
        p[:, rows_of(g), :] = image
        gather_tiles(g, left_of(value), bounds[g, 0], 2, acc, ut, gv)
        return (
            carry[0] + fold(mine * mine),
            carry[1] + fold(mine * image),
            carry[2] + fold(image * image),
        )

    zero = jnp.zeros((GROUP, LANES), F32)
    carry = lax.fori_loop(0, groups, run, (zero,) * 3, unroll=2)

    @pl.when(bounds[0, 2] > 2)
    def _():
        def crowded(g, inner):
            value = w[:, rows_of(g), :] + extra[which_extra(g, groups)]

            def more(index, innermost):
                gather_tiles(g, left_of(value), index, 1, acc, ut, gv)
                return innermost

            return lax.fori_loop(bounds[g, 0] + 2, bounds[g, 1], more, inner)

        lax.fori_loop(0, groups, crowded, 0)

    def stations(index, carry):
        lanes = tile_lanes(index, 1)
        sampled = jnp.sum(acc[:, :, lanes], axis=1, keepdims=True)
        mine = sb[:, :, lanes]
        live = info[1, :, lanes][None]
        image = live * (sampled + info[0, :, lanes][None] * mine) + (1.0 - live) * mine
        ps[:, :, lanes] = image
        for step in range(steps):
            flat_rows[pl.ds(step, 1), lanes] = image[step, 0:1]
        part = 1.0 / GROUP
        return (
            carry[0] + part * fold(mine * mine),
            carry[1] + part * fold(mine * image),
            carry[2] + part * fold(image * image),
        )

    carry = lax.fori_loop(0, tiles, stations, carry)
    ps[:, :, pl.ds(slots, 2 * LANES)] = jnp.zeros((steps, GROUP, 2 * LANES), F32)
    bb, bp, pp = (whole(x) for x in carry)
    lane = iota((GROUP, LANES), 1)
    value = jnp.where(lane == 0, bb / bp, 0.0)
    value = jnp.where(lane == 1, bb, value)
    value = jnp.where(lane == 2, bp, value)
    value = jnp.where(lane == 3, pp, value)
    sums[...] = value
    scatter_all(p, z, strips, ps, ut, sv, bounds)
    pieces = three(flat_rows[...])

    def unsort_block(block, carry):
        lanes = tile_lanes(block, 1)
        order = (iota((slots, LANES), 0) == rank[:, lanes]).astype(F32).astype(BF16)
        out = dot(pieces, order)
        unsorted[:, lanes] = out[:steps] + out[steps : 2 * steps] + out[2 * steps :]
        return carry

    lax.fori_loop(0, tiles, unsort_block, 0)


def image_two_kernel(
    w, above, below, edge, noise, b, p, z_first, z, sb, ps, info, sums,
    q, message, extra,
):
    steps, rows, _ = w.shape
    groups = rows // GROUP
    tiles = sb.shape[2] // LANES - 2
    fill_extra(extra, above, below, edge)
    shift = jnp.broadcast_to(sums[0:1, 0:1], (GROUP, LANES))[None]

    def run(g, carry):
        here = rows_of(g)
        value = w[:, here, :] + extra[which_extra(g, groups)]
        mine = p[:, here, :]
        scaled = noise[here, :][None] * mine
        q[:, here, :] = value + scaled
        residual = b[:, here, :] - shift * mine
        second = z[:, here, :]
        moved = z_first[:, here, :] - shift * second
        return (
            carry[0] + fold(residual * residual),
            carry[1] + fold(moved * value + residual * scaled),
            carry[2] + fold(second * value + mine * scaled),
        )

    zero = jnp.zeros((GROUP, LANES), F32)
    carry = lax.fori_loop(0, groups, run, (zero,) * 3)

    def stations(index, carry):
        lanes = tile_lanes(index, 1)
        mine = ps[:, :, lanes]
        live = info[1, :, lanes]
        scaled = (live * info[0, :, lanes] + (1.0 - live))[None] * mine
        residual = sb[:, :, lanes] - shift * mine
        part = 1.0 / GROUP
        return (
            carry[0] + part * fold(residual * residual),
            carry[1] + part * fold(residual * scaled),
            carry[2] + part * fold(mine * scaled),
        )

    carry = lax.fori_loop(0, tiles, stations, carry)
    lane = iota((1, LANES), 1)
    value = jnp.where(lane < 4, sums[0:1, :], 0.0)
    for place, x in enumerate(carry):
        value = jnp.where(lane == 4 + place, whole(x), value)
    message[...] = jnp.broadcast_to(value, message.shape)


def final_kernel(received, b, p, q, obs, unsorted, count, solution_out, residual_out, station_out):
    everything = received[...]

    def column(index):
        return everything[:, index : index + 1]

    def total(x):
        return jnp.sum(x, axis=0, keepdims=True)

    shift, bb, bp, pp = (column(i) for i in range(4))
    rr, rq, pq = (column(i) for i in range(4, 7))
    norm = total(bb)
    alpha = norm / total(bp)
    delta = shift - alpha
    rp = bp - shift * pp
    ru = rp - shift * rq
    pu = pp - shift * pq
    norm_next = total(rr + 2.0 * delta * rp + delta * delta * pp)
    energy = total(ru + delta * (rq + pu) + delta * delta * pq)
    beta = norm_next / norm
    alpha_next = norm_next / (energy - beta * norm_next / alpha)
    along = alpha + alpha_next * (1.0 + beta)
    twice = alpha_next * alpha
    part = solution_out.shape[0]
    rows = solution_out.shape[1]
    start = pl.program_id(0) * part
    chunk = 64
    wide_along = jnp.broadcast_to(along, (chunk, LANES))
    wide_twice = jnp.broadcast_to(twice, (chunk, LANES))
    pieces = rows // chunk

    def run(index, carry):
        step = index // pieces
        here = pl.ds(pl.multiple_of((index % pieces) * chunk, chunk), chunk)
        first = b[start + step, here, :]
        second = p[start + step, here, :]
        solution_out[step, here, :] = wide_along * first - wide_twice * second
        residual_out[step, here, :] = (
            first - wide_along * second + wide_twice * q[start + step, here, :]
        )
        return carry

    lax.fori_loop(0, part * pieces, run, 0, unroll=2)

    @pl.when(pl.program_id(0) == 0)
    def _():
        steps, slots = obs.shape
        live = iota((steps, slots), 1) < count[0, 0]
        own = jnp.where(live, obs[...], 0.0)
        station_out[...] = along * own - twice * unsorted[...]


VMEM = pl.BlockSpec(memory_space=pltpu.VMEM)
SMEM = pl.BlockSpec(memory_space=pltpu.SMEM)


def call(kernel, outs, ins, operands, scratch=(), flops=10**9, moved=10**7, limit=8, **extra):
    return pl.pallas_call(
        kernel,
        out_shape=outs,
        in_specs=ins,
        out_specs=[VMEM] * len(outs),
        scratch_shapes=list(scratch),
        compiler_params=pltpu.CompilerParams(vmem_limit_bytes=limit * 2**20),
        cost_estimate=pl.CostEstimate(flops=flops, bytes_accessed=moved, transcendentals=0),
        **extra,
    )(*operands)


def exchange(first, second, axis):
    count = lax.axis_size(axis)
    forward = [(i, i + 1) for i in range(count - 1)]
    backward = [(target, source) for source, target in forward]
    return lax.ppermute(first, axis, forward), lax.ppermute(second, axis, backward)


def body(
    grid_obs, grid_noise, station_obs, station_noise, station_offset, station_cell,
    station_count, time_cov,
):
    steps, rows, cols = grid_obs.shape
    slots = station_obs.shape[3]
    wide = steps * GROUP
    groups = rows // GROUP
    lanes = slots + 2 * LANES
    devices = lax.axis_size("row") * lax.axis_size("col")
    obs = station_obs.reshape(steps, slots)
    shape = jax.ShapeDtypeStruct
    field = shape((steps, rows, cols), F32)
    rim = shape((2, steps, GROUP, cols), F32)
    strips_shape = shape((2, rows, wide), F32)
    station_field = shape((steps, GROUP, lanes), F32)
    extra = pltpu.VMEM((3, steps, GROUP, LANES), F32)
    sb, info, rank, sv, gv, ut, bounds, mix, mat, band_rows, band_cols, edge = call(
        prepare_kernel,
        [
            station_field,
            shape((2, GROUP, lanes), F32),
            shape((1, slots), jnp.int32),
            shape((2, lanes, 2 * LANES), BF16),
            shape((3 * LANES, lanes), BF16),
            shape((rows, lanes), F32),
            shape((groups, LANES), jnp.int32),
            shape((wide, 3 * wide), BF16),
            shape((4, wide, wide), BF16),
            shape((rows, 3 * rows), BF16),
            shape((2 * LANES, 2 * LANES), BF16),
            shape((4, wide, wide), BF16),
        ],
        [SMEM] + [VMEM] * 5,
        (
            station_count,
            station_cell.reshape(1, slots),
            station_offset.reshape(2, slots),
            station_noise.reshape(1, slots),
            obs,
            time_cov,
        ),
        [pltpu.VMEM((steps + 8, slots), F32), pltpu.VMEM((steps + 8, slots), F32)],
    )
    z_first, strips = call(
        scatter_kernel,
        [field, strips_shape],
        [SMEM] + [VMEM] * 4,
        (bounds, grid_obs, sb, ut, sv),
        limit=4,
    )

    def smooth(z, strips):
        from_left, from_right = exchange(strips[1], strips[0], "col")
        u, u_edges = call(
            first_filter_kernel,
            [field, rim],
            [VMEM] * 3,
            (z, mix, band_cols),
            [pltpu.VMEM((groups // 2, 2, wide, 2 * LANES), BF16)],
        )
        sides, full_edges = call(
            edge_kernel,
            [strips_shape, rim],
            [VMEM] * 5,
            (from_left, from_right, u_edges, mat, band_rows),
            limit=4,
        )
        above, below = exchange(full_edges[1], full_edges[0], "row")
        (w,) = call(
            second_filter_kernel, [field], [VMEM] * 3, (u, sides, band_rows), limit=4
        )
        return w, above, below

    w, above, below = smooth(z_first, strips)
    p, ps, z, strips, sums, unsorted = call(
        image_one_kernel,
        [field, station_field, field, strips_shape, shape((GROUP, LANES), F32), shape((steps, slots), F32)],
        [SMEM] + [VMEM] * 12,
        (bounds, w, above, below, edge, grid_noise, grid_obs, sb, info, ut, gv, sv, rank),
        [pltpu.VMEM((steps, GROUP, lanes), F32), extra, pltpu.VMEM((steps, slots), F32)],
    )
    w, above, below = smooth(z, strips)
    q, message = call(
        image_two_kernel,
        [field, shape((devices, LANES), F32)],
        [VMEM] * 13,
        (w, above, below, edge, grid_noise, grid_obs, p, z_first, z, sb, ps, info, sums),
        [extra],
        limit=4,
    )
    received = lax.all_to_all(message, ("row", "col"), 0, 0, tiled=True)
    parts = 8
    block = pl.BlockSpec((steps // parts, rows, cols), lambda i: (i, 0, 0))
    solution_grid, residual_grid, solution_stations = pl.pallas_call(
        final_kernel,
        grid=(parts,),
        out_shape=[field, field, shape((steps, slots), F32)],
        in_specs=[VMEM] * 6 + [SMEM],
        out_specs=[block, block, pl.BlockSpec((steps, slots), lambda i: (0, 0))],
        compiler_params=pltpu.CompilerParams(vmem_limit_bytes=6 * 2**20),
    )(received, grid_obs, p, q, obs, unsorted, station_count)
    return solution_grid, solution_stations.reshape(steps, 1, 1, slots), residual_grid


def solution(mesh):
    placed = (
        P(None, "row", "col"),
        P("row", "col"),
        P(None, "row", "col", None),
        P("row", "col", None),
        P(None, "row", "col", None),
        P("row", "col", None),
        P("row", "col"),
        P(),
    )
    return jax.shard_map(
        body,
        mesh=mesh,
        in_specs=placed,
        out_specs=(P(None, "row", "col"), P(None, "row", "col", None), P(None, "row", "col")),
        check_vma=False,
    )
```

```python
import functools

import jax
import jax.numpy as jnp
from jax import lax
from jax.experimental import pallas as pl
from jax.experimental.pallas import tpu as pltpu
from jax.sharding import PartitionSpec as P

REACH = 8
LANES = 128
GROUP = 8
F32 = jnp.float32
BF16 = jnp.bfloat16
HIGHEST = lax.Precision.HIGHEST


def iota(shape, dim):
    return lax.broadcasted_iota(jnp.int32, shape, dim)


def taper(distance):
    spread = jnp.abs(distance).astype(F32)
    value = (1.0 - spread / (REACH + 1)) * jnp.exp(-spread / 3.0)
    return jnp.where(jnp.abs(distance) <= REACH, value, 0.0)


def split(x):
    high = x.astype(BF16)
    return high, (x - high.astype(F32)).astype(BF16)


def pair(x):
    high, low = split(x)
    return jnp.concatenate([high, low], axis=1)


def dot(a, b):
    return jnp.dot(a, b, preferred_element_type=F32)


def dot_nt(a, b):
    return lax.dot_general(a, b, (((1,), (1,)), ((), ())), preferred_element_type=F32)


def halves(x):
    width = x.shape[1] // 2
    return x[:, :width] + x[:, width:]


def three(x):
    high = x.astype(BF16)
    rest = x - high.astype(F32)
    middle = rest.astype(BF16)
    low = (rest - middle.astype(F32)).astype(BF16)
    return jnp.concatenate([high, middle, low], axis=0)


def cut(x, axis):
    return [
        lax.slice_in_dim(x, start, start + LANES, axis=axis)
        for start in range(0, x.shape[axis], LANES)
    ]


def rows_of(g):
    return pl.ds(pl.multiple_of(g * GROUP, GROUP), GROUP)


def prepare_kernel(
    count, cell_any, offset_any, noise_any, obs_any, base_any,
    base, z, strips, sb, info, rank_out, own, sv, gv, ut, bounds,
    cell_v, offset_v, noise_v, obs_v, bounds_v, table, sorted_rows, copies,
):
    base_copy = pltpu.make_async_copy(base_any, base, copies.at[0])
    base_copy.start()
    small = [
        pltpu.make_async_copy(source, target, copies.at[1 + place])
        for place, (source, target) in enumerate(
            ((cell_any, cell_v), (offset_any, offset_v), (noise_any, noise_v), (obs_any, obs_v))
        )
    ]
    for copy in small:
        copy.start()
    for copy in small:
        copy.wait()
    cell, noise = cell_v[0], noise_v[0]
    steps, slots = own.shape
    tiles = slots // LANES
    rows = base.shape[1]
    groups = rows // GROUP
    slot = iota((1, slots), 1)
    live = slot < count[0, 0]
    where_row = cell // LANES
    where_col = cell - where_row * LANES
    key = jnp.where(live, where_row, rows) * slots + slot
    key = key.astype(F32)
    total = jnp.zeros((1, slots), F32)
    for block in range(tiles):
        piece = key[:, block * LANES : (block + 1) * LANES]
        column = jnp.transpose(jnp.broadcast_to(piece, (LANES, LANES)))
        column = jnp.concatenate([column] * tiles, axis=1)
        less = jnp.where(column < key, 1.0, 0.0)
        total = total + jnp.sum(less, axis=0, keepdims=True)
    rank = total.astype(jnp.int32)
    rank_out[...] = rank
    lived = jnp.where(live, 1.0, 0.0)
    for step in range(steps):
        own[pl.ds(step, 1), :] = obs_v[step, 0] * lived
    table[pl.ds(0, steps), :] = own[...]
    table[pl.ds(steps, 1), :] = where_row.astype(F32)
    table[pl.ds(steps + 1, 1), :] = where_col.astype(F32)
    table[pl.ds(steps + 2, 1), :] = offset_v[0, 0]
    table[pl.ds(steps + 3, 1), :] = offset_v[1, 0]
    table[pl.ds(steps + 4, 1), :] = noise
    table[pl.ds(steps + 5, 1), :] = lived
    table[pl.ds(steps + 6, 2), :] = jnp.zeros((2, slots), F32)
    pieces = three(table[...])
    height = table.shape[0]

    def sort_block(block, carry):
        start = pl.multiple_of(block * LANES, LANES)
        order = (iota((LANES, slots), 0) + start == rank).astype(F32).astype(BF16)
        out = dot_nt(pieces, order)
        sorted_rows[:, pl.ds(start, LANES)] = (
            out[:height] + out[height : 2 * height] + out[2 * height :]
        )
        return carry

    lax.fori_loop(0, tiles, sort_block, 0)
    ordered_row = sorted_rows[pl.ds(steps, 1), :]
    ordered_live = sorted_rows[pl.ds(steps + 5, 1), :]
    first_row = (iota((groups, slots), 0) * GROUP).astype(F32)
    before = jnp.where(ordered_row < first_row - 1.0, ordered_live, 0.0)
    until = jnp.where(ordered_row < first_row + GROUP, ordered_live, 0.0)
    low = jnp.sum(before, axis=1, keepdims=True)
    high = jnp.sum(until, axis=1, keepdims=True)
    start_tile = jnp.where(high > low, jnp.floor(low * (1.0 / LANES)), float(tiles))
    stop_tile = jnp.where(high > low, jnp.floor((high - 1.0) * (1.0 / LANES)) + 1.0, 0.0)
    lane = iota((groups, LANES), 1)
    span = jnp.max(stop_tile - start_tile, axis=0, keepdims=True)
    bounds_v[...] = jnp.where(
        lane == 0, start_tile, jnp.where(lane == 1, stop_tile, span)
    ).astype(jnp.int32)
    bounds_copy = pltpu.make_async_copy(bounds_v, bounds, copies.at[5])
    bounds_copy.start()
    extra = pl.ds(slots, 2 * LANES)
    sb[:, :, extra] = jnp.zeros((steps, GROUP, 2 * LANES), F32)
    info[:, :, extra] = jnp.zeros((2, GROUP, 2 * LANES), F32)
    sv[:, extra, :] = jnp.zeros((2, 2 * LANES, 2 * LANES), BF16)
    gv[:, extra] = jnp.zeros((3 * LANES, 2 * LANES), BF16)
    ut[:, extra] = jnp.zeros((rows, 2 * LANES), F32)
    for block in range(tiles):
        lanes = pl.ds(block * LANES, LANES)
        at_row = sorted_rows[pl.ds(steps, 1), lanes].astype(jnp.int32)
        at_col = sorted_rows[pl.ds(steps + 1, 1), lanes].astype(jnp.int32)
        along_row = sorted_rows[pl.ds(steps + 2, 1), lanes]
        along_col = sorted_rows[pl.ds(steps + 3, 1), lanes]
        row = iota((rows, LANES), 0)
        ut[:, lanes] = jnp.where(row == at_row, 1.0 - along_row, 0.0) + jnp.where(
            row == at_row + 1, along_row, 0.0
        )
        col = iota((LANES, LANES), 0)
        across = jnp.where(col == at_col, 1.0 - along_col, 0.0) + jnp.where(
            col == at_col + 1, along_col, 0.0
        )
        high_part, low_part = split(across)
        gv[:, lanes] = jnp.concatenate([high_part, high_part, low_part], axis=0)
        high_part, low_part = split(jnp.transpose(across))
        sv[0, lanes, :] = jnp.concatenate([high_part, low_part], axis=1)
        sv[1, lanes, :] = jnp.concatenate([high_part, jnp.zeros_like(low_part)], axis=1)
        for place in range(2):
            info[place, :, lanes] = jnp.broadcast_to(
                sorted_rows[pl.ds(steps + 4 + place, 1), lanes], (GROUP, LANES)
            )
        for step in range(steps):
            sb[step, :, lanes] = jnp.broadcast_to(
                sorted_rows[pl.ds(step, 1), lanes], (GROUP, LANES)
            )
    bounds_copy.wait()
    base_copy.wait()
    scatter_all(base, z, strips, sb, ut, sv, bounds)


def matrices_kernel(cov, mix, mat, band_rows, band_cols, edge):
    steps = cov.shape[0]
    rows = band_rows.shape[0]
    wide = steps * GROUP
    spread = (iota((wide, steps), 0) // GROUP == iota((wide, steps), 1)).astype(F32)
    spread_t = (iota((steps, wide), 1) // GROUP == iota((steps, wide), 0)).astype(F32)
    expanded = jnp.dot(
        jnp.dot(spread, cov[...], precision=HIGHEST, preferred_element_type=F32),
        spread_t,
        precision=HIGHEST,
        preferred_element_type=F32,
    )
    a = iota((wide, wide), 0)
    b = iota((wide, wide), 1)
    same = (a % GROUP) == (b % GROUP)
    high_part, low_part = split(jnp.where(same, expanded, 0.0))
    mix[...] = jnp.concatenate([high_part, high_part, low_part], axis=1)
    near = taper((b % GROUP) + REACH - (a % GROUP)) * expanded
    near = jnp.concatenate(
        [jnp.concatenate([x[GROUP:], x[:GROUP]], axis=0) for x in cut(near, 0)], axis=0
    )
    mat[0], mat[1] = split(near)
    far = taper(REACH + (a % GROUP) - (b % GROUP)) * expanded
    far = jnp.concatenate(
        [pltpu.roll(x, LANES - GROUP, 1) for x in cut(far, 1)], axis=1
    )
    mat[2], mat[3] = split(far)
    ra = iota((rows, rows), 0)
    rb = iota((rows, rows), 1)
    high_part, low_part = split(0.25 * taper(ra - rb))
    band_rows[...] = jnp.concatenate([high_part, high_part, low_part], axis=1)
    ca = iota((LANES, LANES), 0)
    cb = iota((LANES, LANES), 1)
    high_part, low_part = split(taper(ca - cb))
    band_cols[...] = jnp.concatenate(
        [
            jnp.concatenate([high_part, low_part], axis=1),
            jnp.concatenate([high_part, jnp.zeros_like(low_part)], axis=1),
        ],
        axis=0,
    )
    block_same = (a // GROUP) == (b // GROUP)
    above = 0.25 * taper((a % GROUP) + REACH - (b % GROUP))
    below = 0.25 * taper(REACH + (b % GROUP) - (a % GROUP))
    edge[0], edge[1] = split(jnp.where(block_same, above, 0.0))
    edge[2], edge[3] = split(jnp.where(block_same, below, 0.0))


def tile_lanes(index, count):
    return pl.ds(pl.multiple_of(index * LANES, LANES), count * LANES)


def spread_tiles(g, first, count, sb, ut, sv):
    steps = sb.shape[0]
    lanes = tile_lanes(first, count)
    scaled = sb[:, :, lanes] * ut[rows_of(g), lanes][None]
    left = pair(scaled.reshape(steps * GROUP, count * LANES))
    right = jnp.concatenate([sv[0, lanes, :], sv[1, lanes, :]], axis=0)
    return halves(dot(left, right)).reshape(steps, GROUP, LANES)


def scatter_all(base, z, strips, sb, ut, sv, bounds):
    groups = base.shape[1] // GROUP

    def run(g, carry):
        value = base[:, rows_of(g), :] + spread_tiles(g, bounds[g, 0], 2, sb, ut, sv)
        z[:, rows_of(g), :] = value
        pack_group(g, value, strips)
        return carry

    lax.fori_loop(0, groups, run, 0, unroll=2)

    @pl.when(bounds[0, 2] > 2)
    def _():
        def crowded(g, carry):
            def more(index, inner):
                z[:, rows_of(g), :] += spread_tiles(g, index, 1, sb, ut, sv)
                return inner

            lax.fori_loop(bounds[g, 0] + 2, bounds[g, 1], more, 0)
            pack_group(g, z[:, rows_of(g), :], strips)
            return carry

        lax.fori_loop(0, groups, crowded, 0)


def pack_group(g, value, strips):
    steps = value.shape[0]
    per = LANES // GROUP
    slot = iota((GROUP, LANES), 1) // GROUP
    for half in range(steps // per):
        left = jnp.zeros((GROUP, LANES), F32)
        right = jnp.zeros((GROUP, LANES), F32)
        for local in range(per):
            moved = value[half * per + local]
            if local:
                moved = pltpu.roll(moved, local * GROUP, 1)
            left = jnp.where(slot == local, moved, left)
            right = jnp.where(slot == (local - 1) % per, moved, right)
        lanes = pl.ds(half * LANES, LANES)
        strips[0, rows_of(g), lanes] = left
        strips[1, rows_of(g), lanes] = right


def unpack(sides, where_rows, count, step):
    per = LANES // GROUP
    half, local = step // per, step % per
    lane = iota((count, LANES), 1)
    lanes = pl.ds(half * LANES, LANES) if isinstance(step, int) else tile_lanes(half, 1)
    both = jnp.where(lane // GROUP == local, sides[0, where_rows, lanes], sides[1, where_rows, lanes])
    both = pltpu.roll(both, (LANES - local * GROUP) % LANES, 1)
    return jnp.where((lane < GROUP) | (lane >= LANES - GROUP), both, 0.0)


def first_filter_kernel(z, mix, band_cols, u, u_edges, y):
    steps, rows, cols = z.shape
    groups = rows // GROUP
    flat = (steps * GROUP, LANES)

    def across(quad, carry):
        parts = [z[:, rows_of(4 * quad + i), :].reshape(flat) for i in range(4)]
        value = halves(dot(pair(jnp.concatenate(parts, axis=0)), band_cols[...]))
        both = split(value)
        for i in range(4):
            for part in range(2):
                y[2 * quad + i // 2, part, :, pl.ds((i % 2) * LANES, LANES)] = both[part][
                    i * flat[0] : (i + 1) * flat[0]
                ]
        return carry

    lax.fori_loop(0, groups // 4, across, 0)

    def mixing(two, carry):
        right = jnp.concatenate([y[two, 0], y[two, 1], y[two, 0]], axis=0)
        out = dot(mix[...], right)
        u[:, rows_of(2 * two), :] = out[:, :LANES].reshape(steps, GROUP, LANES)
        u[:, rows_of(2 * two + 1), :] = out[:, LANES:].reshape(steps, GROUP, LANES)
        return carry

    lax.fori_loop(0, groups // 2, mixing, 0, unroll=2)
    u_edges[0] = u[:, pl.ds(0, GROUP), :]
    u_edges[1] = u[:, pl.ds(rows - GROUP, GROUP), :]


def filter_unsort_kernel(z, mix, band_cols, flat_rows, rank, u, u_edges, unsorted, y):
    first_filter_kernel(z, mix, band_cols, u, u_edges, y)
    steps, slots = flat_rows.shape
    tiles = slots // LANES
    pieces = three(flat_rows[...])

    def unsort_block(block, carry):
        lanes = tile_lanes(block, 1)
        order = (iota((slots, LANES), 0) == rank[:, lanes]).astype(F32).astype(BF16)
        out = dot(pieces, order)
        unsorted[:, lanes] = out[:steps] + out[steps : 2 * steps] + out[2 * steps :]
        return carry

    lax.fori_loop(0, tiles, unsort_block, 0)


def second_filter_kernel(u, sides, band_rows, w):
    steps, rows, cols = u.shape

    def along(two, carry):
        one = split(u[2 * two])
        other = split(u[2 * two + 1])
        high = jnp.concatenate([one[0], other[0]], axis=1)
        low = jnp.concatenate([one[1], other[1]], axis=1)
        out = dot(band_rows[...], jnp.concatenate([high, low, high], axis=0))
        everything = pl.ds(0, rows)
        w[2 * two] = out[:, :LANES] + unpack(sides, everything, rows, 2 * two)
        w[2 * two + 1] = out[:, LANES:] + unpack(sides, everything, rows, 2 * two + 1)
        return carry

    lax.fori_loop(0, steps // 2, along, 0, unroll=2)


def edge_kernel(from_left, from_right, u_edges, mat, band_rows, sides, full_edges):
    steps = u_edges.shape[1]
    rows = from_left.shape[0]
    for side, source in ((0, from_left), (1, from_right)):
        high, low = split(source[...])
        value = dot(high, mat[2 * side]) + dot(low, mat[2 * side])
        value = value + dot(high, mat[2 * side + 1])
        sides[side] = value
    for which, start in ((0, 0), (1, rows - GROUP)):
        for step in range(steps):
            full_edges[which, step] = u_edges[which, step] + unpack(
                sides, pl.ds(start, GROUP), GROUP, step
            )
    for side in range(2):
        high, low = split(sides[side])
        sides[side] = dot(band_rows[...], jnp.concatenate([high, low, high], axis=0))


def fill_extra(extra, above, below, edge):
    steps = above.shape[0]
    flat = (steps * GROUP, LANES)
    for which, source in ((0, above), (1, below)):
        both = pair(source[...].reshape(flat))
        value = halves(dot(edge[2 * which], both)) + dot(edge[2 * which + 1], both[:, :LANES])
        extra[which] = value.reshape(steps, GROUP, LANES)
    extra[2] = jnp.zeros((steps, GROUP, LANES), F32)


def which_extra(g, groups):
    return jnp.where(g == 0, 0, jnp.where(g == groups - 1, 1, 2))


def gather_tiles(g, both, first, count, acc, ut, gv):
    steps = acc.shape[0]
    lanes = tile_lanes(first, count)
    out = dot(both, gv[:, lanes]).reshape(steps, GROUP, count * LANES)
    acc[:, :, lanes] += out * ut[rows_of(g), lanes][None]


def left_of(value):
    steps = value.shape[0]
    high, low = split(value.reshape(steps * GROUP, LANES))
    return jnp.concatenate([high, low, high], axis=1)


def whole(x):
    return jnp.sum(jnp.sum(x, axis=1, keepdims=True), axis=0, keepdims=True)


def fold(x):
    return jnp.sum(x, axis=0)


def image_one_kernel(
    bounds, w, above, below, edge, noise, b, sb, info, ut, gv, sv,
    p, ps, z, strips, sums, flat_rows, acc, extra,
):
    steps, rows, _ = w.shape
    groups = rows // GROUP
    slots = sb.shape[2] - 2 * LANES
    tiles = slots // LANES
    fill_extra(extra, above, below, edge)
    acc[...] = jnp.zeros_like(acc)

    def run(g, carry):
        value = w[:, rows_of(g), :] + extra[which_extra(g, groups)]
        mine = b[:, rows_of(g), :]
        image = value + noise[rows_of(g), :][None] * mine
        p[:, rows_of(g), :] = image
        gather_tiles(g, left_of(value), bounds[g, 0], 2, acc, ut, gv)
        return (
            carry[0] + fold(mine * mine),
            carry[1] + fold(mine * image),
            carry[2] + fold(image * image),
        )

    zero = jnp.zeros((GROUP, LANES), F32)
    carry = lax.fori_loop(0, groups, run, (zero,) * 3, unroll=2)

    @pl.when(bounds[0, 2] > 2)
    def _():
        def crowded(g, inner):
            value = w[:, rows_of(g), :] + extra[which_extra(g, groups)]

            def more(index, innermost):
                gather_tiles(g, left_of(value), index, 1, acc, ut, gv)
                return innermost

            return lax.fori_loop(bounds[g, 0] + 2, bounds[g, 1], more, inner)

        lax.fori_loop(0, groups, crowded, 0)

    def stations(index, carry):
        lanes = tile_lanes(index, 1)
        sampled = jnp.sum(acc[:, :, lanes], axis=1, keepdims=True)
        mine = sb[:, :, lanes]
        live = info[1, :, lanes][None]
        image = live * (sampled + info[0, :, lanes][None] * mine) + (1.0 - live) * mine
        ps[:, :, lanes] = image
        for step in range(steps):
            flat_rows[pl.ds(step, 1), lanes] = image[step, 0:1]
        part = 1.0 / GROUP
        return (
            carry[0] + part * fold(mine * mine),
            carry[1] + part * fold(mine * image),
            carry[2] + part * fold(image * image),
        )

    carry = lax.fori_loop(0, tiles, stations, carry)
    ps[:, :, pl.ds(slots, 2 * LANES)] = jnp.zeros((steps, GROUP, 2 * LANES), F32)
    bb, bp, pp = (whole(x) for x in carry)
    lane = iota((GROUP, LANES), 1)
    value = jnp.where(lane == 0, bb / bp, 0.0)
    value = jnp.where(lane == 1, bb, value)
    value = jnp.where(lane == 2, bp, value)
    value = jnp.where(lane == 3, pp, value)
    sums[...] = value
    scatter_all(p, z, strips, ps, ut, sv, bounds)


def image_two_kernel(
    w, above, below, edge, noise, b, p, z_first, z, sb, ps, info, sums,
    q, message, extra,
):
    steps, rows, _ = w.shape
    groups = rows // GROUP
    tiles = sb.shape[2] // LANES - 2
    fill_extra(extra, above, below, edge)
    shift = jnp.broadcast_to(sums[0:1, 0:1], (GROUP, LANES))[None]

    def run(g, carry):
        here = rows_of(g)
        value = w[:, here, :] + extra[which_extra(g, groups)]
        mine = p[:, here, :]
        scaled = noise[here, :][None] * mine
        q[:, here, :] = value + scaled
        residual = b[:, here, :] - shift * mine
        second = z[:, here, :]
        moved = z_first[:, here, :] - shift * second
        return (
            carry[0] + fold(residual * residual),
            carry[1] + fold(moved * value + residual * scaled),
            carry[2] + fold(second * value + mine * scaled),
        )

    zero = jnp.zeros((GROUP, LANES), F32)
    carry = lax.fori_loop(0, groups, run, (zero,) * 3)

    def stations(index, carry):
        lanes = tile_lanes(index, 1)
        mine = ps[:, :, lanes]
        live = info[1, :, lanes]
        scaled = (live * info[0, :, lanes] + (1.0 - live))[None] * mine
        residual = sb[:, :, lanes] - shift * mine
        part = 1.0 / GROUP
        return (
            carry[0] + part * fold(residual * residual),
            carry[1] + part * fold(residual * scaled),
            carry[2] + part * fold(mine * scaled),
        )

    carry = lax.fori_loop(0, tiles, stations, carry)
    lane = iota((1, LANES), 1)
    value = jnp.where(lane < 4, sums[0:1, :], 0.0)
    for place, x in enumerate(carry):
        value = jnp.where(lane == 4 + place, whole(x), value)
    message[...] = jnp.broadcast_to(value, message.shape)


def final_kernel(
    received, b, p, q, own, unsorted, solution_out, residual_out, station_out,
    solution_v, residual_v, station_v, sems, station_sem,
):
    everything = received[...]

    def column(index):
        return everything[:, index : index + 1]

    def total(x):
        return jnp.sum(x, axis=0, keepdims=True)

    shift, bb, bp, pp = (column(i) for i in range(4))
    rr, rq, pq = (column(i) for i in range(4, 7))
    norm = total(bb)
    alpha = norm / total(bp)
    delta = shift - alpha
    rp = bp - shift * pp
    ru = rp - shift * rq
    pu = pp - shift * pq
    norm_next = total(rr + 2.0 * delta * rp + delta * delta * pp)
    energy = total(ru + delta * (rq + pu) + delta * delta * pq)
    beta = norm_next / norm
    alpha_next = norm_next / (energy - beta * norm_next / alpha)
    along = alpha + alpha_next * (1.0 + beta)
    twice = alpha_next * alpha
    steps, rows, _ = b.shape
    chunk = 64
    tall = (chunk // GROUP, GROUP, LANES)
    wide_along = jnp.broadcast_to(along, (GROUP, LANES))[None]
    wide_twice = jnp.broadcast_to(twice, (GROUP, LANES))[None]

    def copies(place):
        here = pl.ds(place * 2, 2)
        return (
            pltpu.make_async_copy(solution_v.at[here], solution_out.at[here], sems.at[0, place]),
            pltpu.make_async_copy(residual_v.at[here], residual_out.at[here], sems.at[1, place]),
        )

    def run(place, carry):
        for inner in range(2):
            step = place * 2 + inner
            for piece in range(rows // chunk):
                here = pl.ds(piece * chunk, chunk)
                first = b[step, here, :].reshape(tall)
                second = p[step, here, :].reshape(tall)
                third = q[step, here, :].reshape(tall)
                solution_v[step, here, :] = (wide_along * first - wide_twice * second).reshape(
                    chunk, LANES
                )
                residual_v[step, here, :] = (
                    first - wide_along * second + wide_twice * third
                ).reshape(chunk, LANES)
        for copy in copies(place):
            copy.start()
        return carry

    lax.fori_loop(0, steps // 2, run, 0)
    stations = along * own[...] - twice * unsorted[...]
    for step in range(steps):
        station_v[step, 0] = stations[step : step + 1]
    station_copy = pltpu.make_async_copy(station_v, station_out, station_sem)
    station_copy.start()

    def finish(place, carry):
        for copy in copies(place):
            copy.wait()
        return carry

    lax.fori_loop(0, steps // 2, finish, 0)
    station_copy.wait()


VMEM = pl.BlockSpec(memory_space=pltpu.VMEM)
SMEM = pl.BlockSpec(memory_space=pltpu.SMEM)
ANY = pl.BlockSpec(memory_space=pltpu.HBM)


def call(kernel, outs, ins, operands, scratch=(), flops=10**9, moved=10**7, limit=8, **extra):
    return pl.pallas_call(
        kernel,
        out_shape=outs,
        in_specs=ins,
        out_specs=[VMEM] * len(outs),
        scratch_shapes=list(scratch),
        compiler_params=pltpu.CompilerParams(vmem_limit_bytes=limit * 2**20),
        cost_estimate=pl.CostEstimate(flops=flops, bytes_accessed=moved, transcendentals=0),
        **extra,
    )(*operands)


def exchange(first, second, axis):
    count = lax.axis_size(axis)
    forward = [(i, i + 1) for i in range(count - 1)]
    backward = [(target, source) for source, target in forward]
    return lax.ppermute(first, axis, forward), lax.ppermute(second, axis, backward)


def body(
    grid_obs, grid_noise, station_obs, station_noise, station_offset, station_cell,
    station_count, time_cov,
):
    steps, rows, cols = grid_obs.shape
    slots = station_obs.shape[3]
    wide = steps * GROUP
    groups = rows // GROUP
    lanes = slots + 2 * LANES
    devices = lax.axis_size("row") * lax.axis_size("col")
    shape = jax.ShapeDtypeStruct
    field = shape((steps, rows, cols), F32)
    rim = shape((2, steps, GROUP, cols), F32)
    strips_shape = shape((2, rows, wide), F32)
    station_field = shape((steps, GROUP, lanes), F32)
    extra = pltpu.VMEM((3, steps, GROUP, LANES), F32)
    b, z_first, strips, sb, info, rank, own, sv, gv, ut, bounds = pl.pallas_call(
        prepare_kernel,
        out_shape=[
            field,
            field,
            strips_shape,
            station_field,
            shape((2, GROUP, lanes), F32),
            shape((1, slots), jnp.int32),
            shape((steps, slots), F32),
            shape((2, lanes, 2 * LANES), BF16),
            shape((3 * LANES, lanes), BF16),
            shape((rows, lanes), F32),
            shape((groups, LANES), jnp.int32),
        ],
        in_specs=[SMEM] + [ANY] * 5,
        out_specs=[VMEM] * 10 + [SMEM],
        scratch_shapes=[
            pltpu.VMEM((1, 1, slots), jnp.int32),
            pltpu.VMEM((2, 1, 1, slots), F32),
            pltpu.VMEM((1, 1, slots), F32),
            pltpu.VMEM((steps, 1, 1, slots), F32),
            pltpu.VMEM((groups, LANES), jnp.int32),
            pltpu.VMEM((steps + 8, slots), F32),
            pltpu.VMEM((steps + 8, slots), F32),
            pltpu.SemaphoreType.DMA((6,)),
        ],
        compiler_params=pltpu.CompilerParams(vmem_limit_bytes=8 * 2**20),
        cost_estimate=pl.CostEstimate(flops=10**9, bytes_accessed=10**7, transcendentals=0),
    )(
        station_count,
        *(
            pltpu.with_memory_space_constraint(x, pltpu.HBM)
            for x in (station_cell, station_offset, station_noise, station_obs, grid_obs)
        ),
    )
    mix, mat, band_rows, band_cols, edge = call(
        matrices_kernel,
        [
            shape((wide, 3 * wide), BF16),
            shape((4, wide, wide), BF16),
            shape((rows, 3 * rows), BF16),
            shape((2 * LANES, 2 * LANES), BF16),
            shape((4, wide, wide), BF16),
        ],
        [VMEM],
        (time_cov,),
    )

    def smooth(z, strips, *more):
        from_left, from_right = exchange(strips[1], strips[0], "col")
        u, u_edges, *unsorted = call(
            filter_unsort_kernel if more else first_filter_kernel,
            [field, rim] + [shape((steps, slots), F32)] * bool(more),
            [VMEM] * (3 + len(more)),
            (z, mix, band_cols, *more),
            [pltpu.VMEM((groups // 2, 2, wide, 2 * LANES), BF16)],
        )
        sides, full_edges = call(
            edge_kernel,
            [strips_shape, rim],
            [VMEM] * 5,
            (from_left, from_right, u_edges, mat, band_rows),
            limit=4,
        )
        above, below = exchange(full_edges[1], full_edges[0], "row")
        (w,) = call(
            second_filter_kernel, [field], [VMEM] * 3, (u, sides, band_rows), limit=4
        )
        return w, above, below, *unsorted

    w, above, below = smooth(z_first, strips)
    p, ps, z, strips, sums, flat_rows = call(
        image_one_kernel,
        [field, station_field, field, strips_shape, shape((GROUP, LANES), F32), shape((steps, slots), F32)],
        [SMEM] + [VMEM] * 11,
        (bounds, w, above, below, edge, grid_noise, b, sb, info, ut, gv, sv),
        [pltpu.VMEM((steps, GROUP, lanes), F32), extra],
    )
    w, above, below, unsorted = smooth(z, strips, flat_rows, rank)
    q, message = call(
        image_two_kernel,
        [field, shape((devices, LANES), F32)],
        [VMEM] * 13,
        (w, above, below, edge, grid_noise, b, p, z_first, z, sb, ps, info, sums),
        [extra],
        limit=4,
    )
    received = lax.all_to_all(message, ("row", "col"), 0, 0, tiled=True)
    solution_grid, residual_grid, solution_stations = pl.pallas_call(
        final_kernel,
        out_shape=[field, field, shape((steps, 1, 1, slots), F32)],
        in_specs=[VMEM] * 6,
        out_specs=[ANY, ANY, ANY],
        scratch_shapes=[
            pltpu.VMEM((steps, rows, cols), F32),
            pltpu.VMEM((steps, rows, cols), F32),
            pltpu.VMEM((steps, 1, 1, slots), F32),
            pltpu.SemaphoreType.DMA((2, steps // 2)),
            pltpu.SemaphoreType.DMA(()),
        ],
        compiler_params=pltpu.CompilerParams(vmem_limit_bytes=10 * 2**20),
    )(received, b, p, q, own, unsorted)
    return solution_grid, solution_stations, residual_grid


def solution(mesh):
    placed = (
        P(None, "row", "col"),
        P("row", "col"),
        P(None, "row", "col", None),
        P("row", "col", None),
        P(None, "row", "col", None),
        P("row", "col", None),
        P("row", "col"),
        P(),
    )
    return jax.shard_map(
        body,
        mesh=mesh,
        in_specs=placed,
        out_specs=(P(None, "row", "col"), P(None, "row", "col", None), P(None, "row", "col")),
        check_vma=False,
    )
```

```python
import functools

import jax
import jax.numpy as jnp
from jax import lax
from jax.experimental import pallas as pl
from jax.experimental.pallas import tpu as pltpu
from jax.sharding import PartitionSpec as P

REACH = 8
LANES = 128
GROUP = 8
F32 = jnp.float32
BF16 = jnp.bfloat16
HIGHEST = lax.Precision.HIGHEST


def iota(shape, dim):
    return lax.broadcasted_iota(jnp.int32, shape, dim)


def taper(distance):
    spread = jnp.abs(distance).astype(F32)
    value = (1.0 - spread / (REACH + 1)) * jnp.exp(-spread / 3.0)
    return jnp.where(jnp.abs(distance) <= REACH, value, 0.0)


def split(x):
    high = x.astype(BF16)
    return high, (x - high.astype(F32)).astype(BF16)


def pair(x):
    high, low = split(x)
    return jnp.concatenate([high, low], axis=1)


def dot(a, b):
    return jnp.dot(a, b, preferred_element_type=F32)


def dot_nt(a, b):
    return lax.dot_general(a, b, (((1,), (1,)), ((), ())), preferred_element_type=F32)


def halves(x):
    width = x.shape[1] // 2
    return x[:, :width] + x[:, width:]


def three(x):
    high = x.astype(BF16)
    rest = x - high.astype(F32)
    middle = rest.astype(BF16)
    low = (rest - middle.astype(F32)).astype(BF16)
    return jnp.concatenate([high, middle, low], axis=0)


def cut(x, axis):
    return [
        lax.slice_in_dim(x, start, start + LANES, axis=axis)
        for start in range(0, x.shape[axis], LANES)
    ]


def slot_of(axis, side):
    odd = lax.rem(lax.axis_index(axis), 2)
    return odd if side else 1 - odd


def chunks(steps, size=GROUP):
    return [pl.ds(start, size) for start in range(0, steps, size)]


def rows_of(g):
    return pl.ds(pl.multiple_of(g * GROUP, GROUP), GROUP)


def prepare_kernel(
    count, cell_any, offset_any, noise_any, obs_any, base_any,
    base, z, strips, sb, info, rank_out, own, sv, gv, ut, bounds,
    cell_v, offset_v, noise_v, obs_v, bounds_v, table, sorted_rows, copies,
):
    base_copy = pltpu.make_async_copy(base_any, base, copies.at[0])
    base_copy.start()
    small = [
        pltpu.make_async_copy(source, target, copies.at[1 + place])
        for place, (source, target) in enumerate(
            ((cell_any, cell_v), (offset_any, offset_v), (noise_any, noise_v), (obs_any, obs_v))
        )
    ]
    for copy in small:
        copy.start()
    for copy in small:
        copy.wait()
    cell, noise = cell_v[0], noise_v[0]
    steps, slots = own.shape
    tiles = slots // LANES
    rows = base.shape[1]
    groups = rows // GROUP
    slot = iota((1, slots), 1)
    live = slot < count[0, 0]
    where_row = cell // LANES
    where_col = cell - where_row * LANES
    key = jnp.where(live, where_row, rows) * slots + slot
    key = key.astype(F32)
    total = jnp.zeros((1, slots), F32)
    for block in range(tiles):
        piece = key[:, block * LANES : (block + 1) * LANES]
        column = jnp.transpose(jnp.broadcast_to(piece, (LANES, LANES)))
        column = jnp.concatenate([column] * tiles, axis=1)
        less = jnp.where(column < key, 1.0, 0.0)
        total = total + jnp.sum(less, axis=0, keepdims=True)
    rank = total.astype(jnp.int32)
    rank_out[...] = rank
    lived = jnp.where(live, 1.0, 0.0)
    for step in range(steps):
        own[pl.ds(step, 1), :] = obs_v[step, 0] * lived
    table[pl.ds(0, steps), :] = own[...]
    table[pl.ds(steps, 1), :] = where_row.astype(F32)
    table[pl.ds(steps + 1, 1), :] = where_col.astype(F32)
    table[pl.ds(steps + 2, 1), :] = offset_v[0, 0]
    table[pl.ds(steps + 3, 1), :] = offset_v[1, 0]
    table[pl.ds(steps + 4, 1), :] = noise
    table[pl.ds(steps + 5, 1), :] = lived
    table[pl.ds(steps + 6, 2), :] = jnp.zeros((2, slots), F32)
    pieces = three(table[...])
    height = table.shape[0]

    def sort_block(block, carry):
        start = pl.multiple_of(block * LANES, LANES)
        order = (iota((LANES, slots), 0) + start == rank).astype(F32).astype(BF16)
        out = dot_nt(pieces, order)
        sorted_rows[:, pl.ds(start, LANES)] = (
            out[:height] + out[height : 2 * height] + out[2 * height :]
        )
        return carry

    lax.fori_loop(0, tiles, sort_block, 0)
    ordered_row = sorted_rows[pl.ds(steps, 1), :]
    ordered_live = sorted_rows[pl.ds(steps + 5, 1), :]
    first_row = (iota((groups, slots), 0) * GROUP).astype(F32)
    before = jnp.where(ordered_row < first_row - 1.0, ordered_live, 0.0)
    until = jnp.where(ordered_row < first_row + GROUP, ordered_live, 0.0)
    low = jnp.sum(before, axis=1, keepdims=True)
    high = jnp.sum(until, axis=1, keepdims=True)
    start_tile = jnp.where(high > low, jnp.floor(low * (1.0 / LANES)), float(tiles))
    stop_tile = jnp.where(high > low, jnp.floor((high - 1.0) * (1.0 / LANES)) + 1.0, 0.0)
    lane = iota((groups, LANES), 1)
    span = jnp.max(stop_tile - start_tile, axis=0, keepdims=True)
    bounds_v[...] = jnp.where(
        lane == 0, start_tile, jnp.where(lane == 1, stop_tile, span)
    ).astype(jnp.int32)
    bounds_copy = pltpu.make_async_copy(bounds_v, bounds, copies.at[5])
    bounds_copy.start()
    extra = pl.ds(slots, 2 * LANES)
    sb[:, :, extra] = jnp.zeros((steps, GROUP, 2 * LANES), F32)
    info[:, :, extra] = jnp.zeros((2, GROUP, 2 * LANES), F32)
    sv[:, extra, :] = jnp.zeros((2, 2 * LANES, 2 * LANES), BF16)
    gv[:, extra] = jnp.zeros((3 * LANES, 2 * LANES), BF16)
    ut[:, extra] = jnp.zeros((rows, 2 * LANES), F32)
    for block in range(tiles):
        lanes = pl.ds(block * LANES, LANES)
        at_row = sorted_rows[pl.ds(steps, 1), lanes].astype(jnp.int32)
        at_col = sorted_rows[pl.ds(steps + 1, 1), lanes].astype(jnp.int32)
        along_row = sorted_rows[pl.ds(steps + 2, 1), lanes]
        along_col = sorted_rows[pl.ds(steps + 3, 1), lanes]
        row = iota((rows, LANES), 0)
        ut[:, lanes] = jnp.where(row == at_row, 1.0 - along_row, 0.0) + jnp.where(
            row == at_row + 1, along_row, 0.0
        )
        col = iota((LANES, LANES), 0)
        across = jnp.where(col == at_col, 1.0 - along_col, 0.0) + jnp.where(
            col == at_col + 1, along_col, 0.0
        )
        high_part, low_part = split(across)
        gv[:, lanes] = jnp.concatenate([high_part, high_part, low_part], axis=0)
        high_part, low_part = split(jnp.transpose(across))
        sv[0, lanes, :] = jnp.concatenate([high_part, low_part], axis=1)
        sv[1, lanes, :] = jnp.concatenate([high_part, jnp.zeros_like(low_part)], axis=1)
        for place in range(2):
            info[place, :, lanes] = jnp.broadcast_to(
                sorted_rows[pl.ds(steps + 4 + place, 1), lanes], (GROUP, LANES)
            )
        for step in range(steps):
            sb[step, :, lanes] = jnp.broadcast_to(
                sorted_rows[pl.ds(step, 1), lanes], (GROUP, LANES)
            )
    bounds_copy.wait()
    base_copy.wait()
    scatter_all(base, z, strips, sb, ut, sv, bounds)


def matrices_kernel(cov, mix, mat, band_rows, band_cols, edge):
    steps = cov.shape[0]
    rows = band_rows.shape[0]
    wide = steps * GROUP
    spread = (iota((wide, steps), 0) // GROUP == iota((wide, steps), 1)).astype(F32)
    spread_t = (iota((steps, wide), 1) // GROUP == iota((steps, wide), 0)).astype(F32)
    expanded = jnp.dot(
        jnp.dot(spread, cov[...], precision=HIGHEST, preferred_element_type=F32),
        spread_t,
        precision=HIGHEST,
        preferred_element_type=F32,
    )
    a = iota((wide, wide), 0)
    b = iota((wide, wide), 1)
    same = (a % GROUP) == (b % GROUP)
    high_part, low_part = split(jnp.where(same, expanded, 0.0))
    mix[...] = jnp.concatenate([high_part, high_part, low_part], axis=1)
    near = taper((b % GROUP) + REACH - (a % GROUP)) * expanded
    near = jnp.concatenate(
        [jnp.concatenate([x[GROUP:], x[:GROUP]], axis=0) for x in cut(near, 0)], axis=0
    )
    mat[0], mat[1] = split(near)
    far = taper(REACH + (a % GROUP) - (b % GROUP)) * expanded
    far = jnp.concatenate(
        [pltpu.roll(x, LANES - GROUP, 1) for x in cut(far, 1)], axis=1
    )
    mat[2], mat[3] = split(far)
    ra = iota((rows, rows), 0)
    rb = iota((rows, rows), 1)
    high_part, low_part = split(0.25 * taper(ra - rb))
    band_rows[...] = jnp.concatenate([high_part, high_part, low_part], axis=1)
    ca = iota((LANES, LANES), 0)
    cb = iota((LANES, LANES), 1)
    high_part, low_part = split(taper(ca - cb))
    band_cols[...] = jnp.concatenate(
        [
            jnp.concatenate([high_part, low_part], axis=1),
            jnp.concatenate([high_part, jnp.zeros_like(low_part)], axis=1),
        ],
        axis=0,
    )
    block_same = (a // GROUP) == (b // GROUP)
    above = 0.25 * taper((a % GROUP) + REACH - (b % GROUP))
    below = 0.25 * taper(REACH + (b % GROUP) - (a % GROUP))
    edge[0], edge[1] = split(jnp.where(block_same, above, 0.0))
    edge[2], edge[3] = split(jnp.where(block_same, below, 0.0))


def tile_lanes(index, count):
    return pl.ds(pl.multiple_of(index * LANES, LANES), count * LANES)


def spread_tiles(g, first, count, sb, ut, sv):
    steps = sb.shape[0]
    lanes = tile_lanes(first, count)
    weight = ut[rows_of(g), lanes][None]
    left = jnp.concatenate(
        [
            pair((sb[times, :, lanes] * weight).reshape(GROUP * GROUP, count * LANES))
            for times in chunks(steps)
        ],
        axis=0,
    )
    right = jnp.concatenate([sv[0, lanes, :], sv[1, lanes, :]], axis=0)
    return halves(dot(left, right)).reshape(steps, GROUP, LANES)


def scatter_all(base, z, strips, sb, ut, sv, bounds):
    groups = base.shape[1] // GROUP

    def run(g, carry):
        value = base[:, rows_of(g), :] + spread_tiles(g, bounds[g, 0], 2, sb, ut, sv)
        z[:, rows_of(g), :] = value
        pack_group(g, value, strips)
        return carry

    lax.fori_loop(0, groups, run, 0, unroll=2)

    @pl.when(bounds[0, 2] > 2)
    def _():
        def crowded(g, carry):
            def more(index, inner):
                z[:, rows_of(g), :] += spread_tiles(g, index, 1, sb, ut, sv)
                return inner

            lax.fori_loop(bounds[g, 0] + 2, bounds[g, 1], more, 0)
            pack_group(g, z[:, rows_of(g), :], strips)
            return carry

        lax.fori_loop(0, groups, crowded, 0)


def pack_group(g, value, strips):
    steps = value.shape[0]
    per = LANES // GROUP
    slot = iota((GROUP, LANES), 1) // GROUP
    for half in range(steps // per):
        left = jnp.zeros((GROUP, LANES), F32)
        right = jnp.zeros((GROUP, LANES), F32)
        for local in range(per):
            moved = value[half * per + local]
            if local:
                moved = pltpu.roll(moved, local * GROUP, 1)
            left = jnp.where(slot == local, moved, left)
            right = jnp.where(slot == (local - 1) % per, moved, right)
        lanes = pl.ds(half * LANES, LANES)
        strips[slot_of("col", 0), rows_of(g), lanes] = left
        strips[slot_of("col", 1), rows_of(g), lanes] = right


def unpack(sides, where_rows, count, step):
    per = LANES // GROUP
    half, local = step // per, step % per
    lane = iota((count, LANES), 1)
    lanes = pl.ds(half * LANES, LANES) if isinstance(step, int) else tile_lanes(half, 1)
    both = jnp.where(lane // GROUP == local, sides[0, where_rows, lanes], sides[1, where_rows, lanes])
    both = pltpu.roll(both, (LANES - local * GROUP) % LANES, 1)
    return jnp.where((lane < GROUP) | (lane >= LANES - GROUP), both, 0.0)


def first_filter_kernel(z, mix, band_cols, u, u_edges, y):
    steps, rows, cols = z.shape
    groups = rows // GROUP
    flat = (steps * GROUP, LANES)

    def across(quad, carry):
        parts = [z[:, rows_of(4 * quad + i), :].reshape(flat) for i in range(4)]
        value = halves(dot(pair(jnp.concatenate(parts, axis=0)), band_cols[...]))
        both = split(value)
        for i in range(4):
            for part in range(2):
                y[2 * quad + i // 2, part, :, pl.ds((i % 2) * LANES, LANES)] = both[part][
                    i * flat[0] : (i + 1) * flat[0]
                ]
        return carry

    lax.fori_loop(0, groups // 4, across, 0)

    def mixing(two, carry):
        right = jnp.concatenate([y[two, 0], y[two, 1], y[two, 0]], axis=0)
        out = dot(mix[...], right)
        u[:, rows_of(2 * two), :] = out[:, :LANES].reshape(steps, GROUP, LANES)
        u[:, rows_of(2 * two + 1), :] = out[:, LANES:].reshape(steps, GROUP, LANES)
        return carry

    lax.fori_loop(0, groups // 2, mixing, 0, unroll=2)
    u_edges[0] = u[:, pl.ds(0, GROUP), :]
    u_edges[1] = u[:, pl.ds(rows - GROUP, GROUP), :]


def filter_unsort_kernel(z, mix, band_cols, flat_rows, rank, u, u_edges, unsorted, y):
    first_filter_kernel(z, mix, band_cols, u, u_edges, y)
    steps, slots = flat_rows.shape
    tiles = slots // LANES
    pieces = three(flat_rows[...])

    def unsort_block(block, carry):
        lanes = tile_lanes(block, 1)
        order = (iota((slots, LANES), 0) == rank[:, lanes]).astype(F32).astype(BF16)
        out = dot(pieces, order)
        unsorted[:, lanes] = out[:steps] + out[steps : 2 * steps] + out[2 * steps :]
        return carry

    lax.fori_loop(0, tiles, unsort_block, 0)


def second_filter_kernel(u, sides, band_rows, w):
    steps, rows, cols = u.shape

    def along(two, carry):
        one = split(u[2 * two])
        other = split(u[2 * two + 1])
        high = jnp.concatenate([one[0], other[0]], axis=1)
        low = jnp.concatenate([one[1], other[1]], axis=1)
        out = dot(band_rows[...], jnp.concatenate([high, low, high], axis=0))
        everything = pl.ds(0, rows)
        w[2 * two] = out[:, :LANES] + unpack(sides, everything, rows, 2 * two)
        w[2 * two + 1] = out[:, LANES:] + unpack(sides, everything, rows, 2 * two + 1)
        return carry

    lax.fori_loop(0, steps // 2, along, 0, unroll=2)


def edge_kernel(first, second, u_edges, mat, band_rows, sides, full_edges):
    steps = u_edges.shape[1]
    rows = first.shape[0]
    for place, source in ((0, first), (1, second)):
        side = slot_of("col", place)
        high, low = split(source[...])
        value = dot(high, mat[2 * side]) + dot(low, mat[2 * side])
        value = value + dot(high, mat[2 * side + 1])
        sides[side] = value
    for which, start in ((0, 0), (1, rows - GROUP)):
        slot = slot_of("row", which)
        for step in range(steps):
            full_edges[slot, step] = u_edges[which, step] + unpack(
                sides, pl.ds(start, GROUP), GROUP, step
            )
    for side in range(2):
        high, low = split(sides[side])
        sides[side] = dot(band_rows[...], jnp.concatenate([high, low, high], axis=0))


def fill_extra(extra, first, second, edge):
    steps = first.shape[0]
    flat = (steps * GROUP, LANES)
    for place, source in ((0, first), (1, second)):
        which = slot_of("row", place)
        both = pair(source[...].reshape(flat))
        value = halves(dot(edge[2 * which], both)) + dot(edge[2 * which + 1], both[:, :LANES])
        extra[which] = value.reshape(steps, GROUP, LANES)
    extra[2] = jnp.zeros((steps, GROUP, LANES), F32)


def which_extra(g, groups):
    return jnp.where(g == 0, 0, jnp.where(g == groups - 1, 1, 2))


def gather_tiles(g, both, first, count, acc, ut, gv):
    steps = acc.shape[0]
    lanes = tile_lanes(first, count)
    out = dot(both, gv[:, lanes]).reshape(steps, GROUP, count * LANES)
    weight = ut[rows_of(g), lanes][None]
    for times in chunks(steps):
        acc[times, :, lanes] += out[times.start : times.start + times.size] * weight


def left_of(value):
    steps = value.shape[0]
    high, low = split(value.reshape(steps * GROUP, LANES))
    return jnp.concatenate([high, low, high], axis=1)


def whole(x):
    return jnp.sum(jnp.sum(x, axis=1, keepdims=True), axis=0, keepdims=True)


def fold(x):
    return jnp.sum(x, axis=0)


def image_one_kernel(
    bounds, w, above, below, edge, noise, b, sb, info, ut, gv, sv,
    p, ps, z, strips, sums, flat_rows, acc, extra,
):
    steps, rows, _ = w.shape
    groups = rows // GROUP
    slots = sb.shape[2] - 2 * LANES
    tiles = slots // LANES
    fill_extra(extra, above, below, edge)
    acc[...] = jnp.zeros_like(acc)

    def run(g, carry):
        here = rows_of(g)
        which = which_extra(g, groups)
        spread = noise[here, :][None]
        first, second, third = carry
        left = []
        for times in chunks(steps):
            value = w[times, here, :] + extra[which, times]
            left.append(left_of(value))
            mine = b[times, here, :]
            image = value + spread * mine
            p[times, here, :] = image
            first = first + fold(mine * mine)
            second = second + fold(mine * image)
            third = third + fold(image * image)
        gather_tiles(g, jnp.concatenate(left, axis=0), bounds[g, 0], 2, acc, ut, gv)
        return first, second, third

    zero = jnp.zeros((GROUP, LANES), F32)
    carry = lax.fori_loop(0, groups, run, (zero,) * 3, unroll=2)

    @pl.when(bounds[0, 2] > 2)
    def _():
        def crowded(g, inner):
            value = w[:, rows_of(g), :] + extra[which_extra(g, groups)]

            def more(index, innermost):
                gather_tiles(g, left_of(value), index, 1, acc, ut, gv)
                return innermost

            return lax.fori_loop(bounds[g, 0] + 2, bounds[g, 1], more, inner)

        lax.fori_loop(0, groups, crowded, 0)

    def stations(index, carry):
        lanes = tile_lanes(index, 1)
        sampled = jnp.sum(acc[:, :, lanes], axis=1, keepdims=True)
        mine = sb[:, :, lanes]
        live = info[1, :, lanes][None]
        image = live * (sampled + info[0, :, lanes][None] * mine) + (1.0 - live) * mine
        ps[:, :, lanes] = image
        for step in range(steps):
            flat_rows[pl.ds(step, 1), lanes] = image[step, 0:1]
        part = 1.0 / GROUP
        return (
            carry[0] + part * fold(mine * mine),
            carry[1] + part * fold(mine * image),
            carry[2] + part * fold(image * image),
        )

    carry = lax.fori_loop(0, tiles, stations, carry)
    ps[:, :, pl.ds(slots, 2 * LANES)] = jnp.zeros((steps, GROUP, 2 * LANES), F32)
    bb, bp, pp = (whole(x) for x in carry)
    lane = iota((GROUP, LANES), 1)
    value = jnp.where(lane == 0, bb / bp, 0.0)
    value = jnp.where(lane == 1, bb, value)
    value = jnp.where(lane == 2, bp, value)
    value = jnp.where(lane == 3, pp, value)
    sums[...] = value
    scatter_all(p, z, strips, ps, ut, sv, bounds)


def image_two_kernel(
    w, above, below, edge, noise, b, p, z_first, z, sb, ps, info, sums,
    q, message, extra,
):
    steps, rows, _ = w.shape
    groups = rows // GROUP
    tiles = sb.shape[2] // LANES - 2
    fill_extra(extra, above, below, edge)
    shift = jnp.broadcast_to(sums[0:1, 0:1], (GROUP, LANES))[None]

    def run(g, carry):
        here = rows_of(g)
        which = which_extra(g, groups)
        spread = noise[here, :][None]
        first, second, third = carry
        for times in chunks(steps, 4):
            value = w[times, here, :] + extra[which, times]
            mine = p[times, here, :]
            scaled = spread * mine
            q[times, here, :] = value + scaled
            residual = b[times, here, :] - shift * mine
            image = z[times, here, :]
            moved = z_first[times, here, :] - shift * image
            first = first + fold(residual * residual)
            second = second + fold(moved * value + residual * scaled)
            third = third + fold(image * value + mine * scaled)
        return first, second, third

    zero = jnp.zeros((GROUP, LANES), F32)
    carry = lax.fori_loop(0, groups, run, (zero,) * 3)

    def stations(index, carry):
        lanes = tile_lanes(index, 1)
        mine = ps[:, :, lanes]
        live = info[1, :, lanes]
        scaled = (live * info[0, :, lanes] + (1.0 - live))[None] * mine
        residual = sb[:, :, lanes] - shift * mine
        part = 1.0 / GROUP
        return (
            carry[0] + part * fold(residual * residual),
            carry[1] + part * fold(residual * scaled),
            carry[2] + part * fold(mine * scaled),
        )

    carry = lax.fori_loop(0, tiles, stations, carry)
    lane = iota((1, LANES), 1)
    value = jnp.where(lane < 4, sums[0:1, :], 0.0)
    for place, x in enumerate(carry):
        value = jnp.where(lane == 4 + place, whole(x), value)
    message[...] = jnp.broadcast_to(value, message.shape)


def final_kernel(
    received, b, p, q, own, unsorted, solution_out, residual_out, station_out,
    solution_v, residual_v, station_v, sems, station_sem,
):
    everything = received[...]

    def column(index):
        return everything[:, index : index + 1]

    def total(x):
        return jnp.sum(x, axis=0, keepdims=True)

    shift, bb, bp, pp = (column(i) for i in range(4))
    rr, rq, pq = (column(i) for i in range(4, 7))
    norm = total(bb)
    alpha = norm / total(bp)
    delta = shift - alpha
    rp = bp - shift * pp
    ru = rp - shift * rq
    pu = pp - shift * pq
    norm_next = total(rr + 2.0 * delta * rp + delta * delta * pp)
    energy = total(ru + delta * (rq + pu) + delta * delta * pq)
    beta = norm_next / norm
    alpha_next = norm_next / (energy - beta * norm_next / alpha)
    along = alpha + alpha_next * (1.0 + beta)
    twice = alpha_next * alpha
    steps, rows, _ = b.shape
    chunk = 64
    tall = (chunk // GROUP, GROUP, LANES)
    wide_along = jnp.broadcast_to(along, (GROUP, LANES))[None]
    wide_twice = jnp.broadcast_to(twice, (GROUP, LANES))[None]

    def copies(place):
        here = pl.ds(place * 2, 2)
        return (
            pltpu.make_async_copy(solution_v.at[here], solution_out.at[here], sems.at[0, place]),
            pltpu.make_async_copy(residual_v.at[here], residual_out.at[here], sems.at[1, place]),
        )

    def run(place, carry):
        for inner in range(2):
            step = place * 2 + inner
            for piece in range(rows // chunk):
                here = pl.ds(piece * chunk, chunk)
                first = b[step, here, :].reshape(tall)
                second = p[step, here, :].reshape(tall)
                third = q[step, here, :].reshape(tall)
                solution_v[step, here, :] = (wide_along * first - wide_twice * second).reshape(
                    chunk, LANES
                )
                residual_v[step, here, :] = (
                    first - wide_along * second + wide_twice * third
                ).reshape(chunk, LANES)
        for copy in copies(place):
            copy.start()
        return carry

    lax.fori_loop(0, steps // 2, run, 0)
    stations = along * own[...] - twice * unsorted[...]
    for step in range(steps):
        station_v[step, 0] = stations[step : step + 1]
    station_copy = pltpu.make_async_copy(station_v, station_out, station_sem)
    station_copy.start()

    def finish(place, carry):
        for copy in copies(place):
            copy.wait()
        return carry

    lax.fori_loop(0, steps // 2, finish, 0)
    station_copy.wait()


VMEM = pl.BlockSpec(memory_space=pltpu.VMEM)
SMEM = pl.BlockSpec(memory_space=pltpu.SMEM)
ANY = pl.BlockSpec(memory_space=pltpu.HBM)


def call(kernel, outs, ins, operands, scratch=(), flops=10**9, moved=10**7, limit=8, **extra):
    return pl.pallas_call(
        kernel,
        out_shape=outs,
        in_specs=ins,
        out_specs=[VMEM] * len(outs),
        scratch_shapes=list(scratch),
        compiler_params=pltpu.CompilerParams(vmem_limit_bytes=limit * 2**20),
        cost_estimate=pl.CostEstimate(flops=flops, bytes_accessed=moved, transcendentals=0),
        **extra,
    )(*operands)


def exchange(both, axis):
    count = lax.axis_size(axis)
    pairs = [[(i, i + 1) for i in range(start, count - 1, 2)] for start in (0, 1)]
    return tuple(
        lax.ppermute(both[place], axis, found + [(b, a) for a, b in found])
        for place, found in enumerate(pairs)
    )


def body(
    grid_obs, grid_noise, station_obs, station_noise, station_offset, station_cell,
    station_count, time_cov,
):
    steps, rows, cols = grid_obs.shape
    slots = station_obs.shape[3]
    wide = steps * GROUP
    groups = rows // GROUP
    lanes = slots + 2 * LANES
    devices = lax.axis_size("row") * lax.axis_size("col")
    shape = jax.ShapeDtypeStruct
    field = shape((steps, rows, cols), F32)
    rim = shape((2, steps, GROUP, cols), F32)
    strips_shape = shape((2, rows, wide), F32)
    station_field = shape((steps, GROUP, lanes), F32)
    extra = pltpu.VMEM((3, steps, GROUP, LANES), F32)
    b, z_first, strips, sb, info, rank, own, sv, gv, ut, bounds = pl.pallas_call(
        prepare_kernel,
        out_shape=[
            field,
            field,
            strips_shape,
            station_field,
            shape((2, GROUP, lanes), F32),
            shape((1, slots), jnp.int32),
            shape((steps, slots), F32),
            shape((2, lanes, 2 * LANES), BF16),
            shape((3 * LANES, lanes), BF16),
            shape((rows, lanes), F32),
            shape((groups, LANES), jnp.int32),
        ],
        in_specs=[SMEM] + [ANY] * 5,
        out_specs=[VMEM] * 10 + [SMEM],
        scratch_shapes=[
            pltpu.VMEM((1, 1, slots), jnp.int32),
            pltpu.VMEM((2, 1, 1, slots), F32),
            pltpu.VMEM((1, 1, slots), F32),
            pltpu.VMEM((steps, 1, 1, slots), F32),
            pltpu.VMEM((groups, LANES), jnp.int32),
            pltpu.VMEM((steps + 8, slots), F32),
            pltpu.VMEM((steps + 8, slots), F32),
            pltpu.SemaphoreType.DMA((6,)),
        ],
        compiler_params=pltpu.CompilerParams(vmem_limit_bytes=8 * 2**20),
        cost_estimate=pl.CostEstimate(flops=10**9, bytes_accessed=10**7, transcendentals=0),
    )(
        station_count,
        *(
            pltpu.with_memory_space_constraint(x, pltpu.HBM)
            for x in (station_cell, station_offset, station_noise, station_obs, grid_obs)
        ),
    )
    mix, mat, band_rows, band_cols, edge = call(
        matrices_kernel,
        [
            shape((wide, 3 * wide), BF16),
            shape((4, wide, wide), BF16),
            shape((rows, 3 * rows), BF16),
            shape((2 * LANES, 2 * LANES), BF16),
            shape((4, wide, wide), BF16),
        ],
        [VMEM],
        (time_cov,),
    )

    def smooth(z, strips, *more):
        from_left, from_right = exchange(strips, "col")
        u, u_edges, *unsorted = call(
            filter_unsort_kernel if more else first_filter_kernel,
            [field, rim] + [shape((steps, slots), F32)] * bool(more),
            [VMEM] * (3 + len(more)),
            (z, mix, band_cols, *more),
            [pltpu.VMEM((groups // 2, 2, wide, 2 * LANES), BF16)],
        )
        sides, full_edges = call(
            edge_kernel,
            [strips_shape, rim],
            [VMEM] * 5,
            (from_left, from_right, u_edges, mat, band_rows),
            limit=4,
        )
        above, below = exchange(full_edges, "row")
        (w,) = call(
            second_filter_kernel, [field], [VMEM] * 3, (u, sides, band_rows), limit=4
        )
        return w, above, below, *unsorted

    w, above, below = smooth(z_first, strips)
    p, ps, z, strips, sums, flat_rows = call(
        image_one_kernel,
        [field, station_field, field, strips_shape, shape((GROUP, LANES), F32), shape((steps, slots), F32)],
        [SMEM] + [VMEM] * 11,
        (bounds, w, above, below, edge, grid_noise, b, sb, info, ut, gv, sv),
        [pltpu.VMEM((steps, GROUP, lanes), F32), extra],
    )
    w, above, below, unsorted = smooth(z, strips, flat_rows, rank)
    q, message = call(
        image_two_kernel,
        [field, shape((devices, LANES), F32)],
        [VMEM] * 13,
        (w, above, below, edge, grid_noise, b, p, z_first, z, sb, ps, info, sums),
        [extra],
        limit=4,
    )
    received = lax.all_to_all(message, ("row", "col"), 0, 0, tiled=True)
    solution_grid, residual_grid, solution_stations = pl.pallas_call(
        final_kernel,
        out_shape=[field, field, shape((steps, 1, 1, slots), F32)],
        in_specs=[VMEM] * 6,
        out_specs=[ANY, ANY, ANY],
        scratch_shapes=[
            pltpu.VMEM((steps, rows, cols), F32),
            pltpu.VMEM((steps, rows, cols), F32),
            pltpu.VMEM((steps, 1, 1, slots), F32),
            pltpu.SemaphoreType.DMA((2, steps // 2)),
            pltpu.SemaphoreType.DMA(()),
        ],
        compiler_params=pltpu.CompilerParams(vmem_limit_bytes=10 * 2**20),
    )(received, b, p, q, own, unsorted)
    return solution_grid, solution_stations, residual_grid


def solution(mesh):
    placed = (
        P(None, "row", "col"),
        P("row", "col"),
        P(None, "row", "col", None),
        P("row", "col", None),
        P(None, "row", "col", None),
        P("row", "col", None),
        P("row", "col"),
        P(),
    )
    return jax.shard_map(
        body,
        mesh=mesh,
        in_specs=placed,
        out_specs=(P(None, "row", "col"), P(None, "row", "col", None), P(None, "row", "col")),
        check_vma=False,
    )
```

```python
import functools

import jax
import jax.numpy as jnp
from jax import lax
from jax.experimental import pallas as pl
from jax.experimental.pallas import tpu as pltpu
from jax.sharding import PartitionSpec as P

REACH = 8
LANES = 128
HALF = LANES // 2
GROUP = 8
F32 = jnp.float32
BF16 = jnp.bfloat16
HIGHEST = lax.Precision.HIGHEST


def iota(shape, dim):
    return lax.broadcasted_iota(jnp.int32, shape, dim)


def taper(distance):
    spread = jnp.abs(distance).astype(F32)
    value = (1.0 - spread / (REACH + 1)) * jnp.exp(-spread / 3.0)
    return jnp.where(jnp.abs(distance) <= REACH, value, 0.0)


def split(x):
    high = x.astype(BF16)
    return high, (x - high.astype(F32)).astype(BF16)


def pair(x):
    high, low = split(x)
    return jnp.concatenate([high, low], axis=1)


def doubled(weights):
    high, low = split(weights)
    return jnp.concatenate(
        [
            jnp.concatenate([high, low], axis=1),
            jnp.concatenate([high, jnp.zeros_like(low)], axis=1),
        ],
        axis=0,
    )


def dot(a, b):
    return jnp.dot(a, b, preferred_element_type=F32)


def dot_nt(a, b):
    return lax.dot_general(a, b, (((1,), (1,)), ((), ())), preferred_element_type=F32)


def halves(x):
    width = x.shape[1] // 2
    return x[:, :width] + x[:, width:]


def three(x):
    high = x.astype(BF16)
    rest = x - high.astype(F32)
    middle = rest.astype(BF16)
    low = (rest - middle.astype(F32)).astype(BF16)
    return jnp.concatenate([high, middle, low], axis=0)


def cut(x, axis):
    return [
        lax.slice_in_dim(x, start, start + LANES, axis=axis)
        for start in range(0, x.shape[axis], LANES)
    ]


def slot_of(axis, side):
    odd = lax.rem(lax.axis_index(axis), 2)
    return odd if side else 1 - odd


def chunks(steps, size=GROUP):
    return [pl.ds(start, size) for start in range(0, steps, size)]


def rows_of(g):
    return pl.ds(pl.multiple_of(g * GROUP, GROUP), GROUP)


def prepare_kernel(
    count, cell_any, offset_any, noise_any, obs_any, base_any,
    base, z, strips, sb, info, rank_out, own, sv, gv, ut, bounds,
    cell_v, offset_v, noise_v, obs_v, bounds_v, table, sorted_rows, shifted_rows, copies,
):
    base_copy = pltpu.make_async_copy(base_any, base, copies.at[0])
    base_copy.start()
    small = [
        pltpu.make_async_copy(source, target, copies.at[1 + place])
        for place, (source, target) in enumerate(
            ((cell_any, cell_v), (offset_any, offset_v), (noise_any, noise_v), (obs_any, obs_v))
        )
    ]
    for copy in small:
        copy.start()
    for copy in small:
        copy.wait()
    cell, noise = cell_v[0], noise_v[0]
    steps, slots = own.shape
    tiles = slots // LANES
    rows = base.shape[1]
    groups = rows // GROUP
    slot = iota((1, slots), 1)
    live = slot < count[0, 0]
    where_row = cell // LANES
    where_col = cell - where_row * LANES
    key = jnp.where(live, where_row, rows) * slots + slot
    key = key.astype(F32)
    total = jnp.zeros((1, slots), F32)
    for block in range(tiles):
        piece = key[:, block * LANES : (block + 1) * LANES]
        column = jnp.transpose(jnp.broadcast_to(piece, (LANES, LANES)))
        column = jnp.concatenate([column] * tiles, axis=1)
        less = jnp.where(column < key, 1.0, 0.0)
        total = total + jnp.sum(less, axis=0, keepdims=True)
    rank = total.astype(jnp.int32)
    rank_out[...] = rank
    lived = jnp.where(live, 1.0, 0.0)
    for step in range(steps):
        own[pl.ds(step, 1), :] = obs_v[step, 0] * lived
    table[pl.ds(0, steps), :] = own[...]
    table[pl.ds(steps, 1), :] = where_row.astype(F32)
    table[pl.ds(steps + 1, 1), :] = where_col.astype(F32)
    table[pl.ds(steps + 2, 1), :] = offset_v[0, 0]
    table[pl.ds(steps + 3, 1), :] = offset_v[1, 0]
    table[pl.ds(steps + 4, 1), :] = noise
    table[pl.ds(steps + 5, 1), :] = lived
    table[pl.ds(steps + 6, 2), :] = jnp.zeros((2, slots), F32)
    pieces = three(table[...])
    height = table.shape[0]

    def sort_block(block, carry):
        start = pl.multiple_of(block * LANES, LANES)
        order = (iota((LANES, slots), 0) + start == rank).astype(F32).astype(BF16)
        out = dot_nt(pieces, order)
        sorted_rows[:, pl.ds(start, LANES)] = (
            out[:height] + out[height : 2 * height] + out[2 * height :]
        )
        return carry

    lax.fori_loop(0, tiles, sort_block, 0, unroll=2)
    ordered_row = sorted_rows[pl.ds(steps, 1), :]
    ordered_live = sorted_rows[pl.ds(steps + 5, 1), :]
    first_row = (iota((groups, slots), 0) * GROUP).astype(F32)
    before = jnp.where(ordered_row < first_row - 1.0, ordered_live, 0.0)
    until = jnp.where(ordered_row < first_row + GROUP, ordered_live, 0.0)
    low = jnp.sum(before, axis=1, keepdims=True)
    high = jnp.sum(until, axis=1, keepdims=True)
    start_tile = jnp.where(high > low, jnp.floor(low * (1.0 / HALF)), float(2 * tiles))
    reached = jnp.where(high > low, high - HALF * start_tile, 1.0)
    needed = jnp.floor((reached + (LANES - 1.0)) * (1.0 / LANES))
    most = jnp.max(needed, axis=0, keepdims=True)
    lane = iota((groups, LANES), 1)
    bounds_v[...] = jnp.where(
        lane == 0, start_tile, jnp.where(lane == 1, needed, most)
    ).astype(jnp.int32)
    bounds_copy = pltpu.make_async_copy(bounds_v, bounds, copies.at[5])
    bounds_copy.start()
    lane = iota(shifted_rows.shape[:1] + (LANES,), 1)
    for block in range(tiles):
        lanes = pl.ds(block * LANES, LANES)
        after = jnp.zeros((shifted_rows.shape[0], LANES), F32)
        if block + 1 < tiles:
            after = sorted_rows[:, pl.ds((block + 1) * LANES, LANES)]
        shifted_rows[:, lanes] = pltpu.roll(
            jnp.where(lane < HALF, after, sorted_rows[:, lanes]), HALF, 1
        )
        for place in range(2):
            info[place, :, lanes] = jnp.broadcast_to(
                sorted_rows[pl.ds(steps + 4 + place, 1), lanes], (GROUP, LANES)
            )
    none = tile_lanes(2 * tiles, 1)
    sb[:, :, none] = jnp.zeros((steps, GROUP, LANES), F32)
    ut[:, none] = jnp.zeros((rows, LANES), F32)
    for target in (sv, gv):
        target[2 * tiles] = jnp.zeros((2 * LANES, 2 * LANES), BF16)
    for tile in range(2 * tiles):
        source = shifted_rows if tile % 2 else sorted_rows
        place = pl.ds(tile // 2 * LANES, LANES)
        lanes = pl.ds(tile * LANES, LANES)
        at_row = source[pl.ds(steps, 1), place].astype(jnp.int32)
        at_col = source[pl.ds(steps + 1, 1), place].astype(jnp.int32)
        along_row = source[pl.ds(steps + 2, 1), place]
        along_col = source[pl.ds(steps + 3, 1), place]
        row = iota((rows, LANES), 0)
        ut[:, lanes] = jnp.where(
            row == at_row, 1.0 - along_row, jnp.where(row == at_row + 1, along_row, 0.0)
        )
        col = iota((LANES, LANES), 0)
        across = jnp.where(
            col == at_col, 1.0 - along_col, jnp.where(col == at_col + 1, along_col, 0.0)
        )
        gv[tile] = doubled(across)
        sv[tile] = doubled(jnp.transpose(across))
        for step in range(steps):
            sb[step, :, lanes] = jnp.broadcast_to(source[pl.ds(step, 1), place], (GROUP, LANES))
    bounds_copy.wait()
    base_copy.wait()
    scatter_all(base, z, strips, sb, ut, sv, bounds)


def matrices_kernel(cov, mix, mat, band_rows, band_cols, edge):
    steps = cov.shape[0]
    rows = band_rows.shape[0]
    wide = steps * GROUP
    spread = (iota((wide, steps), 0) // GROUP == iota((wide, steps), 1)).astype(F32)
    spread_t = (iota((steps, wide), 1) // GROUP == iota((steps, wide), 0)).astype(F32)
    expanded = jnp.dot(
        jnp.dot(spread, cov[...], precision=HIGHEST, preferred_element_type=F32),
        spread_t,
        precision=HIGHEST,
        preferred_element_type=F32,
    )
    a = iota((wide, wide), 0)
    b = iota((wide, wide), 1)
    same = (a % GROUP) == (b % GROUP)
    high_part, low_part = split(jnp.where(same, expanded, 0.0))
    mix[...] = jnp.concatenate([high_part, high_part, low_part], axis=1)
    near = taper((b % GROUP) + REACH - (a % GROUP)) * expanded
    near = jnp.concatenate(
        [jnp.concatenate([x[GROUP:], x[:GROUP]], axis=0) for x in cut(near, 0)], axis=0
    )
    mat[0], mat[1] = split(near)
    far = taper(REACH + (a % GROUP) - (b % GROUP)) * expanded
    far = jnp.concatenate(
        [pltpu.roll(x, LANES - GROUP, 1) for x in cut(far, 1)], axis=1
    )
    mat[2], mat[3] = split(far)
    ra = iota((rows, rows), 0)
    rb = iota((rows, rows), 1)
    high_part, low_part = split(0.25 * taper(ra - rb))
    band_rows[...] = jnp.concatenate([high_part, high_part, low_part], axis=1)
    ca = iota((LANES, LANES), 0)
    cb = iota((LANES, LANES), 1)
    band_cols[...] = doubled(taper(ca - cb))
    block_same = (a // GROUP) == (b // GROUP)
    above = 0.25 * taper((a % GROUP) + REACH - (b % GROUP))
    below = 0.25 * taper(REACH + (b % GROUP) - (a % GROUP))
    edge[0], edge[1] = split(jnp.where(block_same, above, 0.0))
    edge[2], edge[3] = split(jnp.where(block_same, below, 0.0))


def tile_lanes(index, count):
    return pl.ds(pl.multiple_of(index * LANES, LANES), count * LANES)


def spread_tile(g, index, sb, ut, sv):
    steps = sb.shape[0]
    lanes = tile_lanes(index, 1)
    weight = ut[rows_of(g), lanes][None]
    left = jnp.concatenate(
        [
            pair((sb[times, :, lanes] * weight).reshape(GROUP * GROUP, LANES))
            for times in chunks(steps)
        ],
        axis=0,
    )
    return halves(dot(left, sv[index])).reshape(steps, GROUP, LANES)


def scatter_all(base, z, strips, sb, ut, sv, bounds):
    groups = base.shape[1] // GROUP

    def run(g, carry):
        value = base[:, rows_of(g), :] + spread_tile(g, bounds[g, 0], sb, ut, sv)
        z[:, rows_of(g), :] = value
        pack_group(g, value, strips)
        return carry

    lax.fori_loop(0, groups, run, 0, unroll=2)

    @pl.when(bounds[0, 2] > 1)
    def _():
        def crowded(g, carry):
            def more(index, inner):
                z[:, rows_of(g), :] += spread_tile(g, bounds[g, 0] + 2 * index, sb, ut, sv)
                return inner

            lax.fori_loop(1, bounds[g, 1], more, 0)
            pack_group(g, z[:, rows_of(g), :], strips)
            return carry

        lax.fori_loop(0, groups, crowded, 0)


def pack_group(g, value, strips):
    steps = value.shape[0]
    per = LANES // GROUP
    slot = iota((GROUP, LANES), 1) // GROUP
    for half in range(steps // per):
        left = jnp.zeros((GROUP, LANES), F32)
        right = jnp.zeros((GROUP, LANES), F32)
        for local in range(per):
            moved = value[half * per + local]
            if local:
                moved = pltpu.roll(moved, local * GROUP, 1)
            left = jnp.where(slot == local, moved, left)
            right = jnp.where(slot == (local - 1) % per, moved, right)
        lanes = pl.ds(half * LANES, LANES)
        strips[slot_of("col", 0), rows_of(g), lanes] = left
        strips[slot_of("col", 1), rows_of(g), lanes] = right


def unpack(sides, where_rows, count, step):
    per = LANES // GROUP
    half, local = step // per, step % per
    lane = iota((count, LANES), 1)
    lanes = pl.ds(half * LANES, LANES) if isinstance(step, int) else tile_lanes(half, 1)
    both = jnp.where(lane // GROUP == local, sides[0, where_rows, lanes], sides[1, where_rows, lanes])
    both = pltpu.roll(both, (LANES - local * GROUP) % LANES, 1)
    return jnp.where((lane < GROUP) | (lane >= LANES - GROUP), both, 0.0)


def first_filter_kernel(z, mix, band_cols, u, u_edges, y):
    steps, rows, cols = z.shape
    groups = rows // GROUP
    flat = (steps * GROUP, LANES)

    def across(quad, carry):
        parts = [z[:, rows_of(4 * quad + i), :].reshape(flat) for i in range(4)]
        value = halves(dot(pair(jnp.concatenate(parts, axis=0)), band_cols[...]))
        both = split(value)
        for i in range(4):
            for part in range(2):
                y[2 * quad + i // 2, part, :, pl.ds((i % 2) * LANES, LANES)] = both[part][
                    i * flat[0] : (i + 1) * flat[0]
                ]
        return carry

    lax.fori_loop(0, groups // 4, across, 0)

    def mixing(two, carry):
        right = jnp.concatenate([y[two, 0], y[two, 1], y[two, 0]], axis=0)
        out = dot(mix[...], right)
        u[:, rows_of(2 * two), :] = out[:, :LANES].reshape(steps, GROUP, LANES)
        u[:, rows_of(2 * two + 1), :] = out[:, LANES:].reshape(steps, GROUP, LANES)
        return carry

    lax.fori_loop(0, groups // 2, mixing, 0, unroll=2)
    u_edges[0] = u[:, pl.ds(0, GROUP), :]
    u_edges[1] = u[:, pl.ds(rows - GROUP, GROUP), :]


def filter_unsort_kernel(z, mix, band_cols, flat_rows, rank, u, u_edges, unsorted, y):
    first_filter_kernel(z, mix, band_cols, u, u_edges, y)
    steps, slots = flat_rows.shape
    tiles = slots // LANES
    pieces = three(flat_rows[...])

    def unsort_block(block, carry):
        lanes = tile_lanes(block, 1)
        order = (iota((slots, LANES), 0) == rank[:, lanes]).astype(F32).astype(BF16)
        out = dot(pieces, order)
        unsorted[:, lanes] = out[:steps] + out[steps : 2 * steps] + out[2 * steps :]
        return carry

    lax.fori_loop(0, tiles, unsort_block, 0)


def second_filter_kernel(u, sides, band_rows, w):
    steps, rows, cols = u.shape

    def along(two, carry):
        one = split(u[2 * two])
        other = split(u[2 * two + 1])
        high = jnp.concatenate([one[0], other[0]], axis=1)
        low = jnp.concatenate([one[1], other[1]], axis=1)
        out = dot(band_rows[...], jnp.concatenate([high, low, high], axis=0))
        everything = pl.ds(0, rows)
        w[2 * two] = out[:, :LANES] + unpack(sides, everything, rows, 2 * two)
        w[2 * two + 1] = out[:, LANES:] + unpack(sides, everything, rows, 2 * two + 1)
        return carry

    lax.fori_loop(0, steps // 2, along, 0, unroll=2)


def edge_kernel(first, second, u_edges, mat, band_rows, sides, full_edges):
    steps = u_edges.shape[1]
    rows = first.shape[0]
    for place, source in ((0, first), (1, second)):
        side = slot_of("col", place)
        high, low = split(source[...])
        value = dot(high, mat[2 * side]) + dot(low, mat[2 * side])
        value = value + dot(high, mat[2 * side + 1])
        sides[side] = value
    for which, start in ((0, 0), (1, rows - GROUP)):
        slot = slot_of("row", which)
        for step in range(steps):
            full_edges[slot, step] = u_edges[which, step] + unpack(
                sides, pl.ds(start, GROUP), GROUP, step
            )
    for side in range(2):
        high, low = split(sides[side])
        sides[side] = dot(band_rows[...], jnp.concatenate([high, low, high], axis=0))


def fill_extra(extra, first, second, edge):
    steps = first.shape[0]
    flat = (steps * GROUP, LANES)
    for place, source in ((0, first), (1, second)):
        which = slot_of("row", place)
        both = pair(source[...].reshape(flat))
        value = halves(dot(edge[2 * which], both)) + dot(edge[2 * which + 1], both[:, :LANES])
        extra[which] = value.reshape(steps, GROUP, LANES)
    extra[2] = jnp.zeros((steps, GROUP, LANES), F32)


def which_extra(g, groups):
    return jnp.where(g == 0, 0, jnp.where(g == groups - 1, 1, 2))


def gather_tile(g, both, index, acc, ut, gv):
    steps = acc.shape[0]
    lanes = tile_lanes(index, 1)
    out = halves(dot(both, gv[index])).reshape(steps, GROUP, LANES)
    weight = ut[rows_of(g), lanes][None]
    for times in chunks(steps):
        acc[times, :, lanes] += out[times.start : times.start + times.size] * weight


def whole(x):
    return jnp.sum(jnp.sum(x, axis=1, keepdims=True), axis=0, keepdims=True)


def fold(x):
    return jnp.sum(x, axis=0)


def image_one_kernel(
    bounds, w, above, below, edge, noise, b, sb, info, ut, gv, sv,
    p, ps, z, strips, sums, flat_rows, acc, extra,
):
    steps, rows, _ = w.shape
    groups = rows // GROUP
    tiles = info.shape[2] // LANES
    fill_extra(extra, above, below, edge)
    acc[...] = jnp.zeros_like(acc)

    def run(g, carry):
        here = rows_of(g)
        which = which_extra(g, groups)
        spread = noise[here, :][None]
        first, second, third = carry
        left = []
        for times in chunks(steps):
            value = w[times, here, :] + extra[which, times]
            left.append(pair(value.reshape(GROUP * GROUP, LANES)))
            mine = b[times, here, :]
            image = value + spread * mine
            p[times, here, :] = image
            first = first + fold(mine * mine)
            second = second + fold(mine * image)
            third = third + fold(image * image)
        gather_tile(g, jnp.concatenate(left, axis=0), bounds[g, 0], acc, ut, gv)
        return first, second, third

    zero = jnp.zeros((GROUP, LANES), F32)
    carry = lax.fori_loop(0, groups, run, (zero,) * 3, unroll=2)

    @pl.when(bounds[0, 2] > 1)
    def _():
        def crowded(g, inner):
            value = w[:, rows_of(g), :] + extra[which_extra(g, groups)]
            both = pair(value.reshape(steps * GROUP, LANES))

            def more(index, innermost):
                gather_tile(g, both, bounds[g, 0] + 2 * index, acc, ut, gv)
                return innermost

            return lax.fori_loop(1, bounds[g, 1], more, inner)

        lax.fori_loop(0, groups, crowded, 0)

    lane = iota((1, 1, LANES), 2)
    none = 2 * tiles

    def stations(index, carry):
        lanes = tile_lanes(2 * index, 1)
        place = tile_lanes(index, 1)
        before = tile_lanes(jnp.where(index == 0, none, 2 * index - 1), 1)
        after = tile_lanes(2 * index + 1, 1)
        first, second, third = carry
        part = 1.0 / GROUP
        live = info[1, :, place][None]
        spread = live * info[0, :, place][None] + (1.0 - live)
        for times in chunks(steps):
            other = jnp.where(lane < HALF, acc[times, :, after], acc[times, :, before])
            mixed = acc[times, :, lanes] + pltpu.roll(other, HALF, 2)
            sampled = jnp.sum(mixed, axis=1, keepdims=True)
            mine = sb[times, :, lanes]
            image = live * sampled + spread * mine
            ps[times, :, lanes] = image
            for step in range(GROUP):
                flat_rows[pl.ds(times.start + step, 1), place] = image[step, 0:1]
            first = first + part * fold(mine * mine)
            second = second + part * fold(mine * image)
            third = third + part * fold(image * image)
        return first, second, third

    carry = lax.fori_loop(0, tiles, stations, carry)
    ps[:, :, tile_lanes(none, 1)] = jnp.zeros((steps, GROUP, LANES), F32)

    def between(index, inner):
        for times in chunks(steps):
            other = jnp.where(
                lane < HALF,
                ps[times, :, tile_lanes(2 * index + 2, 1)],
                ps[times, :, tile_lanes(2 * index, 1)],
            )
            ps[times, :, tile_lanes(2 * index + 1, 1)] = pltpu.roll(other, HALF, 2)
        return inner

    lax.fori_loop(0, tiles, between, 0)
    bb, bp, pp = (whole(x) for x in carry)
    lane = iota((GROUP, LANES), 1)
    value = jnp.where(lane == 0, bb / bp, 0.0)
    value = jnp.where(lane == 1, bb, value)
    value = jnp.where(lane == 2, bp, value)
    value = jnp.where(lane == 3, pp, value)
    sums[...] = value
    scatter_all(p, z, strips, ps, ut, sv, bounds)


def image_two_kernel(
    w, above, below, edge, noise, b, p, z_first, z, sb, ps, info, sums,
    q, message, extra,
):
    steps, rows, _ = w.shape
    groups = rows // GROUP
    tiles = info.shape[2] // LANES
    fill_extra(extra, above, below, edge)
    shift = jnp.broadcast_to(sums[0:1, 0:1], (GROUP, LANES))[None]

    def run(g, carry):
        here = rows_of(g)
        which = which_extra(g, groups)
        spread = noise[here, :][None]
        first, second, third = carry
        for times in chunks(steps, 4):
            value = w[times, here, :] + extra[which, times]
            mine = p[times, here, :]
            scaled = spread * mine
            q[times, here, :] = value + scaled
            residual = b[times, here, :] - shift * mine
            image = z[times, here, :]
            moved = z_first[times, here, :] - shift * image
            first = first + fold(residual * residual)
            second = second + fold(moved * value + residual * scaled)
            third = third + fold(image * value + mine * scaled)
        return first, second, third

    zero = jnp.zeros((GROUP, LANES), F32)
    carry = lax.fori_loop(0, groups, run, (zero,) * 3)

    def stations(index, carry):
        lanes = tile_lanes(2 * index, 1)
        place = tile_lanes(index, 1)
        mine = ps[:, :, lanes]
        live = info[1, :, place]
        scaled = (live * info[0, :, place] + (1.0 - live))[None] * mine
        residual = sb[:, :, lanes] - shift * mine
        part = 1.0 / GROUP
        return (
            carry[0] + part * fold(residual * residual),
            carry[1] + part * fold(residual * scaled),
            carry[2] + part * fold(mine * scaled),
        )

    carry = lax.fori_loop(0, tiles, stations, carry)
    lane = iota((1, LANES), 1)
    value = jnp.where(lane < 4, sums[0:1, :], 0.0)
    for place, x in enumerate(carry):
        value = jnp.where(lane == 4 + place, whole(x), value)
    message[...] = jnp.broadcast_to(value, message.shape)


def final_kernel(
    received, b, p, q, own, unsorted, solution_out, residual_out, station_out,
    solution_v, residual_v, station_v, sems, station_sem,
):
    everything = received[...]

    def column(index):
        return everything[:, index : index + 1]

    def total(x):
        return jnp.sum(x, axis=0, keepdims=True)

    shift, bb, bp, pp = (column(i) for i in range(4))
    rr, rq, pq = (column(i) for i in range(4, 7))
    norm = total(bb)
    alpha = norm / total(bp)
    delta = shift - alpha
    rp = bp - shift * pp
    ru = rp - shift * rq
    pu = pp - shift * pq
    norm_next = total(rr + 2.0 * delta * rp + delta * delta * pp)
    energy = total(ru + delta * (rq + pu) + delta * delta * pq)
    beta = norm_next / norm
    alpha_next = norm_next / (energy - beta * norm_next / alpha)
    along = alpha + alpha_next * (1.0 + beta)
    twice = alpha_next * alpha
    steps, rows, _ = b.shape
    chunk = 64
    tall = (chunk // GROUP, GROUP, LANES)
    wide_along = jnp.broadcast_to(along, (GROUP, LANES))[None]
    wide_twice = jnp.broadcast_to(twice, (GROUP, LANES))[None]

    def copies(place):
        here = pl.ds(place * 2, 2)
        return (
            pltpu.make_async_copy(solution_v.at[here], solution_out.at[here], sems.at[0, place]),
            pltpu.make_async_copy(residual_v.at[here], residual_out.at[here], sems.at[1, place]),
        )

    def run(place, carry):
        for inner in range(2):
            step = place * 2 + inner
            for piece in range(rows // chunk):
                here = pl.ds(piece * chunk, chunk)
                first = b[step, here, :].reshape(tall)
                second = p[step, here, :].reshape(tall)
                third = q[step, here, :].reshape(tall)
                solution_v[step, here, :] = (wide_along * first - wide_twice * second).reshape(
                    chunk, LANES
                )
                residual_v[step, here, :] = (
                    first - wide_along * second + wide_twice * third
                ).reshape(chunk, LANES)
        for copy in copies(place):
            copy.start()
        return carry

    lax.fori_loop(0, steps // 2, run, 0)
    stations = along * own[...] - twice * unsorted[...]
    for step in range(steps):
        station_v[step, 0] = stations[step : step + 1]
    station_copy = pltpu.make_async_copy(station_v, station_out, station_sem)
    station_copy.start()

    def finish(place, carry):
        for copy in copies(place):
            copy.wait()
        return carry

    lax.fori_loop(0, steps // 2, finish, 0)
    station_copy.wait()


VMEM = pl.BlockSpec(memory_space=pltpu.VMEM)
SMEM = pl.BlockSpec(memory_space=pltpu.SMEM)
ANY = pl.BlockSpec(memory_space=pltpu.HBM)


def call(kernel, outs, ins, operands, scratch=(), flops=10**9, moved=10**7, limit=8, **extra):
    return pl.pallas_call(
        kernel,
        out_shape=outs,
        in_specs=ins,
        out_specs=[VMEM] * len(outs),
        scratch_shapes=list(scratch),
        compiler_params=pltpu.CompilerParams(vmem_limit_bytes=limit * 2**20),
        cost_estimate=pl.CostEstimate(flops=flops, bytes_accessed=moved, transcendentals=0),
        **extra,
    )(*operands)


def exchange(both, axis):
    count = lax.axis_size(axis)
    pairs = [[(i, i + 1) for i in range(start, count - 1, 2)] for start in (0, 1)]
    return tuple(
        lax.ppermute(both[place], axis, found + [(b, a) for a, b in found])
        for place, found in enumerate(pairs)
    )


def body(
    grid_obs, grid_noise, station_obs, station_noise, station_offset, station_cell,
    station_count, time_cov,
):
    steps, rows, cols = grid_obs.shape
    slots = station_obs.shape[3]
    wide = steps * GROUP
    groups = rows // GROUP
    tiles = 2 * (slots // LANES) + 1
    lanes = tiles * LANES
    devices = lax.axis_size("row") * lax.axis_size("col")
    shape = jax.ShapeDtypeStruct
    field = shape((steps, rows, cols), F32)
    rim = shape((2, steps, GROUP, cols), F32)
    strips_shape = shape((2, rows, wide), F32)
    station_field = shape((steps, GROUP, lanes), F32)
    extra = pltpu.VMEM((3, steps, GROUP, LANES), F32)
    b, z_first, strips, sb, info, rank, own, sv, gv, ut, bounds = pl.pallas_call(
        prepare_kernel,
        out_shape=[
            field,
            field,
            strips_shape,
            station_field,
            shape((2, GROUP, slots), F32),
            shape((1, slots), jnp.int32),
            shape((steps, slots), F32),
            shape((tiles, 2 * LANES, 2 * LANES), BF16),
            shape((tiles, 2 * LANES, 2 * LANES), BF16),
            shape((rows, lanes), F32),
            shape((groups, LANES), jnp.int32),
        ],
        in_specs=[SMEM] + [ANY] * 5,
        out_specs=[VMEM] * 10 + [SMEM],
        scratch_shapes=[
            pltpu.VMEM((1, 1, slots), jnp.int32),
            pltpu.VMEM((2, 1, 1, slots), F32),
            pltpu.VMEM((1, 1, slots), F32),
            pltpu.VMEM((steps, 1, 1, slots), F32),
            pltpu.VMEM((groups, LANES), jnp.int32),
            pltpu.VMEM((steps + 8, slots), F32),
            pltpu.VMEM((steps + 8, slots), F32),
            pltpu.VMEM((steps + 8, slots), F32),
            pltpu.SemaphoreType.DMA((6,)),
        ],
        compiler_params=pltpu.CompilerParams(vmem_limit_bytes=8 * 2**20),
        cost_estimate=pl.CostEstimate(flops=10**9, bytes_accessed=10**7, transcendentals=0),
    )(
        station_count,
        *(
            pltpu.with_memory_space_constraint(x, pltpu.HBM)
            for x in (station_cell, station_offset, station_noise, station_obs, grid_obs)
        ),
    )
    mix, mat, band_rows, band_cols, edge = call(
        matrices_kernel,
        [
            shape((wide, 3 * wide), BF16),
            shape((4, wide, wide), BF16),
            shape((rows, 3 * rows), BF16),
            shape((2 * LANES, 2 * LANES), BF16),
            shape((4, wide, wide), BF16),
        ],
        [VMEM],
        (time_cov,),
    )

    def smooth(z, strips, *more):
        from_left, from_right = exchange(strips, "col")
        u, u_edges, *unsorted = call(
            filter_unsort_kernel if more else first_filter_kernel,
            [field, rim] + [shape((steps, slots), F32)] * bool(more),
            [VMEM] * (3 + len(more)),
            (z, mix, band_cols, *more),
            [pltpu.VMEM((groups // 2, 2, wide, 2 * LANES), BF16)],
        )
        sides, full_edges = call(
            edge_kernel,
            [strips_shape, rim],
            [VMEM] * 5,
            (from_left, from_right, u_edges, mat, band_rows),
            limit=4,
        )
        above, below = exchange(full_edges, "row")
        (w,) = call(
            second_filter_kernel, [field], [VMEM] * 3, (u, sides, band_rows), limit=4
        )
        return w, above, below, *unsorted

    w, above, below = smooth(z_first, strips)
    p, ps, z, strips, sums, flat_rows = call(
        image_one_kernel,
        [field, station_field, field, strips_shape, shape((GROUP, LANES), F32), shape((steps, slots), F32)],
        [SMEM] + [VMEM] * 11,
        (bounds, w, above, below, edge, grid_noise, b, sb, info, ut, gv, sv),
        [pltpu.VMEM((steps, GROUP, lanes), F32), extra],
    )
    w, above, below, unsorted = smooth(z, strips, flat_rows, rank)
    q, message = call(
        image_two_kernel,
        [field, shape((devices, LANES), F32)],
        [VMEM] * 13,
        (w, above, below, edge, grid_noise, b, p, z_first, z, sb, ps, info, sums),
        [extra],
        limit=4,
    )
    received = lax.all_to_all(message, ("row", "col"), 0, 0, tiled=True)
    solution_grid, residual_grid, solution_stations = pl.pallas_call(
        final_kernel,
        out_shape=[field, field, shape((steps, 1, 1, slots), F32)],
        in_specs=[VMEM] * 6,
        out_specs=[ANY, ANY, ANY],
        scratch_shapes=[
            pltpu.VMEM((steps, rows, cols), F32),
            pltpu.VMEM((steps, rows, cols), F32),
            pltpu.VMEM((steps, 1, 1, slots), F32),
            pltpu.SemaphoreType.DMA((2, steps // 2)),
            pltpu.SemaphoreType.DMA(()),
        ],
        compiler_params=pltpu.CompilerParams(vmem_limit_bytes=10 * 2**20),
    )(received, b, p, q, own, unsorted)
    return solution_grid, solution_stations, residual_grid


def solution(mesh):
    placed = (
        P(None, "row", "col"),
        P("row", "col"),
        P(None, "row", "col", None),
        P("row", "col", None),
        P(None, "row", "col", None),
        P("row", "col", None),
        P("row", "col"),
        P(),
    )
    return jax.shard_map(
        body,
        mesh=mesh,
        in_specs=placed,
        out_specs=(P(None, "row", "col"), P(None, "row", "col", None), P(None, "row", "col")),
        check_vma=False,
    )
```

```python
import functools

import jax
import jax.numpy as jnp
from jax import lax
from jax.experimental import pallas as pl
from jax.experimental.pallas import tpu as pltpu
from jax.sharding import PartitionSpec as P

REACH = 8
LANES = 128
HALF = LANES // 2
GROUP = 8
F32 = jnp.float32
BF16 = jnp.bfloat16
HIGHEST = lax.Precision.HIGHEST


def iota(shape, dim):
    return lax.broadcasted_iota(jnp.int32, shape, dim)


def taper(distance):
    spread = jnp.abs(distance).astype(F32)
    value = (1.0 - spread / (REACH + 1)) * jnp.exp(-spread / 3.0)
    return jnp.where(jnp.abs(distance) <= REACH, value, 0.0)


def split(x):
    high = x.astype(BF16)
    return high, (x - high.astype(F32)).astype(BF16)


def pair(x):
    high, low = split(x)
    return jnp.concatenate([high, low], axis=1)


def doubled(weights):
    high, low = split(weights)
    return jnp.concatenate(
        [
            jnp.concatenate([high, low], axis=1),
            jnp.concatenate([high, jnp.zeros_like(low)], axis=1),
        ],
        axis=0,
    )


def dot(a, b):
    return jnp.dot(a, b, preferred_element_type=F32)


def dot_nt(a, b):
    return lax.dot_general(a, b, (((1,), (1,)), ((), ())), preferred_element_type=F32)


def halves(x):
    width = x.shape[1] // 2
    return x[:, :width] + x[:, width:]


def three(x):
    high = x.astype(BF16)
    rest = x - high.astype(F32)
    middle = rest.astype(BF16)
    low = (rest - middle.astype(F32)).astype(BF16)
    return jnp.concatenate([high, middle, low], axis=0)


def cut(x, axis):
    return [
        lax.slice_in_dim(x, start, start + LANES, axis=axis)
        for start in range(0, x.shape[axis], LANES)
    ]


def slot_of(axis, side):
    odd = lax.rem(lax.axis_index(axis), 2)
    return odd if side else 1 - odd


def chunks(steps, size=GROUP):
    return [pl.ds(start, size) for start in range(0, steps, size)]


def shifted_block(source, block, blocks):
    here = source[:, pl.ds(block * LANES, LANES)]
    after = jnp.zeros_like(here)
    if block + 1 < blocks:
        after = source[:, pl.ds((block + 1) * LANES, LANES)]
    return pltpu.roll(jnp.where(iota(here.shape, 1) < HALF, after, here), HALF, 1)


def spread_rows(even, odd, target, steps, blocks):
    for tile in range(2 * blocks):
        source = odd if tile % 2 else even
        place = pl.ds(tile // 2 * LANES, LANES)
        for step in range(steps):
            target[step, :, pl.ds(tile * LANES, LANES)] = jnp.broadcast_to(
                source[pl.ds(step, 1), place], (GROUP, LANES)
            )


def rows_of(g):
    return pl.ds(pl.multiple_of(g * GROUP, GROUP), GROUP)


def prepare_kernel(
    count, cell_any, offset_any, noise_any, obs_any, base_any,
    base, z, strips, sb, ordered, info, rank_out, own, sv, gv, spots,
    band_rows, band_cols, edge, bounds,
    cell_v, offset_v, noise_v, obs_v, bounds_v, table, sorted_rows, shifted_rows, copies,
):
    base_copy = pltpu.make_async_copy(base_any, base, copies.at[0])
    base_copy.start()
    small = [
        pltpu.make_async_copy(source, target, copies.at[1 + place])
        for place, (source, target) in enumerate(
            ((cell_any, cell_v), (offset_any, offset_v), (noise_any, noise_v), (obs_any, obs_v))
        )
    ]
    for copy in small:
        copy.start()
    fixed_matrices(band_rows, band_cols, edge)
    for copy in small:
        copy.wait()
    cell, noise = cell_v[0], noise_v[0]
    steps, slots = own.shape
    tiles = slots // LANES
    rows = base.shape[1]
    groups = rows // GROUP
    slot = iota((1, slots), 1)
    live = slot < count[0, 0]
    where_row = cell // LANES
    where_col = cell - where_row * LANES
    key = jnp.where(live, where_row, rows) * slots + slot
    key = key.astype(F32)
    total = jnp.zeros((1, slots), F32)
    for block in range(tiles):
        piece = key[:, block * LANES : (block + 1) * LANES]
        column = jnp.transpose(jnp.broadcast_to(piece, (LANES, LANES)))
        column = jnp.concatenate([column] * tiles, axis=1)
        less = jnp.where(column < key, 1.0, 0.0)
        total = total + jnp.sum(less, axis=0, keepdims=True)
    rank = total.astype(jnp.int32)
    rank_out[...] = rank
    lived = jnp.where(live, 1.0, 0.0)
    for step in range(steps):
        own[pl.ds(step, 1), :] = obs_v[step, 0] * lived
    table[pl.ds(0, steps), :] = own[...]
    table[pl.ds(steps, 1), :] = where_row.astype(F32)
    table[pl.ds(steps + 1, 1), :] = where_col.astype(F32)
    table[pl.ds(steps + 2, 1), :] = offset_v[0, 0]
    table[pl.ds(steps + 3, 1), :] = offset_v[1, 0]
    table[pl.ds(steps + 4, 1), :] = noise
    table[pl.ds(steps + 5, 1), :] = lived
    table[pl.ds(steps + 6, 2), :] = jnp.zeros((2, slots), F32)
    pieces = three(table[...])
    height = table.shape[0]

    def sort_block(block, carry):
        start = pl.multiple_of(block * LANES, LANES)
        order = (iota((LANES, slots), 0) + start == rank).astype(F32).astype(BF16)
        out = dot_nt(pieces, order)
        sorted_rows[:, pl.ds(start, LANES)] = (
            out[:height] + out[height : 2 * height] + out[2 * height :]
        )
        return carry

    lax.fori_loop(0, tiles, sort_block, 0, unroll=2)
    ordered_row = sorted_rows[pl.ds(steps, 1), :]
    ordered_live = sorted_rows[pl.ds(steps + 5, 1), :]
    first_row = (iota((groups, slots), 0) * GROUP).astype(F32)
    before = jnp.where(ordered_row < first_row - 1.0, ordered_live, 0.0)
    until = jnp.where(ordered_row < first_row + GROUP, ordered_live, 0.0)
    low = jnp.sum(before, axis=1, keepdims=True)
    high = jnp.sum(until, axis=1, keepdims=True)
    start_tile = jnp.where(high > low, jnp.floor(low * (1.0 / HALF)), float(2 * tiles))
    reached = jnp.where(high > low, high - HALF * start_tile, 1.0)
    needed = jnp.floor((reached + (LANES - 1.0)) * (1.0 / LANES))
    most = jnp.max(needed, axis=0, keepdims=True)
    lane = iota((groups, LANES), 1)
    bounds_v[...] = jnp.where(
        lane == 0, start_tile, jnp.where(lane == 1, needed, most)
    ).astype(jnp.int32)
    bounds_copy = pltpu.make_async_copy(bounds_v, bounds, copies.at[5])
    bounds_copy.start()
    ordered[...] = sorted_rows[pl.ds(0, steps), :]
    alive = sorted_rows[pl.ds(steps + 5, 1), :]
    info[pl.ds(0, 1), :] = alive * sorted_rows[pl.ds(steps + 4, 1), :] + (1.0 - alive)
    info[pl.ds(1, 1), :] = alive
    for block in range(tiles):
        shifted_rows[:, pl.ds(block * LANES, LANES)] = shifted_block(sorted_rows, block, tiles)
    none = tile_lanes(2 * tiles, 1)
    sb[:, :, none] = jnp.zeros((steps, GROUP, LANES), F32)
    spots[:, :, none] = jnp.full((2, GROUP, LANES), -1000.0, F32)
    for target in (sv, gv):
        target[2 * tiles] = jnp.zeros((2 * LANES, 2 * LANES), BF16)
    spread_rows(sorted_rows, shifted_rows, sb, steps, tiles)
    for tile in range(2 * tiles):
        source = shifted_rows if tile % 2 else sorted_rows
        place = pl.ds(tile // 2 * LANES, LANES)
        lanes = pl.ds(tile * LANES, LANES)
        spots[0, :, lanes] = jnp.broadcast_to(source[pl.ds(steps, 1), place], (GROUP, LANES))
        spots[1, :, lanes] = jnp.broadcast_to(source[pl.ds(steps + 2, 1), place], (GROUP, LANES))
        at_col = source[pl.ds(steps + 1, 1), place].astype(jnp.int32)
        along_col = source[pl.ds(steps + 3, 1), place]
        col = iota((LANES, LANES), 0)
        across = jnp.where(
            col == at_col, 1.0 - along_col, jnp.where(col == at_col + 1, along_col, 0.0)
        )
        gv[tile] = doubled(across)
        if tile % 2 == 0:
            sv[tile] = doubled(jnp.transpose(across))
    for tile in range(1, 2 * tiles, 2):
        for start in (0, LANES):
            sv[tile, pl.ds(start, HALF), :] = sv[tile - 1, pl.ds(start + HALF, HALF), :]
            sv[tile, pl.ds(start + HALF, HALF), :] = sv[tile + 1, pl.ds(start, HALF), :]
    bounds_copy.wait()
    base_copy.wait()
    scatter_all(base, z, strips, sb, spots, sv, bounds)


def matrices_kernel(cov, mix, mat):
    steps = cov.shape[0]
    wide = steps * GROUP
    spread = (iota((wide, steps), 0) // GROUP == iota((wide, steps), 1)).astype(F32)
    spread_t = (iota((steps, wide), 1) // GROUP == iota((steps, wide), 0)).astype(F32)
    expanded = jnp.dot(
        jnp.dot(spread, cov[...], precision=HIGHEST, preferred_element_type=F32),
        spread_t,
        precision=HIGHEST,
        preferred_element_type=F32,
    )
    a = iota((wide, wide), 0)
    b = iota((wide, wide), 1)
    same = (a % GROUP) == (b % GROUP)
    high_part, low_part = split(jnp.where(same, expanded, 0.0))
    mix[...] = jnp.concatenate([high_part, high_part, low_part], axis=1)
    near = taper((b % GROUP) + REACH - (a % GROUP)) * expanded
    near = jnp.concatenate(
        [jnp.concatenate([x[GROUP:], x[:GROUP]], axis=0) for x in cut(near, 0)], axis=0
    )
    mat[0], mat[1] = split(near)
    far = taper(REACH + (a % GROUP) - (b % GROUP)) * expanded
    far = jnp.concatenate(
        [pltpu.roll(x, LANES - GROUP, 1) for x in cut(far, 1)], axis=1
    )
    mat[2], mat[3] = split(far)


def fixed_matrices(band_rows, band_cols, edge):
    rows = band_rows.shape[0]
    wide = edge.shape[1]
    a = iota((wide, wide), 0)
    b = iota((wide, wide), 1)
    ra = iota((rows, rows), 0)
    rb = iota((rows, rows), 1)
    high_part, low_part = split(0.25 * taper(ra - rb))
    band_rows[...] = jnp.concatenate([high_part, high_part, low_part], axis=1)
    ca = iota((LANES, LANES), 0)
    cb = iota((LANES, LANES), 1)
    band_cols[...] = doubled(taper(ca - cb))
    block_same = (a // GROUP) == (b // GROUP)
    above = 0.25 * taper((a % GROUP) + REACH - (b % GROUP))
    below = 0.25 * taper(REACH + (b % GROUP) - (a % GROUP))
    edge[0], edge[1] = split(jnp.where(block_same, above, 0.0))
    edge[2], edge[3] = split(jnp.where(block_same, below, 0.0))


def tile_lanes(index, count):
    return pl.ds(pl.multiple_of(index * LANES, LANES), count * LANES)


def row_weights(g, lanes, spots):
    row = (iota((GROUP, LANES), 0) + g * GROUP).astype(F32)
    offset = row - spots[0, :, lanes]
    along = spots[1, :, lanes]
    return jnp.where(offset == 0.0, 1.0 - along, jnp.where(offset == 1.0, along, 0.0))[None]


def spread_tile(g, index, sb, spots, sv):
    steps = sb.shape[0]
    lanes = tile_lanes(index, 1)
    weight = row_weights(g, lanes, spots)
    left = jnp.concatenate(
        [
            pair((sb[times, :, lanes] * weight).reshape(GROUP * GROUP, LANES))
            for times in chunks(steps)
        ],
        axis=0,
    )
    return halves(dot(left, sv[index])).reshape(steps, GROUP, LANES)


def scatter_all(base, z, strips, sb, spots, sv, bounds):
    groups = base.shape[1] // GROUP

    def run(g, carry):
        value = base[:, rows_of(g), :] + spread_tile(g, bounds[g, 0], sb, spots, sv)
        z[:, rows_of(g), :] = value
        pack_group(g, value, strips)
        return carry

    lax.fori_loop(0, groups, run, 0, unroll=2)

    @pl.when(bounds[0, 2] > 1)
    def _():
        def crowded(g, carry):
            def more(index, inner):
                z[:, rows_of(g), :] += spread_tile(g, bounds[g, 0] + 2 * index, sb, spots, sv)
                return inner

            lax.fori_loop(1, bounds[g, 1], more, 0)
            pack_group(g, z[:, rows_of(g), :], strips)
            return carry

        lax.fori_loop(0, groups, crowded, 0)


def pack_group(g, value, strips):
    steps = value.shape[0]
    per = LANES // GROUP
    slot = iota((GROUP, LANES), 1) // GROUP
    for half in range(steps // per):
        left = jnp.zeros((GROUP, LANES), F32)
        right = jnp.zeros((GROUP, LANES), F32)
        for local in range(per):
            moved = value[half * per + local]
            if local:
                moved = pltpu.roll(moved, local * GROUP, 1)
            left = jnp.where(slot == local, moved, left)
            right = jnp.where(slot == (local - 1) % per, moved, right)
        lanes = pl.ds(half * LANES, LANES)
        strips[slot_of("col", 0), rows_of(g), lanes] = left
        strips[slot_of("col", 1), rows_of(g), lanes] = right


def unpack(sides, where_rows, count, step):
    per = LANES // GROUP
    half, local = step // per, step % per
    lane = iota((count, LANES), 1)
    lanes = pl.ds(half * LANES, LANES) if isinstance(step, int) else tile_lanes(half, 1)
    both = jnp.where(lane // GROUP == local, sides[0, where_rows, lanes], sides[1, where_rows, lanes])
    both = pltpu.roll(both, (LANES - local * GROUP) % LANES, 1)
    return jnp.where((lane < GROUP) | (lane >= LANES - GROUP), both, 0.0)


def first_filter_kernel(z, mix, band_cols, u, u_edges, y):
    steps, rows, cols = z.shape
    groups = rows // GROUP
    flat = (steps * GROUP, LANES)

    def across(quad, carry):
        parts = [z[:, rows_of(4 * quad + i), :].reshape(flat) for i in range(4)]
        value = halves(dot(pair(jnp.concatenate(parts, axis=0)), band_cols[...]))
        both = split(value)
        for i in range(4):
            for part in range(2):
                y[2 * quad + i // 2, part, :, pl.ds((i % 2) * LANES, LANES)] = both[part][
                    i * flat[0] : (i + 1) * flat[0]
                ]
        return carry

    lax.fori_loop(0, groups // 4, across, 0)

    def mixing(two, carry):
        right = jnp.concatenate([y[two, 0], y[two, 1], y[two, 0]], axis=0)
        out = dot(mix[...], right)
        u[:, rows_of(2 * two), :] = out[:, :LANES].reshape(steps, GROUP, LANES)
        u[:, rows_of(2 * two + 1), :] = out[:, LANES:].reshape(steps, GROUP, LANES)
        return carry

    lax.fori_loop(0, groups // 2, mixing, 0, unroll=2)
    u_edges[0] = u[:, pl.ds(0, GROUP), :]
    u_edges[1] = u[:, pl.ds(rows - GROUP, GROUP), :]


def filter_unsort_kernel(z, mix, band_cols, flat_rows, rank, u, u_edges, unsorted, y):
    first_filter_kernel(z, mix, band_cols, u, u_edges, y)
    steps, slots = flat_rows.shape
    tiles = slots // LANES
    pieces = three(flat_rows[...])

    def unsort_block(block, carry):
        lanes = tile_lanes(block, 1)
        order = (iota((slots, LANES), 0) == rank[:, lanes]).astype(F32).astype(BF16)
        out = dot(pieces, order)
        unsorted[:, lanes] = out[:steps] + out[steps : 2 * steps] + out[2 * steps :]
        return carry

    lax.fori_loop(0, tiles, unsort_block, 0)


def second_filter_kernel(u, sides, band_rows, w):
    steps, rows, cols = u.shape

    def along(two, carry):
        one = split(u[2 * two])
        other = split(u[2 * two + 1])
        high = jnp.concatenate([one[0], other[0]], axis=1)
        low = jnp.concatenate([one[1], other[1]], axis=1)
        out = dot(band_rows[...], jnp.concatenate([high, low, high], axis=0))
        everything = pl.ds(0, rows)
        w[2 * two] = out[:, :LANES] + unpack(sides, everything, rows, 2 * two)
        w[2 * two + 1] = out[:, LANES:] + unpack(sides, everything, rows, 2 * two + 1)
        return carry

    lax.fori_loop(0, steps // 2, along, 0, unroll=2)


def edge_kernel(first, second, u_edges, mat, band_rows, sides, full_edges):
    steps = u_edges.shape[1]
    rows = first.shape[0]
    for place, source in ((0, first), (1, second)):
        side = slot_of("col", place)
        high, low = split(source[...])
        value = dot(high, mat[2 * side]) + dot(low, mat[2 * side])
        value = value + dot(high, mat[2 * side + 1])
        sides[side] = value
    for which, start in ((0, 0), (1, rows - GROUP)):
        slot = slot_of("row", which)
        for step in range(steps):
            full_edges[slot, step] = u_edges[which, step] + unpack(
                sides, pl.ds(start, GROUP), GROUP, step
            )
    for side in range(2):
        high, low = split(sides[side])
        sides[side] = dot(band_rows[...], jnp.concatenate([high, low, high], axis=0))


def fill_extra(extra, first, second, edge):
    steps = first.shape[0]
    flat = (steps * GROUP, LANES)
    for place, source in ((0, first), (1, second)):
        which = slot_of("row", place)
        both = pair(source[...].reshape(flat))
        value = halves(dot(edge[2 * which], both)) + dot(edge[2 * which + 1], both[:, :LANES])
        extra[which] = value.reshape(steps, GROUP, LANES)
    extra[2] = jnp.zeros((steps, GROUP, LANES), F32)


def which_extra(g, groups):
    return jnp.where(g == 0, 0, jnp.where(g == groups - 1, 1, 2))


def gather_tile(g, both, index, acc, spots, gv):
    steps = acc.shape[0]
    lanes = tile_lanes(index, 1)
    out = halves(dot(both, gv[index])).reshape(steps, GROUP, LANES)
    weight = row_weights(g, lanes, spots)
    for times in chunks(steps):
        acc[times, :, lanes] += out[times.start : times.start + times.size] * weight


def whole(x):
    return jnp.sum(jnp.sum(x, axis=1, keepdims=True), axis=0, keepdims=True)


def fold(x):
    return jnp.sum(x, axis=0)


def fold_flat(x):
    return fold(x.reshape(x.shape[0] // GROUP, GROUP, LANES))


def image_one_kernel(
    bounds, w, above, below, edge, noise, b, ordered, info, spots, gv, sv,
    p, z, strips, sums, flat_rows, acc, extra, ps, compact, shifted,
):
    steps, rows, _ = w.shape
    groups = rows // GROUP
    tiles = info.shape[1] // LANES
    fill_extra(extra, above, below, edge)
    acc[...] = jnp.zeros_like(acc)

    def run(g, carry):
        here = rows_of(g)
        which = which_extra(g, groups)
        spread = noise[here, :][None]
        first, second, third = carry
        left = []
        for times in chunks(steps):
            value = w[times, here, :] + extra[which, times]
            left.append(pair(value.reshape(GROUP * GROUP, LANES)))
            mine = b[times, here, :]
            image = value + spread * mine
            p[times, here, :] = image
            first = first + fold(mine * mine)
            second = second + fold(mine * image)
            third = third + fold(image * image)
        gather_tile(g, jnp.concatenate(left, axis=0), bounds[g, 0], acc, spots, gv)
        return first, second, third

    zero = jnp.zeros((GROUP, LANES), F32)
    carry = lax.fori_loop(0, groups, run, (zero,) * 3, unroll=2)

    @pl.when(bounds[0, 2] > 1)
    def _():
        def crowded(g, inner):
            value = w[:, rows_of(g), :] + extra[which_extra(g, groups)]
            both = pair(value.reshape(steps * GROUP, LANES))

            def more(index, innermost):
                gather_tile(g, both, bounds[g, 0] + 2 * index, acc, spots, gv)
                return innermost

            return lax.fori_loop(1, bounds[g, 1], more, inner)

        lax.fori_loop(0, groups, crowded, 0)

    wide = steps * GROUP
    adds = (iota((steps, 2 * wide), 1) % wide // GROUP == iota((steps, 2 * wide), 0)).astype(F32)
    adds = adds.astype(BF16)

    def fold_rows(index, inner):
        lanes = tile_lanes(2 * index, 2)
        high, low = split(acc[:, :, lanes].reshape(wide, 2 * LANES))
        compact[:, lanes] = dot(adds, jnp.concatenate([high, low], axis=0))
        return inner

    lax.fori_loop(0, tiles, fold_rows, 0)
    lane = iota((steps, LANES), 1)
    first, second, third = carry
    for block in range(tiles):
        place = pl.ds(block * LANES, LANES)
        before = jnp.zeros((steps, LANES), F32)
        if block:
            before = compact[:, pl.ds((2 * block - 1) * LANES, LANES)]
        after = compact[:, pl.ds((2 * block + 1) * LANES, LANES)]
        sampled = compact[:, pl.ds(2 * block * LANES, LANES)] + pltpu.roll(
            jnp.where(lane < HALF, after, before), HALF, 1
        )
        mine = ordered[:, place]
        image = info[pl.ds(1, 1), place] * sampled + info[pl.ds(0, 1), place] * mine
        flat_rows[:, place] = image
        first = first + fold_flat(mine * mine)
        second = second + fold_flat(mine * image)
        third = third + fold_flat(image * image)
    carry = first, second, third
    for block in range(tiles):
        shifted[:, pl.ds(block * LANES, LANES)] = shifted_block(flat_rows, block, tiles)
    ps[:, :, tile_lanes(2 * tiles, 1)] = jnp.zeros((steps, GROUP, LANES), F32)
    spread_rows(flat_rows, shifted, ps, steps, tiles)
    bb, bp, pp = (whole(x) for x in carry)
    lane = iota((GROUP, LANES), 1)
    value = jnp.where(lane == 0, bb / bp, 0.0)
    value = jnp.where(lane == 1, bb, value)
    value = jnp.where(lane == 2, bp, value)
    value = jnp.where(lane == 3, pp, value)
    sums[...] = value
    scatter_all(p, z, strips, ps, spots, sv, bounds)


def image_two_kernel(
    w, above, below, edge, noise, b, p, z_first, z, ordered, flat_rows, info, sums,
    q, message, extra,
):
    steps, rows, _ = w.shape
    groups = rows // GROUP
    tiles = info.shape[1] // LANES
    fill_extra(extra, above, below, edge)
    shift = jnp.broadcast_to(sums[0:1, 0:1], (GROUP, LANES))[None]

    def run(g, carry):
        here = rows_of(g)
        which = which_extra(g, groups)
        spread = noise[here, :][None]
        first, second, third = carry
        for times in chunks(steps, 4):
            value = w[times, here, :] + extra[which, times]
            mine = p[times, here, :]
            scaled = spread * mine
            q[times, here, :] = value + scaled
            residual = b[times, here, :] - shift * mine
            image = z[times, here, :]
            moved = z_first[times, here, :] - shift * image
            first = first + fold(residual * residual)
            second = second + fold(moved * value + residual * scaled)
            third = third + fold(image * value + mine * scaled)
        return first, second, third

    zero = jnp.zeros((GROUP, LANES), F32)
    carry = lax.fori_loop(0, groups, run, (zero,) * 3)

    first, second, third = carry
    own_shift = sums[0:1, 0:1]
    for block in range(tiles):
        place = pl.ds(block * LANES, LANES)
        mine = flat_rows[:, place]
        scaled = info[pl.ds(0, 1), place] * mine
        residual = ordered[:, place] - own_shift * mine
        first = first + fold_flat(residual * residual)
        second = second + fold_flat(residual * scaled)
        third = third + fold_flat(mine * scaled)
    carry = first, second, third
    lane = iota((1, LANES), 1)
    value = jnp.where(lane < 4, sums[0:1, :], 0.0)
    for place, x in enumerate(carry):
        value = jnp.where(lane == 4 + place, whole(x), value)
    message[...] = jnp.broadcast_to(value, message.shape)


def final_kernel(
    received, b, p, q, own, unsorted, solution_out, residual_out, station_out,
    solution_v, residual_v, station_v, sems, station_sem,
):
    everything = received[...]

    def column(index):
        return everything[:, index : index + 1]

    def total(x):
        return jnp.sum(x, axis=0, keepdims=True)

    shift, bb, bp, pp = (column(i) for i in range(4))
    rr, rq, pq = (column(i) for i in range(4, 7))
    norm = total(bb)
    alpha = norm / total(bp)
    delta = shift - alpha
    rp = bp - shift * pp
    ru = rp - shift * rq
    pu = pp - shift * pq
    norm_next = total(rr + 2.0 * delta * rp + delta * delta * pp)
    energy = total(ru + delta * (rq + pu) + delta * delta * pq)
    beta = norm_next / norm
    alpha_next = norm_next / (energy - beta * norm_next / alpha)
    along = alpha + alpha_next * (1.0 + beta)
    twice = alpha_next * alpha
    steps, rows, _ = b.shape
    chunk = 64
    tall = (chunk // GROUP, GROUP, LANES)
    wide_along = jnp.broadcast_to(along, (GROUP, LANES))[None]
    wide_twice = jnp.broadcast_to(twice, (GROUP, LANES))[None]

    def copies(place):
        here = pl.ds(place * 2, 2)
        return (
            pltpu.make_async_copy(solution_v.at[here], solution_out.at[here], sems.at[0, place]),
            pltpu.make_async_copy(residual_v.at[here], residual_out.at[here], sems.at[1, place]),
        )

    def run(place, carry):
        for inner in range(2):
            step = place * 2 + inner
            for piece in range(rows // chunk):
                here = pl.ds(piece * chunk, chunk)
                first = b[step, here, :].reshape(tall)
                second = p[step, here, :].reshape(tall)
                third = q[step, here, :].reshape(tall)
                solution_v[step, here, :] = (wide_along * first - wide_twice * second).reshape(
                    chunk, LANES
                )
                residual_v[step, here, :] = (
                    first - wide_along * second + wide_twice * third
                ).reshape(chunk, LANES)
        for copy in copies(place):
            copy.start()
        return carry

    lax.fori_loop(0, steps // 2, run, 0)
    stations = along * own[...] - twice * unsorted[...]
    for step in range(steps):
        station_v[step, 0] = stations[step : step + 1]
    station_copy = pltpu.make_async_copy(station_v, station_out, station_sem)
    station_copy.start()

    def finish(place, carry):
        for copy in copies(place):
            copy.wait()
        return carry

    lax.fori_loop(0, steps // 2, finish, 0)
    station_copy.wait()


VMEM = pl.BlockSpec(memory_space=pltpu.VMEM)
SMEM = pl.BlockSpec(memory_space=pltpu.SMEM)
ANY = pl.BlockSpec(memory_space=pltpu.HBM)


def call(kernel, outs, ins, operands, scratch=(), flops=10**9, moved=10**7, limit=8, **extra):
    return pl.pallas_call(
        kernel,
        out_shape=outs,
        in_specs=ins,
        out_specs=[VMEM] * len(outs),
        scratch_shapes=list(scratch),
        compiler_params=pltpu.CompilerParams(vmem_limit_bytes=limit * 2**20),
        cost_estimate=pl.CostEstimate(flops=flops, bytes_accessed=moved, transcendentals=0),
        **extra,
    )(*operands)


def exchange(both, axis):
    count = lax.axis_size(axis)
    pairs = [[(i, i + 1) for i in range(start, count - 1, 2)] for start in (0, 1)]
    return tuple(
        lax.ppermute(both[place], axis, found + [(b, a) for a, b in found])
        for place, found in enumerate(pairs)
    )


def body(
    grid_obs, grid_noise, station_obs, station_noise, station_offset, station_cell,
    station_count, time_cov,
):
    steps, rows, cols = grid_obs.shape
    slots = station_obs.shape[3]
    wide = steps * GROUP
    groups = rows // GROUP
    tiles = 2 * (slots // LANES) + 1
    lanes = tiles * LANES
    devices = lax.axis_size("row") * lax.axis_size("col")
    shape = jax.ShapeDtypeStruct
    field = shape((steps, rows, cols), F32)
    rim = shape((2, steps, GROUP, cols), F32)
    strips_shape = shape((2, rows, wide), F32)
    station_field = shape((steps, GROUP, lanes), F32)
    extra = pltpu.VMEM((3, steps, GROUP, LANES), F32)
    (
        b, z_first, strips, sb, ordered, info, rank, own, sv, gv, spots,
        band_rows, band_cols, edge, bounds,
    ) = pl.pallas_call(
        prepare_kernel,
        out_shape=[
            field,
            field,
            strips_shape,
            station_field,
            shape((steps, slots), F32),
            shape((2, slots), F32),
            shape((1, slots), jnp.int32),
            shape((steps, slots), F32),
            shape((tiles, 2 * LANES, 2 * LANES), BF16),
            shape((tiles, 2 * LANES, 2 * LANES), BF16),
            shape((2, GROUP, lanes), F32),
            shape((rows, 3 * rows), BF16),
            shape((2 * LANES, 2 * LANES), BF16),
            shape((4, wide, wide), BF16),
            shape((groups, LANES), jnp.int32),
        ],
        in_specs=[SMEM] + [ANY] * 5,
        out_specs=[VMEM] * 14 + [SMEM],
        scratch_shapes=[
            pltpu.VMEM((1, 1, slots), jnp.int32),
            pltpu.VMEM((2, 1, 1, slots), F32),
            pltpu.VMEM((1, 1, slots), F32),
            pltpu.VMEM((steps, 1, 1, slots), F32),
            pltpu.VMEM((groups, LANES), jnp.int32),
            pltpu.VMEM((steps + 8, slots), F32),
            pltpu.VMEM((steps + 8, slots), F32),
            pltpu.VMEM((steps + 8, slots), F32),
            pltpu.SemaphoreType.DMA((6,)),
        ],
        compiler_params=pltpu.CompilerParams(vmem_limit_bytes=8 * 2**20),
        cost_estimate=pl.CostEstimate(flops=10**9, bytes_accessed=10**7, transcendentals=0),
    )(
        station_count,
        *(
            pltpu.with_memory_space_constraint(x, pltpu.HBM)
            for x in (station_cell, station_offset, station_noise, station_obs, grid_obs)
        ),
    )
    mix, mat = call(
        matrices_kernel,
        [shape((wide, 3 * wide), BF16), shape((4, wide, wide), BF16)],
        [VMEM],
        (time_cov,),
    )

    def smooth(z, strips, *more):
        from_left, from_right = exchange(strips, "col")
        u, u_edges, *unsorted = call(
            filter_unsort_kernel if more else first_filter_kernel,
            [field, rim] + [shape((steps, slots), F32)] * bool(more),
            [VMEM] * (3 + len(more)),
            (z, mix, band_cols, *more),
            [pltpu.VMEM((groups // 2, 2, wide, 2 * LANES), BF16)],
        )
        sides, full_edges = call(
            edge_kernel,
            [strips_shape, rim],
            [VMEM] * 5,
            (from_left, from_right, u_edges, mat, band_rows),
            limit=4,
        )
        above, below = exchange(full_edges, "row")
        (w,) = call(
            second_filter_kernel, [field], [VMEM] * 3, (u, sides, band_rows), limit=4
        )
        return w, above, below, *unsorted

    w, above, below = smooth(z_first, strips)
    p, z, strips, sums, flat_rows = call(
        image_one_kernel,
        [field, field, strips_shape, shape((GROUP, LANES), F32), shape((steps, slots), F32)],
        [SMEM] + [VMEM] * 11,
        (bounds, w, above, below, edge, grid_noise, b, ordered, info, spots, gv, sv),
        [
            pltpu.VMEM((steps, GROUP, lanes), F32),
            extra,
            pltpu.VMEM((steps, GROUP, lanes), F32),
            pltpu.VMEM((steps, lanes), F32),
            pltpu.VMEM((steps, slots), F32),
        ],
        limit=12,
    )
    w, above, below, unsorted = smooth(z, strips, flat_rows, rank)
    q, message = call(
        image_two_kernel,
        [field, shape((devices, LANES), F32)],
        [VMEM] * 13,
        (w, above, below, edge, grid_noise, b, p, z_first, z, ordered, flat_rows, info, sums),
        [extra],
        limit=4,
    )
    received = lax.all_to_all(message, ("row", "col"), 0, 0, tiled=True)
    solution_grid, residual_grid, solution_stations = pl.pallas_call(
        final_kernel,
        out_shape=[field, field, shape((steps, 1, 1, slots), F32)],
        in_specs=[VMEM] * 6,
        out_specs=[ANY, ANY, ANY],
        scratch_shapes=[
            pltpu.VMEM((steps, rows, cols), F32),
            pltpu.VMEM((steps, rows, cols), F32),
            pltpu.VMEM((steps, 1, 1, slots), F32),
            pltpu.SemaphoreType.DMA((2, steps // 2)),
            pltpu.SemaphoreType.DMA(()),
        ],
        compiler_params=pltpu.CompilerParams(vmem_limit_bytes=10 * 2**20),
    )(received, b, p, q, own, unsorted)
    return solution_grid, solution_stations, residual_grid


def solution(mesh):
    placed = (
        P(None, "row", "col"),
        P("row", "col"),
        P(None, "row", "col", None),
        P("row", "col", None),
        P(None, "row", "col", None),
        P("row", "col", None),
        P("row", "col"),
        P(),
    )
    return jax.shard_map(
        body,
        mesh=mesh,
        in_specs=placed,
        out_specs=(P(None, "row", "col"), P(None, "row", "col", None), P(None, "row", "col")),
        check_vma=False,
    )
```

```python
import functools

import jax
import jax.numpy as jnp
from jax import lax
from jax.experimental import pallas as pl
from jax.experimental.pallas import tpu as pltpu
from jax.sharding import PartitionSpec as P

REACH = 8
LANES = 128
HALF = LANES // 2
GROUP = 8
F32 = jnp.float32
BF16 = jnp.bfloat16
HIGHEST = lax.Precision.HIGHEST


def iota(shape, dim):
    return lax.broadcasted_iota(jnp.int32, shape, dim)


def taper(distance):
    spread = jnp.abs(distance).astype(F32)
    value = (1.0 - spread / (REACH + 1)) * jnp.exp(-spread / 3.0)
    return jnp.where(jnp.abs(distance) <= REACH, value, 0.0)


def split(x):
    high = x.astype(BF16)
    return high, (x - high.astype(F32)).astype(BF16)


def pair(x):
    high, low = split(x)
    return jnp.concatenate([high, low], axis=1)


def doubled(weights):
    high, low = split(weights)
    return jnp.concatenate(
        [
            jnp.concatenate([high, low], axis=1),
            jnp.concatenate([high, jnp.zeros_like(low)], axis=1),
        ],
        axis=0,
    )


def dot(a, b):
    return jnp.dot(a, b, preferred_element_type=F32)


def dot_nt(a, b):
    return lax.dot_general(a, b, (((1,), (1,)), ((), ())), preferred_element_type=F32)


def halves(x):
    width = x.shape[1] // 2
    return x[:, :width] + x[:, width:]


def three(x):
    high = x.astype(BF16)
    rest = x - high.astype(F32)
    middle = rest.astype(BF16)
    low = (rest - middle.astype(F32)).astype(BF16)
    return jnp.concatenate([high, middle, low], axis=0)


def cut(x, axis):
    return [
        lax.slice_in_dim(x, start, start + LANES, axis=axis)
        for start in range(0, x.shape[axis], LANES)
    ]


def slot_of(axis, side):
    odd = lax.rem(lax.axis_index(axis), 2)
    return odd if side else 1 - odd


def chunks(steps, size=GROUP):
    return [pl.ds(start, size) for start in range(0, steps, size)]


def shifted_block(source, block, blocks):
    here = source[:, pl.ds(block * LANES, LANES)]
    after = jnp.zeros_like(here)
    if block + 1 < blocks:
        after = source[:, pl.ds((block + 1) * LANES, LANES)]
    return pltpu.roll(jnp.where(iota(here.shape, 1) < HALF, after, here), HALF, 1)


def spread_rows(even, odd, target, steps, blocks):
    for tile in range(2 * blocks):
        source = odd if tile % 2 else even
        place = pl.ds(tile // 2 * LANES, LANES)
        for step in range(steps):
            target[step, :, pl.ds(tile * LANES, LANES)] = jnp.broadcast_to(
                source[pl.ds(step, 1), place], (GROUP, LANES)
            )


def rows_of(g):
    return pl.ds(pl.multiple_of(g * GROUP, GROUP), GROUP)


def prepare_kernel(
    count, cell_any, offset_any, noise_any, obs_any, base_any,
    base, z, strips, sb, ordered, info, rank_out, own, sv, gv, spots,
    band_rows, band_cols, edge, bounds,
    cell_v, offset_v, noise_v, obs_v, bounds_v, table, sorted_rows, shifted_rows, copies,
):
    small = [
        pltpu.make_async_copy(source, target, copies.at[1 + place])
        for place, (source, target) in enumerate(
            ((cell_any, cell_v), (offset_any, offset_v), (noise_any, noise_v), (obs_any, obs_v))
        )
    ]
    for copy in small:
        copy.start()
    base_copy = pltpu.make_async_copy(base_any, base, copies.at[0])
    base_copy.start()
    fixed_matrices(band_rows, band_cols, edge)
    for copy in small:
        copy.wait()
    cell, noise = cell_v[0], noise_v[0]
    steps, slots = own.shape
    tiles = slots // LANES
    rows = base.shape[1]
    groups = rows // GROUP
    slot = iota((1, slots), 1)
    live = slot < count[0, 0]
    where_row = cell // LANES
    where_col = cell - where_row * LANES
    key = jnp.where(live, where_row, rows) * slots + slot
    key = key.astype(F32)
    total = jnp.zeros((1, slots), F32)
    for block in range(tiles):
        piece = key[:, block * LANES : (block + 1) * LANES]
        column = jnp.transpose(jnp.broadcast_to(piece, (LANES, LANES)))
        column = jnp.concatenate([column] * tiles, axis=1)
        less = jnp.where(column < key, 1.0, 0.0)
        total = total + jnp.sum(less, axis=0, keepdims=True)
    rank = total.astype(jnp.int32)
    rank_out[...] = rank
    lived = jnp.where(live, 1.0, 0.0)
    for step in range(steps):
        own[pl.ds(step, 1), :] = obs_v[step, 0] * lived
    table[pl.ds(0, steps), :] = own[...]
    table[pl.ds(steps, 1), :] = where_row.astype(F32)
    table[pl.ds(steps + 1, 1), :] = where_col.astype(F32)
    table[pl.ds(steps + 2, 1), :] = offset_v[0, 0]
    table[pl.ds(steps + 3, 1), :] = offset_v[1, 0]
    table[pl.ds(steps + 4, 1), :] = noise
    table[pl.ds(steps + 5, 1), :] = lived
    table[pl.ds(steps + 6, 2), :] = jnp.zeros((2, slots), F32)
    pieces = three(table[...])
    height = table.shape[0]

    def sort_block(block, carry):
        start = pl.multiple_of(block * LANES, LANES)
        order = (iota((LANES, slots), 0) + start == rank).astype(F32).astype(BF16)
        out = dot_nt(pieces, order)
        sorted_rows[:, pl.ds(start, LANES)] = (
            out[:height] + out[height : 2 * height] + out[2 * height :]
        )
        return carry

    lax.fori_loop(0, tiles, sort_block, 0, unroll=2)
    ordered_row = sorted_rows[pl.ds(steps, 1), :]
    ordered_live = sorted_rows[pl.ds(steps + 5, 1), :]
    first_row = (iota((groups, slots), 0) * GROUP).astype(F32)
    before = jnp.where(ordered_row < first_row - 1.0, ordered_live, 0.0)
    until = jnp.where(ordered_row < first_row + GROUP, ordered_live, 0.0)
    low = jnp.sum(before, axis=1, keepdims=True)
    high = jnp.sum(until, axis=1, keepdims=True)
    start_tile = jnp.where(high > low, jnp.floor(low * (1.0 / HALF)), float(2 * tiles))
    reached = jnp.where(high > low, high - HALF * start_tile, 1.0)
    needed = jnp.floor((reached + (LANES - 1.0)) * (1.0 / LANES))
    most = jnp.max(needed, axis=0, keepdims=True)
    lane = iota((groups, LANES), 1)
    bounds_v[...] = jnp.where(
        lane == 0, start_tile, jnp.where(lane == 1, needed, most)
    ).astype(jnp.int32)
    bounds_copy = pltpu.make_async_copy(bounds_v, bounds, copies.at[5])
    bounds_copy.start()
    ordered[...] = sorted_rows[pl.ds(0, steps), :]
    alive = sorted_rows[pl.ds(steps + 5, 1), :]
    info[pl.ds(0, 1), :] = alive * sorted_rows[pl.ds(steps + 4, 1), :] + (1.0 - alive)
    info[pl.ds(1, 1), :] = alive
    for block in range(tiles):
        shifted_rows[:, pl.ds(block * LANES, LANES)] = shifted_block(sorted_rows, block, tiles)
    none = tile_lanes(2 * tiles, 1)
    sb[:, :, none] = jnp.zeros((steps, GROUP, LANES), F32)
    spots[:, :, none] = jnp.full((2, GROUP, LANES), -1000.0, F32)
    for target in (sv, gv):
        target[2 * tiles] = jnp.zeros((2 * LANES, 2 * LANES), BF16)
    spread_rows(sorted_rows, shifted_rows, sb, steps, tiles)
    for tile in range(2 * tiles):
        source = shifted_rows if tile % 2 else sorted_rows
        place = pl.ds(tile // 2 * LANES, LANES)
        lanes = pl.ds(tile * LANES, LANES)
        spots[0, :, lanes] = jnp.broadcast_to(source[pl.ds(steps, 1), place], (GROUP, LANES))
        spots[1, :, lanes] = jnp.broadcast_to(source[pl.ds(steps + 2, 1), place], (GROUP, LANES))
        at_col = source[pl.ds(steps + 1, 1), place].astype(jnp.int32)
        along_col = source[pl.ds(steps + 3, 1), place]
        col = iota((LANES, LANES), 0)
        across = jnp.where(
            col == at_col, 1.0 - along_col, jnp.where(col == at_col + 1, along_col, 0.0)
        )
        gv[tile] = doubled(across)
        if tile % 2 == 0:
            sv[tile] = doubled(jnp.transpose(across))
    for tile in range(1, 2 * tiles, 2):
        for start in (0, LANES):
            sv[tile, pl.ds(start, HALF), :] = sv[tile - 1, pl.ds(start + HALF, HALF), :]
            sv[tile, pl.ds(start + HALF, HALF), :] = sv[tile + 1, pl.ds(start, HALF), :]
    bounds_copy.wait()
    base_copy.wait()
    scatter_all(base, z, strips, sb, spots, sv, bounds)


def matrices_kernel(cov, mix, mat):
    steps = cov.shape[0]
    wide = steps * GROUP
    spread = (iota((wide, steps), 0) // GROUP == iota((wide, steps), 1)).astype(F32)
    spread_t = (iota((steps, wide), 1) // GROUP == iota((steps, wide), 0)).astype(F32)
    expanded = jnp.dot(
        jnp.dot(spread, cov[...], precision=HIGHEST, preferred_element_type=F32),
        spread_t,
        precision=HIGHEST,
        preferred_element_type=F32,
    )
    a = iota((wide, wide), 0)
    b = iota((wide, wide), 1)
    same = (a % GROUP) == (b % GROUP)
    high_part, low_part = split(jnp.where(same, expanded, 0.0))
    mix[...] = jnp.concatenate([high_part, high_part, low_part], axis=1)
    near = taper((b % GROUP) + REACH - (a % GROUP)) * expanded
    near = jnp.concatenate(
        [jnp.concatenate([x[GROUP:], x[:GROUP]], axis=0) for x in cut(near, 0)], axis=0
    )
    mat[0], mat[1] = split(near)
    far = taper(REACH + (a % GROUP) - (b % GROUP)) * expanded
    far = jnp.concatenate(
        [pltpu.roll(x, LANES - GROUP, 1) for x in cut(far, 1)], axis=1
    )
    mat[2], mat[3] = split(far)


def fixed_matrices(band_rows, band_cols, edge):
    rows = band_rows.shape[0]
    wide = edge.shape[1]
    a = iota((wide, wide), 0)
    b = iota((wide, wide), 1)
    ra = iota((rows, rows), 0)
    rb = iota((rows, rows), 1)
    high_part, low_part = split(0.25 * taper(ra - rb))
    band_rows[...] = jnp.concatenate([high_part, high_part, low_part], axis=1)
    ca = iota((LANES, LANES), 0)
    cb = iota((LANES, LANES), 1)
    band_cols[...] = doubled(taper(ca - cb))
    block_same = (a // GROUP) == (b // GROUP)
    above = 0.25 * taper((a % GROUP) + REACH - (b % GROUP))
    below = 0.25 * taper(REACH + (b % GROUP) - (a % GROUP))
    edge[0], edge[1] = split(jnp.where(block_same, above, 0.0))
    edge[2], edge[3] = split(jnp.where(block_same, below, 0.0))


def tile_lanes(index, count):
    return pl.ds(pl.multiple_of(index * LANES, LANES), count * LANES)


def row_weights(g, lanes, spots):
    row = (iota((GROUP, LANES), 0) + g * GROUP).astype(F32)
    offset = row - spots[0, :, lanes]
    along = spots[1, :, lanes]
    return jnp.where(offset == 0.0, 1.0 - along, jnp.where(offset == 1.0, along, 0.0))[None]


def spread_tile(g, index, sb, spots, sv):
    steps = sb.shape[0]
    lanes = tile_lanes(index, 1)
    weight = row_weights(g, lanes, spots)
    left = jnp.concatenate(
        [
            pair((sb[times, :, lanes] * weight).reshape(GROUP * GROUP, LANES))
            for times in chunks(steps)
        ],
        axis=0,
    )
    return halves(dot(left, sv[index])).reshape(steps, GROUP, LANES)


def scatter_all(base, z, strips, sb, spots, sv, bounds):
    groups = base.shape[1] // GROUP

    def run(g, carry):
        value = base[:, rows_of(g), :] + spread_tile(g, bounds[g, 0], sb, spots, sv)
        z[:, rows_of(g), :] = value
        pack_group(g, value, strips)
        return carry

    lax.fori_loop(0, groups, run, 0, unroll=8)

    @pl.when(bounds[0, 2] > 1)
    def _():
        def crowded(g, carry):
            def more(index, inner):
                z[:, rows_of(g), :] += spread_tile(g, bounds[g, 0] + 2 * index, sb, spots, sv)
                return inner

            lax.fori_loop(1, bounds[g, 1], more, 0)
            pack_group(g, z[:, rows_of(g), :], strips)
            return carry

        lax.fori_loop(0, groups, crowded, 0)


def pack_group(g, value, strips):
    steps = value.shape[0]
    per = LANES // GROUP
    slot = iota((GROUP, LANES), 1) // GROUP
    for half in range(steps // per):
        left = jnp.zeros((GROUP, LANES), F32)
        right = jnp.zeros((GROUP, LANES), F32)
        for local in range(per):
            moved = value[half * per + local]
            if local:
                moved = pltpu.roll(moved, local * GROUP, 1)
            left = jnp.where(slot == local, moved, left)
            right = jnp.where(slot == (local - 1) % per, moved, right)
        lanes = pl.ds(half * LANES, LANES)
        strips[slot_of("col", 0), rows_of(g), lanes] = left
        strips[slot_of("col", 1), rows_of(g), lanes] = right


def unpack(sides, where_rows, count, step):
    per = LANES // GROUP
    half, local = step // per, step % per
    lane = iota((count, LANES), 1)
    lanes = pl.ds(half * LANES, LANES) if isinstance(step, int) else tile_lanes(half, 1)
    both = jnp.where(lane // GROUP == local, sides[0, where_rows, lanes], sides[1, where_rows, lanes])
    both = pltpu.roll(both, (LANES - local * GROUP) % LANES, 1)
    return jnp.where((lane < GROUP) | (lane >= LANES - GROUP), both, 0.0)


def first_filter_kernel(z, mix, band_cols, u, u_edges, y):
    steps, rows, cols = z.shape
    groups = rows // GROUP
    flat = (steps * GROUP, LANES)

    def across(quad, carry):
        parts = [z[:, rows_of(4 * quad + i), :].reshape(flat) for i in range(4)]
        value = halves(dot(pair(jnp.concatenate(parts, axis=0)), band_cols[...]))
        both = split(value)
        for i in range(4):
            for part in range(2):
                y[2 * quad + i // 2, part, :, pl.ds((i % 2) * LANES, LANES)] = both[part][
                    i * flat[0] : (i + 1) * flat[0]
                ]
        return carry

    lax.fori_loop(0, groups // 4, across, 0, unroll=4)

    def mixing(two, carry):
        right = jnp.concatenate([y[two, 0], y[two, 1], y[two, 0]], axis=0)
        out = dot(mix[...], right)
        u[:, rows_of(2 * two), :] = out[:, :LANES].reshape(steps, GROUP, LANES)
        u[:, rows_of(2 * two + 1), :] = out[:, LANES:].reshape(steps, GROUP, LANES)
        return carry

    lax.fori_loop(0, groups // 2, mixing, 0, unroll=8)
    u_edges[0] = u[:, pl.ds(0, GROUP), :]
    u_edges[1] = u[:, pl.ds(rows - GROUP, GROUP), :]


def filter_unsort_kernel(z, mix, band_cols, flat_rows, rank, u, u_edges, unsorted, y):
    first_filter_kernel(z, mix, band_cols, u, u_edges, y)
    steps, slots = flat_rows.shape
    tiles = slots // LANES
    pieces = three(flat_rows[...])

    def unsort_block(block, carry):
        lanes = tile_lanes(block, 1)
        order = (iota((slots, LANES), 0) == rank[:, lanes]).astype(F32).astype(BF16)
        out = dot(pieces, order)
        unsorted[:, lanes] = out[:steps] + out[steps : 2 * steps] + out[2 * steps :]
        return carry

    lax.fori_loop(0, tiles, unsort_block, 0)


def second_filter_kernel(u, sides, band_rows, w):
    steps, rows, cols = u.shape

    def along(two, carry):
        one = split(u[2 * two])
        other = split(u[2 * two + 1])
        high = jnp.concatenate([one[0], other[0]], axis=1)
        low = jnp.concatenate([one[1], other[1]], axis=1)
        out = dot(band_rows[...], jnp.concatenate([high, low, high], axis=0))
        everything = pl.ds(0, rows)
        w[2 * two] = out[:, :LANES] + unpack(sides, everything, rows, 2 * two)
        w[2 * two + 1] = out[:, LANES:] + unpack(sides, everything, rows, 2 * two + 1)
        return carry

    lax.fori_loop(0, steps // 2, along, 0, unroll=8)


def edge_kernel(first, second, u_edges, mat, band_rows, sides, full_edges):
    steps = u_edges.shape[1]
    rows = first.shape[0]
    for place, source in ((0, first), (1, second)):
        side = slot_of("col", place)
        high, low = split(source[...])
        value = dot(high, mat[2 * side]) + dot(low, mat[2 * side])
        value = value + dot(high, mat[2 * side + 1])
        sides[side] = value
    for which, start in ((0, 0), (1, rows - GROUP)):
        slot = slot_of("row", which)
        for step in range(steps):
            full_edges[slot, step] = u_edges[which, step] + unpack(
                sides, pl.ds(start, GROUP), GROUP, step
            )
    for side in range(2):
        high, low = split(sides[side])
        sides[side] = dot(band_rows[...], jnp.concatenate([high, low, high], axis=0))


def fill_extra(extra, first, second, edge):
    steps = first.shape[0]
    flat = (steps * GROUP, LANES)
    for place, source in ((0, first), (1, second)):
        which = slot_of("row", place)
        both = pair(source[...].reshape(flat))
        value = halves(dot(edge[2 * which], both)) + dot(edge[2 * which + 1], both[:, :LANES])
        extra[which] = value.reshape(steps, GROUP, LANES)
    extra[2] = jnp.zeros((steps, GROUP, LANES), F32)


def which_extra(g, groups):
    return jnp.where(g == 0, 0, jnp.where(g == groups - 1, 1, 2))


def gather_tile(g, both, index, acc, spots, gv):
    steps = acc.shape[0]
    lanes = tile_lanes(index, 1)
    out = halves(dot(both, gv[index])).reshape(steps, GROUP, LANES)
    weight = row_weights(g, lanes, spots)
    for times in chunks(steps):
        acc[times, :, lanes] += out[times.start : times.start + times.size] * weight


def whole(x):
    return jnp.sum(jnp.sum(x, axis=1, keepdims=True), axis=0, keepdims=True)


def fold(x):
    return jnp.sum(x, axis=0)


def fold_flat(x):
    return fold(x.reshape(x.shape[0] // GROUP, GROUP, LANES))


def image_one_kernel(
    bounds, w, above, below, edge, noise, b, ordered, info, spots, gv, sv,
    p, z, strips, sums, flat_rows, acc, extra, ps, compact, shifted,
):
    steps, rows, _ = w.shape
    groups = rows // GROUP
    tiles = info.shape[1] // LANES
    fill_extra(extra, above, below, edge)
    acc[...] = jnp.zeros_like(acc)

    def run(g, carry):
        here = rows_of(g)
        which = which_extra(g, groups)
        spread = noise[here, :][None]
        first, second, third = carry
        left = []
        for times in chunks(steps):
            value = w[times, here, :] + extra[which, times]
            left.append(pair(value.reshape(GROUP * GROUP, LANES)))
            mine = b[times, here, :]
            image = value + spread * mine
            p[times, here, :] = image
            first = first + fold(mine * mine)
            second = second + fold(mine * image)
            third = third + fold(image * image)
        gather_tile(g, jnp.concatenate(left, axis=0), bounds[g, 0], acc, spots, gv)
        return first, second, third

    zero = jnp.zeros((GROUP, LANES), F32)
    carry = lax.fori_loop(0, groups, run, (zero,) * 3, unroll=2)

    @pl.when(bounds[0, 2] > 1)
    def _():
        def crowded(g, inner):
            value = w[:, rows_of(g), :] + extra[which_extra(g, groups)]
            both = pair(value.reshape(steps * GROUP, LANES))

            def more(index, innermost):
                gather_tile(g, both, bounds[g, 0] + 2 * index, acc, spots, gv)
                return innermost

            return lax.fori_loop(1, bounds[g, 1], more, inner)

        lax.fori_loop(0, groups, crowded, 0)

    wide = steps * GROUP
    adds = (iota((steps, 2 * wide), 1) % wide // GROUP == iota((steps, 2 * wide), 0)).astype(F32)
    adds = adds.astype(BF16)

    def fold_rows(index, inner):
        lanes = tile_lanes(2 * index, 2)
        high, low = split(acc[:, :, lanes].reshape(wide, 2 * LANES))
        compact[:, lanes] = dot(adds, jnp.concatenate([high, low], axis=0))
        return inner

    lax.fori_loop(0, tiles, fold_rows, 0)
    lane = iota((steps, LANES), 1)
    first, second, third = carry
    for block in range(tiles):
        place = pl.ds(block * LANES, LANES)
        before = jnp.zeros((steps, LANES), F32)
        if block:
            before = compact[:, pl.ds((2 * block - 1) * LANES, LANES)]
        after = compact[:, pl.ds((2 * block + 1) * LANES, LANES)]
        sampled = compact[:, pl.ds(2 * block * LANES, LANES)] + pltpu.roll(
            jnp.where(lane < HALF, after, before), HALF, 1
        )
        mine = ordered[:, place]
        image = info[pl.ds(1, 1), place] * sampled + info[pl.ds(0, 1), place] * mine
        flat_rows[:, place] = image
        first = first + fold_flat(mine * mine)
        second = second + fold_flat(mine * image)
        third = third + fold_flat(image * image)
    carry = first, second, third
    for block in range(tiles):
        shifted[:, pl.ds(block * LANES, LANES)] = shifted_block(flat_rows, block, tiles)
    ps[:, :, tile_lanes(2 * tiles, 1)] = jnp.zeros((steps, GROUP, LANES), F32)
    spread_rows(flat_rows, shifted, ps, steps, tiles)
    bb, bp, pp = (whole(x) for x in carry)
    lane = iota((GROUP, LANES), 1)
    value = jnp.where(lane == 0, bb / bp, 0.0)
    value = jnp.where(lane == 1, bb, value)
    value = jnp.where(lane == 2, bp, value)
    value = jnp.where(lane == 3, pp, value)
    sums[...] = value
    scatter_all(p, z, strips, ps, spots, sv, bounds)


def image_two_kernel(
    w, above, below, edge, noise, b, p, z_first, z, ordered, flat_rows, info, sums,
    q, message, extra,
):
    steps, rows, _ = w.shape
    groups = rows // GROUP
    tiles = info.shape[1] // LANES
    fill_extra(extra, above, below, edge)
    shift = jnp.broadcast_to(sums[0:1, 0:1], (GROUP, LANES))[None]

    def run(g, carry):
        here = rows_of(g)
        which = which_extra(g, groups)
        spread = noise[here, :][None]
        first, second, third = carry
        for times in chunks(steps, 4):
            value = w[times, here, :] + extra[which, times]
            mine = p[times, here, :]
            scaled = spread * mine
            q[times, here, :] = value + scaled
            residual = b[times, here, :] - shift * mine
            image = z[times, here, :]
            moved = z_first[times, here, :] - shift * image
            first = first + fold(residual * residual)
            second = second + fold(moved * value + residual * scaled)
            third = third + fold(image * value + mine * scaled)
        return first, second, third

    zero = jnp.zeros((GROUP, LANES), F32)
    carry = lax.fori_loop(0, groups, run, (zero,) * 3, unroll=1)

    first, second, third = carry
    own_shift = sums[0:1, 0:1]
    for block in range(tiles):
        place = pl.ds(block * LANES, LANES)
        mine = flat_rows[:, place]
        scaled = info[pl.ds(0, 1), place] * mine
        residual = ordered[:, place] - own_shift * mine
        first = first + fold_flat(residual * residual)
        second = second + fold_flat(residual * scaled)
        third = third + fold_flat(mine * scaled)
    carry = first, second, third
    lane = iota((1, LANES), 1)
    value = jnp.where(lane < 4, sums[0:1, :], 0.0)
    for place, x in enumerate(carry):
        value = jnp.where(lane == 4 + place, whole(x), value)
    message[...] = jnp.broadcast_to(value, message.shape)


def final_kernel(
    received, b, p, q, own, unsorted, solution_out, residual_out, station_out,
    solution_v, residual_v, station_v, sems, station_sem,
):
    everything = received[...]

    def column(index):
        return everything[:, index : index + 1]

    def total(x):
        return jnp.sum(x, axis=0, keepdims=True)

    shift, bb, bp, pp = (column(i) for i in range(4))
    rr, rq, pq = (column(i) for i in range(4, 7))
    norm = total(bb)
    alpha = norm / total(bp)
    delta = shift - alpha
    rp = bp - shift * pp
    ru = rp - shift * rq
    pu = pp - shift * pq
    norm_next = total(rr + 2.0 * delta * rp + delta * delta * pp)
    energy = total(ru + delta * (rq + pu) + delta * delta * pq)
    beta = norm_next / norm
    alpha_next = norm_next / (energy - beta * norm_next / alpha)
    along = alpha + alpha_next * (1.0 + beta)
    twice = alpha_next * alpha
    steps, rows, _ = b.shape
    chunk = 64
    tall = (chunk // GROUP, GROUP, LANES)
    wide_along = jnp.broadcast_to(along, (GROUP, LANES))[None]
    wide_twice = jnp.broadcast_to(twice, (GROUP, LANES))[None]

    def copies(place):
        here = pl.ds(place * 2, 2)
        return (
            pltpu.make_async_copy(solution_v.at[here], solution_out.at[here], sems.at[0, place]),
            pltpu.make_async_copy(residual_v.at[here], residual_out.at[here], sems.at[1, place]),
        )

    def run(place, carry):
        for inner in range(2):
            step = place * 2 + inner
            for piece in range(rows // chunk):
                here = pl.ds(piece * chunk, chunk)
                first = b[step, here, :].reshape(tall)
                second = p[step, here, :].reshape(tall)
                third = q[step, here, :].reshape(tall)
                solution_v[step, here, :] = (wide_along * first - wide_twice * second).reshape(
                    chunk, LANES
                )
                residual_v[step, here, :] = (
                    first - wide_along * second + wide_twice * third
                ).reshape(chunk, LANES)
        for copy in copies(place):
            copy.start()
        return carry

    lax.fori_loop(0, steps // 2, run, 0)
    stations = along * own[...] - twice * unsorted[...]
    for step in range(steps):
        station_v[step, 0] = stations[step : step + 1]
    station_copy = pltpu.make_async_copy(station_v, station_out, station_sem)
    station_copy.start()

    def finish(place, carry):
        for copy in copies(place):
            copy.wait()
        return carry

    lax.fori_loop(0, steps // 2, finish, 0)
    station_copy.wait()


VMEM = pl.BlockSpec(memory_space=pltpu.VMEM)
SMEM = pl.BlockSpec(memory_space=pltpu.SMEM)
ANY = pl.BlockSpec(memory_space=pltpu.HBM)


def call(kernel, outs, ins, operands, scratch=(), flops=10**9, moved=10**7, limit=8, **extra):
    return pl.pallas_call(
        kernel,
        out_shape=outs,
        in_specs=ins,
        out_specs=[VMEM] * len(outs),
        scratch_shapes=list(scratch),
        compiler_params=pltpu.CompilerParams(vmem_limit_bytes=limit * 2**20),
        cost_estimate=pl.CostEstimate(flops=flops, bytes_accessed=moved, transcendentals=0),
        **extra,
    )(*operands)


def exchange(both, axis):
    count = lax.axis_size(axis)
    pairs = [[(i, i + 1) for i in range(start, count - 1, 2)] for start in (0, 1)]
    return tuple(
        lax.ppermute(both[place], axis, found + [(b, a) for a, b in found])
        for place, found in enumerate(pairs)
    )


def body(
    grid_obs, grid_noise, station_obs, station_noise, station_offset, station_cell,
    station_count, time_cov,
):
    steps, rows, cols = grid_obs.shape
    slots = station_obs.shape[3]
    wide = steps * GROUP
    groups = rows // GROUP
    tiles = 2 * (slots // LANES) + 1
    lanes = tiles * LANES
    devices = lax.axis_size("row") * lax.axis_size("col")
    shape = jax.ShapeDtypeStruct
    field = shape((steps, rows, cols), F32)
    rim = shape((2, steps, GROUP, cols), F32)
    strips_shape = shape((2, rows, wide), F32)
    station_field = shape((steps, GROUP, lanes), F32)
    extra = pltpu.VMEM((3, steps, GROUP, LANES), F32)
    (
        b, z_first, strips, sb, ordered, info, rank, own, sv, gv, spots,
        band_rows, band_cols, edge, bounds,
    ) = pl.pallas_call(
        prepare_kernel,
        out_shape=[
            field,
            field,
            strips_shape,
            station_field,
            shape((steps, slots), F32),
            shape((2, slots), F32),
            shape((1, slots), jnp.int32),
            shape((steps, slots), F32),
            shape((tiles, 2 * LANES, 2 * LANES), BF16),
            shape((tiles, 2 * LANES, 2 * LANES), BF16),
            shape((2, GROUP, lanes), F32),
            shape((rows, 3 * rows), BF16),
            shape((2 * LANES, 2 * LANES), BF16),
            shape((4, wide, wide), BF16),
            shape((groups, LANES), jnp.int32),
        ],
        in_specs=[SMEM] + [ANY] * 5,
        out_specs=[VMEM] * 14 + [SMEM],
        scratch_shapes=[
            pltpu.VMEM((1, 1, slots), jnp.int32),
            pltpu.VMEM((2, 1, 1, slots), F32),
            pltpu.VMEM((1, 1, slots), F32),
            pltpu.VMEM((steps, 1, 1, slots), F32),
            pltpu.VMEM((groups, LANES), jnp.int32),
            pltpu.VMEM((steps + 8, slots), F32),
            pltpu.VMEM((steps + 8, slots), F32),
            pltpu.VMEM((steps + 8, slots), F32),
            pltpu.SemaphoreType.DMA((6,)),
        ],
        compiler_params=pltpu.CompilerParams(vmem_limit_bytes=8 * 2**20),
        cost_estimate=pl.CostEstimate(flops=10**9, bytes_accessed=10**7, transcendentals=0),
    )(
        station_count,
        *(
            pltpu.with_memory_space_constraint(x, pltpu.HBM)
            for x in (station_cell, station_offset, station_noise, station_obs, grid_obs)
        ),
    )
    mix, mat = call(
        matrices_kernel,
        [shape((wide, 3 * wide), BF16), shape((4, wide, wide), BF16)],
        [VMEM],
        (time_cov,),
    )

    def smooth(z, strips, *more):
        from_left, from_right = exchange(strips, "col")
        u, u_edges, *unsorted = call(
            filter_unsort_kernel if more else first_filter_kernel,
            [field, rim] + [shape((steps, slots), F32)] * bool(more),
            [VMEM] * (3 + len(more)),
            (z, mix, band_cols, *more),
            [pltpu.VMEM((groups // 2, 2, wide, 2 * LANES), BF16)],
        )
        sides, full_edges = call(
            edge_kernel,
            [strips_shape, rim],
            [VMEM] * 5,
            (from_left, from_right, u_edges, mat, band_rows),
            limit=4,
        )
        above, below = exchange(full_edges, "row")
        (w,) = call(
            second_filter_kernel, [field], [VMEM] * 3, (u, sides, band_rows), limit=4
        )
        return w, above, below, *unsorted

    w, above, below = smooth(z_first, strips)
    p, z, strips, sums, flat_rows = call(
        image_one_kernel,
        [field, field, strips_shape, shape((GROUP, LANES), F32), shape((steps, slots), F32)],
        [SMEM] + [VMEM] * 11,
        (bounds, w, above, below, edge, grid_noise, b, ordered, info, spots, gv, sv),
        [
            pltpu.VMEM((steps, GROUP, lanes), F32),
            extra,
            pltpu.VMEM((steps, GROUP, lanes), F32),
            pltpu.VMEM((steps, lanes), F32),
            pltpu.VMEM((steps, slots), F32),
        ],
        limit=12,
    )
    w, above, below, unsorted = smooth(z, strips, flat_rows, rank)
    q, message = call(
        image_two_kernel,
        [field, shape((devices, LANES), F32)],
        [VMEM] * 13,
        (w, above, below, edge, grid_noise, b, p, z_first, z, ordered, flat_rows, info, sums),
        [extra],
        limit=4,
    )
    received = lax.all_to_all(message, ("row", "col"), 0, 0, tiled=True)
    solution_grid, residual_grid, solution_stations = pl.pallas_call(
        final_kernel,
        out_shape=[field, field, shape((steps, 1, 1, slots), F32)],
        in_specs=[VMEM] * 6,
        out_specs=[ANY, ANY, ANY],
        scratch_shapes=[
            pltpu.VMEM((steps, rows, cols), F32),
            pltpu.VMEM((steps, rows, cols), F32),
            pltpu.VMEM((steps, 1, 1, slots), F32),
            pltpu.SemaphoreType.DMA((2, steps // 2)),
            pltpu.SemaphoreType.DMA(()),
        ],
        compiler_params=pltpu.CompilerParams(vmem_limit_bytes=10 * 2**20),
    )(received, b, p, q, own, unsorted)
    return solution_grid, solution_stations, residual_grid


def solution(mesh):
    placed = (
        P(None, "row", "col"),
        P("row", "col"),
        P(None, "row", "col", None),
        P("row", "col", None),
        P(None, "row", "col", None),
        P("row", "col", None),
        P("row", "col"),
        P(),
    )
    return jax.shard_map(
        body,
        mesh=mesh,
        in_specs=placed,
        out_specs=(P(None, "row", "col"), P(None, "row", "col", None), P(None, "row", "col")),
        check_vma=False,
    )
```

```python
import functools

import jax
import jax.numpy as jnp
from jax import lax
from jax.experimental import pallas as pl
from jax.experimental.pallas import tpu as pltpu
from jax.sharding import PartitionSpec as P

REACH = 8
LANES = 128
HALF = LANES // 2
GROUP = 8
F32 = jnp.float32
BF16 = jnp.bfloat16
HIGHEST = lax.Precision.HIGHEST


def iota(shape, dim):
    return lax.broadcasted_iota(jnp.int32, shape, dim)


def taper(distance):
    spread = jnp.abs(distance).astype(F32)
    value = (1.0 - spread / (REACH + 1)) * jnp.exp(-spread / 3.0)
    return jnp.where(jnp.abs(distance) <= REACH, value, 0.0)


def split(x):
    high = x.astype(BF16)
    return high, (x - high.astype(F32)).astype(BF16)


def pair(x):
    high, low = split(x)
    return jnp.concatenate([high, low], axis=1)


def doubled(weights):
    high, low = split(weights)
    return jnp.concatenate(
        [
            jnp.concatenate([high, low], axis=1),
            jnp.concatenate([high, jnp.zeros_like(low)], axis=1),
        ],
        axis=0,
    )


def dot(a, b):
    return jnp.dot(a, b, preferred_element_type=F32)


def dot_nt(a, b):
    return lax.dot_general(a, b, (((1,), (1,)), ((), ())), preferred_element_type=F32)


def halves(x):
    width = x.shape[1] // 2
    return x[:, :width] + x[:, width:]


def three(x):
    high = x.astype(BF16)
    rest = x - high.astype(F32)
    middle = rest.astype(BF16)
    low = (rest - middle.astype(F32)).astype(BF16)
    return jnp.concatenate([high, middle, low], axis=0)


def cut(x, axis):
    return [
        lax.slice_in_dim(x, start, start + LANES, axis=axis)
        for start in range(0, x.shape[axis], LANES)
    ]


def slot_of(axis, side):
    odd = lax.rem(lax.axis_index(axis), 2)
    return odd if side else 1 - odd


def chunks(steps, size=GROUP):
    return [pl.ds(start, size) for start in range(0, steps, size)]


def shifted_block(source, block, blocks):
    here = source[:, pl.ds(block * LANES, LANES)]
    after = jnp.zeros_like(here)
    if block + 1 < blocks:
        after = source[:, pl.ds((block + 1) * LANES, LANES)]
    return pltpu.roll(jnp.where(iota(here.shape, 1) < HALF, after, here), HALF, 1)


def spread_rows(even, odd, target, steps, blocks):
    for tile in range(2 * blocks):
        source = odd if tile % 2 else even
        place = pl.ds(tile // 2 * LANES, LANES)
        for step in range(steps):
            target[step, :, pl.ds(tile * LANES, LANES)] = jnp.broadcast_to(
                source[pl.ds(step, 1), place], (GROUP, LANES)
            )


def rows_of(g):
    return pl.ds(pl.multiple_of(g * GROUP, GROUP), GROUP)


def prepare_kernel(
    count, cell_any, offset_any, noise_any, obs_any, base_any,
    base, z, strips, sb, ordered, info, rank_out, own, sv, gv, spots,
    band_rows, band_cols, edge, bounds,
    cell_v, offset_v, noise_v, obs_v, bounds_v, table, sorted_rows, shifted_rows, copies,
):
    small = [
        pltpu.make_async_copy(source, target, copies.at[1 + place])
        for place, (source, target) in enumerate(
            ((cell_any, cell_v), (offset_any, offset_v), (noise_any, noise_v), (obs_any, obs_v))
        )
    ]
    for copy in small:
        copy.start()
    base_copy = pltpu.make_async_copy(base_any, base, copies.at[0])
    base_copy.start()
    fixed_matrices(band_rows, band_cols, edge)
    for copy in small:
        copy.wait()
    cell, noise = cell_v[0], noise_v[0]
    steps, slots = own.shape
    tiles = slots // LANES
    rows = base.shape[1]
    groups = rows // GROUP
    slot = iota((1, slots), 1)
    live = slot < count[0, 0]
    where_row = cell // LANES
    where_col = cell - where_row * LANES
    key = jnp.where(live, where_row, rows) * slots + slot
    key = key.astype(F32)
    total = jnp.zeros((1, slots), F32)
    for block in range(tiles):
        piece = key[:, block * LANES : (block + 1) * LANES]
        column = jnp.transpose(jnp.broadcast_to(piece, (LANES, LANES)))
        column = jnp.concatenate([column] * tiles, axis=1)
        less = jnp.where(column < key, 1.0, 0.0)
        total = total + jnp.sum(less, axis=0, keepdims=True)
    rank = total.astype(jnp.int32)
    rank_out[...] = rank
    lived = jnp.where(live, 1.0, 0.0)
    for step in range(steps):
        own[pl.ds(step, 1), :] = obs_v[step, 0] * lived
    table[pl.ds(0, steps), :] = own[...]
    table[pl.ds(steps, 1), :] = where_row.astype(F32)
    table[pl.ds(steps + 1, 1), :] = where_col.astype(F32)
    table[pl.ds(steps + 2, 1), :] = offset_v[0, 0]
    table[pl.ds(steps + 3, 1), :] = offset_v[1, 0]
    table[pl.ds(steps + 4, 1), :] = noise
    table[pl.ds(steps + 5, 1), :] = lived
    table[pl.ds(steps + 6, 2), :] = jnp.zeros((2, slots), F32)
    pieces = three(table[...])
    height = table.shape[0]

    def sort_block(block, carry):
        start = pl.multiple_of(block * LANES, LANES)
        order = (iota((LANES, slots), 0) + start == rank).astype(F32).astype(BF16)
        out = dot_nt(pieces, order)
        sorted_rows[:, pl.ds(start, LANES)] = (
            out[:height] + out[height : 2 * height] + out[2 * height :]
        )
        return carry

    lax.fori_loop(0, tiles, sort_block, 0, unroll=8)
    ordered_row = sorted_rows[pl.ds(steps, 1), :]
    ordered_live = sorted_rows[pl.ds(steps + 5, 1), :]
    first_row = (iota((groups, slots), 0) * GROUP).astype(F32)
    before = jnp.where(ordered_row < first_row - 1.0, ordered_live, 0.0)
    until = jnp.where(ordered_row < first_row + GROUP, ordered_live, 0.0)
    low = jnp.sum(before, axis=1, keepdims=True)
    high = jnp.sum(until, axis=1, keepdims=True)
    start_tile = jnp.where(high > low, jnp.floor(low * (1.0 / HALF)), float(2 * tiles))
    reached = jnp.where(high > low, high - HALF * start_tile, 1.0)
    needed = jnp.floor((reached + (LANES - 1.0)) * (1.0 / LANES))
    most = jnp.max(needed, axis=0, keepdims=True)
    lane = iota((groups, LANES), 1)
    bounds_v[...] = jnp.where(
        lane == 0, start_tile, jnp.where(lane == 1, needed, most)
    ).astype(jnp.int32)
    bounds_copy = pltpu.make_async_copy(bounds_v, bounds, copies.at[5])
    bounds_copy.start()
    ordered[...] = sorted_rows[pl.ds(0, steps), :]
    alive = sorted_rows[pl.ds(steps + 5, 1), :]
    info[pl.ds(0, 1), :] = alive * sorted_rows[pl.ds(steps + 4, 1), :] + (1.0 - alive)
    info[pl.ds(1, 1), :] = alive
    for block in range(tiles):
        shifted_rows[:, pl.ds(block * LANES, LANES)] = shifted_block(sorted_rows, block, tiles)
    none = tile_lanes(2 * tiles, 1)
    sb[:, :, none] = jnp.zeros((steps, GROUP, LANES), F32)
    spots[:, :, none] = jnp.full((2, GROUP, LANES), -1000.0, F32)
    for target in (sv, gv):
        target[2 * tiles] = jnp.zeros((2 * LANES, 2 * LANES), BF16)
    spread_rows(sorted_rows, shifted_rows, sb, steps, tiles)
    for tile in range(2 * tiles):
        source = shifted_rows if tile % 2 else sorted_rows
        place = pl.ds(tile // 2 * LANES, LANES)
        lanes = pl.ds(tile * LANES, LANES)
        spots[0, :, lanes] = jnp.broadcast_to(source[pl.ds(steps, 1), place], (GROUP, LANES))
        spots[1, :, lanes] = jnp.broadcast_to(source[pl.ds(steps + 2, 1), place], (GROUP, LANES))
        at_col = source[pl.ds(steps + 1, 1), place].astype(jnp.int32)
        along_col = source[pl.ds(steps + 3, 1), place]
        col = iota((LANES, LANES), 0)
        across = jnp.where(
            col == at_col, 1.0 - along_col, jnp.where(col == at_col + 1, along_col, 0.0)
        )
        gv[tile] = doubled(across)
        if tile % 2 == 0:
            sv[tile] = doubled(jnp.transpose(across))
    for tile in range(1, 2 * tiles, 2):
        for start in (0, LANES):
            sv[tile, pl.ds(start, HALF), :] = sv[tile - 1, pl.ds(start + HALF, HALF), :]
            sv[tile, pl.ds(start + HALF, HALF), :] = sv[tile + 1, pl.ds(start, HALF), :]
    bounds_copy.wait()
    base_copy.wait()
    scatter_all(base, z, strips, sb, spots, sv, bounds)


def matrices_kernel(cov, mix, mat):
    steps = cov.shape[0]
    wide = steps * GROUP
    spread = (iota((wide, steps), 0) // GROUP == iota((wide, steps), 1)).astype(F32)
    spread_t = (iota((steps, wide), 1) // GROUP == iota((steps, wide), 0)).astype(F32)
    expanded = jnp.dot(
        jnp.dot(spread, cov[...], precision=HIGHEST, preferred_element_type=F32),
        spread_t,
        precision=HIGHEST,
        preferred_element_type=F32,
    )
    a = iota((wide, wide), 0)
    b = iota((wide, wide), 1)
    same = (a % GROUP) == (b % GROUP)
    high_part, low_part = split(jnp.where(same, expanded, 0.0))
    mix[...] = jnp.concatenate([high_part, high_part, low_part], axis=1)
    near = taper((b % GROUP) + REACH - (a % GROUP)) * expanded
    near = jnp.concatenate(
        [jnp.concatenate([x[GROUP:], x[:GROUP]], axis=0) for x in cut(near, 0)], axis=0
    )
    mat[0], mat[1] = split(near)
    far = taper(REACH + (a % GROUP) - (b % GROUP)) * expanded
    far = jnp.concatenate(
        [pltpu.roll(x, LANES - GROUP, 1) for x in cut(far, 1)], axis=1
    )
    mat[2], mat[3] = split(far)


def fixed_matrices(band_rows, band_cols, edge):
    rows = band_rows.shape[0]
    wide = edge.shape[1]
    a = iota((wide, wide), 0)
    b = iota((wide, wide), 1)
    ra = iota((rows, rows), 0)
    rb = iota((rows, rows), 1)
    high_part, low_part = split(0.25 * taper(ra - rb))
    band_rows[...] = jnp.concatenate([high_part, high_part, low_part], axis=1)
    ca = iota((LANES, LANES), 0)
    cb = iota((LANES, LANES), 1)
    band_cols[...] = doubled(taper(ca - cb))
    block_same = (a // GROUP) == (b // GROUP)
    above = 0.25 * taper((a % GROUP) + REACH - (b % GROUP))
    below = 0.25 * taper(REACH + (b % GROUP) - (a % GROUP))
    edge[0], edge[1] = split(jnp.where(block_same, above, 0.0))
    edge[2], edge[3] = split(jnp.where(block_same, below, 0.0))


def tile_lanes(index, count):
    return pl.ds(pl.multiple_of(index * LANES, LANES), count * LANES)


def row_weights(g, lanes, spots):
    row = (iota((GROUP, LANES), 0) + g * GROUP).astype(F32)
    offset = row - spots[0, :, lanes]
    along = spots[1, :, lanes]
    return jnp.where(offset == 0.0, 1.0 - along, jnp.where(offset == 1.0, along, 0.0))[None]


def spread_tile(g, index, sb, spots, sv):
    steps = sb.shape[0]
    lanes = tile_lanes(index, 1)
    weight = row_weights(g, lanes, spots)
    left = jnp.concatenate(
        [
            pair((sb[times, :, lanes] * weight).reshape(GROUP * GROUP, LANES))
            for times in chunks(steps)
        ],
        axis=0,
    )
    return halves(dot(left, sv[index])).reshape(steps, GROUP, LANES)


def scatter_all(base, z, strips, sb, spots, sv, bounds):
    groups = base.shape[1] // GROUP

    def run(g, carry):
        value = base[:, rows_of(g), :] + spread_tile(g, bounds[g, 0], sb, spots, sv)
        z[:, rows_of(g), :] = value
        pack_group(g, value, strips)
        return carry

    lax.fori_loop(0, groups, run, 0, unroll=32)

    @pl.when(bounds[0, 2] > 1)
    def _():
        def crowded(g, carry):
            def more(index, inner):
                z[:, rows_of(g), :] += spread_tile(g, bounds[g, 0] + 2 * index, sb, spots, sv)
                return inner

            lax.fori_loop(1, bounds[g, 1], more, 0)
            pack_group(g, z[:, rows_of(g), :], strips)
            return carry

        lax.fori_loop(0, groups, crowded, 0)


def pack_group(g, value, strips):
    steps = value.shape[0]
    per = LANES // GROUP
    slot = iota((GROUP, LANES), 1) // GROUP
    for half in range(steps // per):
        left = jnp.zeros((GROUP, LANES), F32)
        right = jnp.zeros((GROUP, LANES), F32)
        for local in range(per):
            moved = value[half * per + local]
            if local:
                moved = pltpu.roll(moved, local * GROUP, 1)
            left = jnp.where(slot == local, moved, left)
            right = jnp.where(slot == (local - 1) % per, moved, right)
        lanes = pl.ds(half * LANES, LANES)
        strips[slot_of("col", 0), rows_of(g), lanes] = left
        strips[slot_of("col", 1), rows_of(g), lanes] = right


def unpack(sides, where_rows, count, step):
    per = LANES // GROUP
    half, local = step // per, step % per
    lane = iota((count, LANES), 1)
    lanes = pl.ds(half * LANES, LANES) if isinstance(step, int) else tile_lanes(half, 1)
    both = jnp.where(lane // GROUP == local, sides[0, where_rows, lanes], sides[1, where_rows, lanes])
    both = pltpu.roll(both, (LANES - local * GROUP) % LANES, 1)
    return jnp.where((lane < GROUP) | (lane >= LANES - GROUP), both, 0.0)


def first_filter_kernel(z, mix, band_cols, u, u_edges, y):
    steps, rows, cols = z.shape
    groups = rows // GROUP
    flat = (steps * GROUP, LANES)

    def across(quad, carry):
        parts = [z[:, rows_of(4 * quad + i), :].reshape(flat) for i in range(4)]
        value = halves(dot(pair(jnp.concatenate(parts, axis=0)), band_cols[...]))
        both = split(value)
        for i in range(4):
            for part in range(2):
                y[2 * quad + i // 2, part, :, pl.ds((i % 2) * LANES, LANES)] = both[part][
                    i * flat[0] : (i + 1) * flat[0]
                ]
        return carry

    lax.fori_loop(0, groups // 4, across, 0, unroll=8)

    def mixing(two, carry):
        right = jnp.concatenate([y[two, 0], y[two, 1], y[two, 0]], axis=0)
        out = dot(mix[...], right)
        u[:, rows_of(2 * two), :] = out[:, :LANES].reshape(steps, GROUP, LANES)
        u[:, rows_of(2 * two + 1), :] = out[:, LANES:].reshape(steps, GROUP, LANES)
        return carry

    lax.fori_loop(0, groups // 2, mixing, 0, unroll=16)
    u_edges[0] = u[:, pl.ds(0, GROUP), :]
    u_edges[1] = u[:, pl.ds(rows - GROUP, GROUP), :]


def filter_unsort_kernel(z, mix, band_cols, flat_rows, rank, u, u_edges, unsorted, y):
    first_filter_kernel(z, mix, band_cols, u, u_edges, y)
    steps, slots = flat_rows.shape
    tiles = slots // LANES
    pieces = three(flat_rows[...])

    def unsort_block(block, carry):
        lanes = tile_lanes(block, 1)
        order = (iota((slots, LANES), 0) == rank[:, lanes]).astype(F32).astype(BF16)
        out = dot(pieces, order)
        unsorted[:, lanes] = out[:steps] + out[steps : 2 * steps] + out[2 * steps :]
        return carry

    lax.fori_loop(0, tiles, unsort_block, 0, unroll=4)


def second_filter_kernel(u, sides, band_rows, w):
    steps, rows, cols = u.shape

    def along(two, carry):
        one = split(u[2 * two])
        other = split(u[2 * two + 1])
        high = jnp.concatenate([one[0], other[0]], axis=1)
        low = jnp.concatenate([one[1], other[1]], axis=1)
        out = dot(band_rows[...], jnp.concatenate([high, low, high], axis=0))
        everything = pl.ds(0, rows)
        w[2 * two] = out[:, :LANES] + unpack(sides, everything, rows, 2 * two)
        w[2 * two + 1] = out[:, LANES:] + unpack(sides, everything, rows, 2 * two + 1)
        return carry

    lax.fori_loop(0, steps // 2, along, 0, unroll=16)


def edge_kernel(first, second, u_edges, mat, band_rows, sides, full_edges):
    steps = u_edges.shape[1]
    rows = first.shape[0]
    for place, source in ((0, first), (1, second)):
        side = slot_of("col", place)
        high, low = split(source[...])
        value = dot(high, mat[2 * side]) + dot(low, mat[2 * side])
        value = value + dot(high, mat[2 * side + 1])
        sides[side] = value
    for which, start in ((0, 0), (1, rows - GROUP)):
        slot = slot_of("row", which)
        for step in range(steps):
            full_edges[slot, step] = u_edges[which, step] + unpack(
                sides, pl.ds(start, GROUP), GROUP, step
            )
    for side in range(2):
        high, low = split(sides[side])
        sides[side] = dot(band_rows[...], jnp.concatenate([high, low, high], axis=0))


def fill_extra(extra, first, second, edge):
    steps = first.shape[0]
    flat = (steps * GROUP, LANES)
    for place, source in ((0, first), (1, second)):
        which = slot_of("row", place)
        both = pair(source[...].reshape(flat))
        value = halves(dot(edge[2 * which], both)) + dot(edge[2 * which + 1], both[:, :LANES])
        extra[which] = value.reshape(steps, GROUP, LANES)
    extra[2] = jnp.zeros((steps, GROUP, LANES), F32)


def which_extra(g, groups):
    return jnp.where(g == 0, 0, jnp.where(g == groups - 1, 1, 2))


def gather_tile(g, both, index, acc, spots, gv):
    steps = acc.shape[0]
    lanes = tile_lanes(index, 1)
    out = halves(dot(both, gv[index])).reshape(steps, GROUP, LANES)
    weight = row_weights(g, lanes, spots)
    for times in chunks(steps):
        acc[times, :, lanes] += out[times.start : times.start + times.size] * weight


def whole(x):
    return jnp.sum(jnp.sum(x, axis=1, keepdims=True), axis=0, keepdims=True)


def fold(x):
    return jnp.sum(x, axis=0)


def fold_flat(x):
    return fold(x.reshape(x.shape[0] // GROUP, GROUP, LANES))


def image_one_kernel(
    bounds, w, above, below, edge, noise, b, ordered, info, spots, gv, sv,
    p, z, strips, sums, flat_rows, acc, extra, ps, compact, shifted,
):
    steps, rows, _ = w.shape
    groups = rows // GROUP
    tiles = info.shape[1] // LANES
    fill_extra(extra, above, below, edge)
    acc[...] = jnp.zeros_like(acc)

    def run(g, carry):
        here = rows_of(g)
        which = which_extra(g, groups)
        spread = noise[here, :][None]
        first, second, third = carry
        left = []
        for times in chunks(steps):
            value = w[times, here, :] + extra[which, times]
            left.append(pair(value.reshape(GROUP * GROUP, LANES)))
            mine = b[times, here, :]
            image = value + spread * mine
            p[times, here, :] = image
            first = first + fold(mine * mine)
            second = second + fold(mine * image)
            third = third + fold(image * image)
        gather_tile(g, jnp.concatenate(left, axis=0), bounds[g, 0], acc, spots, gv)
        return first, second, third

    zero = jnp.zeros((GROUP, LANES), F32)
    carry = lax.fori_loop(0, groups, run, (zero,) * 3, unroll=8)

    @pl.when(bounds[0, 2] > 1)
    def _():
        def crowded(g, inner):
            value = w[:, rows_of(g), :] + extra[which_extra(g, groups)]
            both = pair(value.reshape(steps * GROUP, LANES))

            def more(index, innermost):
                gather_tile(g, both, bounds[g, 0] + 2 * index, acc, spots, gv)
                return innermost

            return lax.fori_loop(1, bounds[g, 1], more, inner)

        lax.fori_loop(0, groups, crowded, 0)

    wide = steps * GROUP
    adds = (iota((steps, 2 * wide), 1) % wide // GROUP == iota((steps, 2 * wide), 0)).astype(F32)
    adds = adds.astype(BF16)

    def fold_rows(index, inner):
        lanes = tile_lanes(2 * index, 2)
        high, low = split(acc[:, :, lanes].reshape(wide, 2 * LANES))
        compact[:, lanes] = dot(adds, jnp.concatenate([high, low], axis=0))
        return inner

    lax.fori_loop(0, tiles, fold_rows, 0)
    lane = iota((steps, LANES), 1)
    first, second, third = carry
    for block in range(tiles):
        place = pl.ds(block * LANES, LANES)
        before = jnp.zeros((steps, LANES), F32)
        if block:
            before = compact[:, pl.ds((2 * block - 1) * LANES, LANES)]
        after = compact[:, pl.ds((2 * block + 1) * LANES, LANES)]
        sampled = compact[:, pl.ds(2 * block * LANES, LANES)] + pltpu.roll(
            jnp.where(lane < HALF, after, before), HALF, 1
        )
        mine = ordered[:, place]
        image = info[pl.ds(1, 1), place] * sampled + info[pl.ds(0, 1), place] * mine
        flat_rows[:, place] = image
        first = first + fold_flat(mine * mine)
        second = second + fold_flat(mine * image)
        third = third + fold_flat(image * image)
    carry = first, second, third
    for block in range(tiles):
        shifted[:, pl.ds(block * LANES, LANES)] = shifted_block(flat_rows, block, tiles)
    ps[:, :, tile_lanes(2 * tiles, 1)] = jnp.zeros((steps, GROUP, LANES), F32)
    spread_rows(flat_rows, shifted, ps, steps, tiles)
    bb, bp, pp = (whole(x) for x in carry)
    lane = iota((GROUP, LANES), 1)
    value = jnp.where(lane == 0, bb / bp, 0.0)
    value = jnp.where(lane == 1, bb, value)
    value = jnp.where(lane == 2, bp, value)
    value = jnp.where(lane == 3, pp, value)
    sums[...] = value
    scatter_all(p, z, strips, ps, spots, sv, bounds)


def image_two_kernel(
    w, above, below, edge, noise, b, p, z_first, z, ordered, flat_rows, info, sums,
    q, message, extra,
):
    steps, rows, _ = w.shape
    groups = rows // GROUP
    tiles = info.shape[1] // LANES
    fill_extra(extra, above, below, edge)
    shift = jnp.broadcast_to(sums[0:1, 0:1], (GROUP, LANES))[None]

    def run(g, carry):
        here = rows_of(g)
        which = which_extra(g, groups)
        spread = noise[here, :][None]
        first, second, third = carry
        for times in chunks(steps, 4):
            value = w[times, here, :] + extra[which, times]
            mine = p[times, here, :]
            scaled = spread * mine
            q[times, here, :] = value + scaled
            residual = b[times, here, :] - shift * mine
            image = z[times, here, :]
            moved = z_first[times, here, :] - shift * image
            first = first + fold(residual * residual)
            second = second + fold(moved * value + residual * scaled)
            third = third + fold(image * value + mine * scaled)
        return first, second, third

    zero = jnp.zeros((GROUP, LANES), F32)
    carry = lax.fori_loop(0, groups, run, (zero,) * 3, unroll=4)

    first, second, third = carry
    own_shift = sums[0:1, 0:1]
    for block in range(tiles):
        place = pl.ds(block * LANES, LANES)
        mine = flat_rows[:, place]
        scaled = info[pl.ds(0, 1), place] * mine
        residual = ordered[:, place] - own_shift * mine
        first = first + fold_flat(residual * residual)
        second = second + fold_flat(residual * scaled)
        third = third + fold_flat(mine * scaled)
    carry = first, second, third
    lane = iota((1, LANES), 1)
    value = jnp.where(lane < 4, sums[0:1, :], 0.0)
    for place, x in enumerate(carry):
        value = jnp.where(lane == 4 + place, whole(x), value)
    message[...] = jnp.broadcast_to(value, message.shape)


def final_kernel(
    received, b, p, q, own, unsorted, solution_out, residual_out, station_out,
    solution_v, residual_v, station_v, sems, station_sem,
):
    everything = received[...]

    def column(index):
        return everything[:, index : index + 1]

    def total(x):
        return jnp.sum(x, axis=0, keepdims=True)

    shift, bb, bp, pp = (column(i) for i in range(4))
    rr, rq, pq = (column(i) for i in range(4, 7))
    norm = total(bb)
    alpha = norm / total(bp)
    delta = shift - alpha
    rp = bp - shift * pp
    ru = rp - shift * rq
    pu = pp - shift * pq
    norm_next = total(rr + 2.0 * delta * rp + delta * delta * pp)
    energy = total(ru + delta * (rq + pu) + delta * delta * pq)
    beta = norm_next / norm
    alpha_next = norm_next / (energy - beta * norm_next / alpha)
    along = alpha + alpha_next * (1.0 + beta)
    twice = alpha_next * alpha
    steps, rows, _ = b.shape
    chunk = 64
    tall = (chunk // GROUP, GROUP, LANES)
    wide_along = jnp.broadcast_to(along, (GROUP, LANES))[None]
    wide_twice = jnp.broadcast_to(twice, (GROUP, LANES))[None]

    def copies(place):
        here = pl.ds(place * 2, 2)
        return (
            pltpu.make_async_copy(solution_v.at[here], solution_out.at[here], sems.at[0, place]),
            pltpu.make_async_copy(residual_v.at[here], residual_out.at[here], sems.at[1, place]),
        )

    def run(place, carry):
        for inner in range(2):
            step = place * 2 + inner
            for piece in range(rows // chunk):
                here = pl.ds(piece * chunk, chunk)
                first = b[step, here, :].reshape(tall)
                second = p[step, here, :].reshape(tall)
                third = q[step, here, :].reshape(tall)
                solution_v[step, here, :] = (wide_along * first - wide_twice * second).reshape(
                    chunk, LANES
                )
                residual_v[step, here, :] = (
                    first - wide_along * second + wide_twice * third
                ).reshape(chunk, LANES)
        for copy in copies(place):
            copy.start()
        return carry

    lax.fori_loop(0, steps // 2, run, 0)
    stations = along * own[...] - twice * unsorted[...]
    for step in range(steps):
        station_v[step, 0] = stations[step : step + 1]
    station_copy = pltpu.make_async_copy(station_v, station_out, station_sem)
    station_copy.start()

    def finish(place, carry):
        for copy in copies(place):
            copy.wait()
        return carry

    lax.fori_loop(0, steps // 2, finish, 0)
    station_copy.wait()


VMEM = pl.BlockSpec(memory_space=pltpu.VMEM)
SMEM = pl.BlockSpec(memory_space=pltpu.SMEM)
ANY = pl.BlockSpec(memory_space=pltpu.HBM)


def call(kernel, outs, ins, operands, scratch=(), flops=10**9, moved=10**7, limit=8, **extra):
    return pl.pallas_call(
        kernel,
        out_shape=outs,
        in_specs=ins,
        out_specs=[VMEM] * len(outs),
        scratch_shapes=list(scratch),
        compiler_params=pltpu.CompilerParams(vmem_limit_bytes=limit * 2**20),
        cost_estimate=pl.CostEstimate(flops=flops, bytes_accessed=moved, transcendentals=0),
        **extra,
    )(*operands)


def exchange(both, axis):
    count = lax.axis_size(axis)
    pairs = [[(i, i + 1) for i in range(start, count - 1, 2)] for start in (0, 1)]
    return tuple(
        lax.ppermute(both[place], axis, found + [(b, a) for a, b in found])
        for place, found in enumerate(pairs)
    )


def body(
    grid_obs, grid_noise, station_obs, station_noise, station_offset, station_cell,
    station_count, time_cov,
):
    steps, rows, cols = grid_obs.shape
    slots = station_obs.shape[3]
    wide = steps * GROUP
    groups = rows // GROUP
    tiles = 2 * (slots // LANES) + 1
    lanes = tiles * LANES
    devices = lax.axis_size("row") * lax.axis_size("col")
    shape = jax.ShapeDtypeStruct
    field = shape((steps, rows, cols), F32)
    rim = shape((2, steps, GROUP, cols), F32)
    strips_shape = shape((2, rows, wide), F32)
    station_field = shape((steps, GROUP, lanes), F32)
    extra = pltpu.VMEM((3, steps, GROUP, LANES), F32)
    (
        b, z_first, strips, sb, ordered, info, rank, own, sv, gv, spots,
        band_rows, band_cols, edge, bounds,
    ) = pl.pallas_call(
        prepare_kernel,
        out_shape=[
            field,
            field,
            strips_shape,
            station_field,
            shape((steps, slots), F32),
            shape((2, slots), F32),
            shape((1, slots), jnp.int32),
            shape((steps, slots), F32),
            shape((tiles, 2 * LANES, 2 * LANES), BF16),
            shape((tiles, 2 * LANES, 2 * LANES), BF16),
            shape((2, GROUP, lanes), F32),
            shape((rows, 3 * rows), BF16),
            shape((2 * LANES, 2 * LANES), BF16),
            shape((4, wide, wide), BF16),
            shape((groups, LANES), jnp.int32),
        ],
        in_specs=[SMEM] + [ANY] * 5,
        out_specs=[VMEM] * 14 + [SMEM],
        scratch_shapes=[
            pltpu.VMEM((1, 1, slots), jnp.int32),
            pltpu.VMEM((2, 1, 1, slots), F32),
            pltpu.VMEM((1, 1, slots), F32),
            pltpu.VMEM((steps, 1, 1, slots), F32),
            pltpu.VMEM((groups, LANES), jnp.int32),
            pltpu.VMEM((steps + 8, slots), F32),
            pltpu.VMEM((steps + 8, slots), F32),
            pltpu.VMEM((steps + 8, slots), F32),
            pltpu.SemaphoreType.DMA((6,)),
        ],
        compiler_params=pltpu.CompilerParams(vmem_limit_bytes=8 * 2**20),
        cost_estimate=pl.CostEstimate(flops=10**9, bytes_accessed=10**7, transcendentals=0),
    )(
        station_count,
        *(
            pltpu.with_memory_space_constraint(x, pltpu.HBM)
            for x in (station_cell, station_offset, station_noise, station_obs, grid_obs)
        ),
    )
    mix, mat = call(
        matrices_kernel,
        [shape((wide, 3 * wide), BF16), shape((4, wide, wide), BF16)],
        [VMEM],
        (time_cov,),
    )

    def smooth(z, strips, *more):
        from_left, from_right = exchange(strips, "col")
        u, u_edges, *unsorted = call(
            filter_unsort_kernel if more else first_filter_kernel,
            [field, rim] + [shape((steps, slots), F32)] * bool(more),
            [VMEM] * (3 + len(more)),
            (z, mix, band_cols, *more),
            [pltpu.VMEM((groups // 2, 2, wide, 2 * LANES), BF16)],
        )
        sides, full_edges = call(
            edge_kernel,
            [strips_shape, rim],
            [VMEM] * 5,
            (from_left, from_right, u_edges, mat, band_rows),
            limit=4,
        )
        above, below = exchange(full_edges, "row")
        (w,) = call(
            second_filter_kernel, [field], [VMEM] * 3, (u, sides, band_rows), limit=4
        )
        return w, above, below, *unsorted

    w, above, below = smooth(z_first, strips)
    p, z, strips, sums, flat_rows = call(
        image_one_kernel,
        [field, field, strips_shape, shape((GROUP, LANES), F32), shape((steps, slots), F32)],
        [SMEM] + [VMEM] * 11,
        (bounds, w, above, below, edge, grid_noise, b, ordered, info, spots, gv, sv),
        [
            pltpu.VMEM((steps, GROUP, lanes), F32),
            extra,
            pltpu.VMEM((steps, GROUP, lanes), F32),
            pltpu.VMEM((steps, lanes), F32),
            pltpu.VMEM((steps, slots), F32),
        ],
        limit=12,
    )
    w, above, below, unsorted = smooth(z, strips, flat_rows, rank)
    q, message = call(
        image_two_kernel,
        [field, shape((devices, LANES), F32)],
        [VMEM] * 13,
        (w, above, below, edge, grid_noise, b, p, z_first, z, ordered, flat_rows, info, sums),
        [extra],
        limit=4,
    )
    received = lax.all_to_all(message, ("row", "col"), 0, 0, tiled=True)
    solution_grid, residual_grid, solution_stations = pl.pallas_call(
        final_kernel,
        out_shape=[field, field, shape((steps, 1, 1, slots), F32)],
        in_specs=[VMEM] * 6,
        out_specs=[ANY, ANY, ANY],
        scratch_shapes=[
            pltpu.VMEM((steps, rows, cols), F32),
            pltpu.VMEM((steps, rows, cols), F32),
            pltpu.VMEM((steps, 1, 1, slots), F32),
            pltpu.SemaphoreType.DMA((2, steps // 2)),
            pltpu.SemaphoreType.DMA(()),
        ],
        compiler_params=pltpu.CompilerParams(vmem_limit_bytes=10 * 2**20),
    )(received, b, p, q, own, unsorted)
    return solution_grid, solution_stations, residual_grid


def solution(mesh):
    placed = (
        P(None, "row", "col"),
        P("row", "col"),
        P(None, "row", "col", None),
        P("row", "col", None),
        P(None, "row", "col", None),
        P("row", "col", None),
        P("row", "col"),
        P(),
    )
    return jax.shard_map(
        body,
        mesh=mesh,
        in_specs=placed,
        out_specs=(P(None, "row", "col"), P(None, "row", "col", None), P(None, "row", "col")),
        check_vma=False,
    )
```

```python
import functools

import jax
import jax.numpy as jnp
from jax import lax
from jax.experimental import pallas as pl
from jax.experimental.pallas import tpu as pltpu
from jax.sharding import PartitionSpec as P

REACH = 8
LANES = 128
HALF = LANES // 2
GROUP = 8
F32 = jnp.float32
BF16 = jnp.bfloat16
HIGHEST = lax.Precision.HIGHEST


def iota(shape, dim):
    return lax.broadcasted_iota(jnp.int32, shape, dim)


def taper(distance):
    spread = jnp.abs(distance).astype(F32)
    value = (1.0 - spread / (REACH + 1)) * jnp.exp(-spread / 3.0)
    return jnp.where(jnp.abs(distance) <= REACH, value, 0.0)


def split(x):
    high = x.astype(BF16)
    return high, (x - high.astype(F32)).astype(BF16)


def pair(x):
    high, low = split(x)
    return jnp.concatenate([high, low], axis=1)


def doubled(weights):
    high, low = split(weights)
    return jnp.concatenate(
        [
            jnp.concatenate([high, low], axis=1),
            jnp.concatenate([high, jnp.zeros_like(low)], axis=1),
        ],
        axis=0,
    )


def dot(a, b):
    return jnp.dot(a, b, preferred_element_type=F32)


def dot_nt(a, b):
    return lax.dot_general(a, b, (((1,), (1,)), ((), ())), preferred_element_type=F32)


def halves(x):
    width = x.shape[1] // 2
    return x[:, :width] + x[:, width:]


def three(x):
    high = x.astype(BF16)
    rest = x - high.astype(F32)
    middle = rest.astype(BF16)
    low = (rest - middle.astype(F32)).astype(BF16)
    return jnp.concatenate([high, middle, low], axis=0)


def cut(x, axis):
    return [
        lax.slice_in_dim(x, start, start + LANES, axis=axis)
        for start in range(0, x.shape[axis], LANES)
    ]


def slot_of(axis, side):
    odd = lax.rem(lax.axis_index(axis), 2)
    return odd if side else 1 - odd


def chunks(steps, size=GROUP):
    return [pl.ds(start, size) for start in range(0, steps, size)]


def shifted_block(source, block, blocks):
    here = source[:, pl.ds(block * LANES, LANES)]
    after = jnp.zeros_like(here)
    if block + 1 < blocks:
        after = source[:, pl.ds((block + 1) * LANES, LANES)]
    return pltpu.roll(jnp.where(iota(here.shape, 1) < HALF, after, here), HALF, 1)


def spread_rows(even, odd, target, steps, blocks):
    for tile in range(2 * blocks):
        source = odd if tile % 2 else even
        place = pl.ds(tile // 2 * LANES, LANES)
        for step in range(steps):
            target[step, :, pl.ds(tile * LANES, LANES)] = jnp.broadcast_to(
                source[pl.ds(step, 1), place], (GROUP, LANES)
            )


def rows_of(g):
    return pl.ds(pl.multiple_of(g * GROUP, GROUP), GROUP)


def prepare_kernel(
    count, cell_any, offset_any, noise_any, obs_any, base_any,
    base, z, strips, sb, ordered, info, rank_out, own, sv, gv, spots,
    band_rows, band_cols, edge, bounds,
    cell_v, offset_v, noise_v, obs_v, bounds_v, table, sorted_rows, shifted_rows, copies,
):
    small = [
        pltpu.make_async_copy(source, target, copies.at[1 + place])
        for place, (source, target) in enumerate(
            ((cell_any, cell_v), (offset_any, offset_v), (noise_any, noise_v), (obs_any, obs_v))
        )
    ]
    for copy in small:
        copy.start()
    base_copy = pltpu.make_async_copy(base_any, base, copies.at[0])
    base_copy.start()
    fixed_matrices(band_rows, band_cols, edge)
    for copy in small:
        copy.wait()
    cell, noise = cell_v[0], noise_v[0]
    steps, slots = own.shape
    tiles = slots // LANES
    rows = base.shape[1]
    groups = rows // GROUP
    slot = iota((1, slots), 1)
    live = slot < count[0, 0]
    where_row = cell // LANES
    where_col = cell - where_row * LANES
    key = jnp.where(live, where_row, rows) * slots + slot
    key = key.astype(F32)
    total = jnp.zeros((1, slots), F32)
    for block in range(tiles):
        piece = key[:, block * LANES : (block + 1) * LANES]
        column = jnp.transpose(jnp.broadcast_to(piece, (LANES, LANES)))
        column = jnp.concatenate([column] * tiles, axis=1)
        less = jnp.where(column < key, 1.0, 0.0)
        total = total + jnp.sum(less, axis=0, keepdims=True)
    rank = total.astype(jnp.int32)
    rank_out[...] = rank
    lived = jnp.where(live, 1.0, 0.0)
    for step in range(steps):
        own[pl.ds(step, 1), :] = obs_v[step, 0] * lived
    table[pl.ds(0, steps), :] = own[...]
    table[pl.ds(steps, 1), :] = where_row.astype(F32)
    table[pl.ds(steps + 1, 1), :] = where_col.astype(F32)
    table[pl.ds(steps + 2, 1), :] = offset_v[0, 0]
    table[pl.ds(steps + 3, 1), :] = offset_v[1, 0]
    table[pl.ds(steps + 4, 1), :] = noise
    table[pl.ds(steps + 5, 1), :] = lived
    table[pl.ds(steps + 6, 2), :] = jnp.zeros((2, slots), F32)
    pieces = three(table[...])
    height = table.shape[0]

    def sort_block(block, carry):
        start = pl.multiple_of(block * LANES, LANES)
        order = (iota((LANES, slots), 0) + start == rank).astype(F32).astype(BF16)
        out = dot_nt(pieces, order)
        sorted_rows[:, pl.ds(start, LANES)] = (
            out[:height] + out[height : 2 * height] + out[2 * height :]
        )
        return carry

    lax.fori_loop(0, tiles, sort_block, 0, unroll=8)
    ordered_row = sorted_rows[pl.ds(steps, 1), :]
    ordered_live = sorted_rows[pl.ds(steps + 5, 1), :]
    first_row = (iota((groups, slots), 0) * GROUP).astype(F32)
    before = jnp.where(ordered_row < first_row - 1.0, ordered_live, 0.0)
    until = jnp.where(ordered_row < first_row + GROUP, ordered_live, 0.0)
    low = jnp.sum(before, axis=1, keepdims=True)
    high = jnp.sum(until, axis=1, keepdims=True)
    start_tile = jnp.where(high > low, jnp.floor(low * (1.0 / HALF)), float(2 * tiles))
    reached = jnp.where(high > low, high - HALF * start_tile, 1.0)
    needed = jnp.floor((reached + (LANES - 1.0)) * (1.0 / LANES))
    most = jnp.max(needed, axis=0, keepdims=True)
    lane = iota((groups, LANES), 1)
    bounds_v[...] = jnp.where(
        lane == 0, start_tile, jnp.where(lane == 1, needed, most)
    ).astype(jnp.int32)
    bounds_copy = pltpu.make_async_copy(bounds_v, bounds, copies.at[5])
    bounds_copy.start()
    ordered[...] = sorted_rows[pl.ds(0, steps), :]
    alive = sorted_rows[pl.ds(steps + 5, 1), :]
    info[pl.ds(0, 1), :] = alive * sorted_rows[pl.ds(steps + 4, 1), :] + (1.0 - alive)
    info[pl.ds(1, 1), :] = alive
    for block in range(tiles):
        shifted_rows[:, pl.ds(block * LANES, LANES)] = shifted_block(sorted_rows, block, tiles)
    none = tile_lanes(2 * tiles, 1)
    sb[:, :, none] = jnp.zeros((steps, GROUP, LANES), F32)
    spots[:, :, none] = jnp.full((2, GROUP, LANES), -1000.0, F32)
    for target in (sv, gv):
        target[2 * tiles] = jnp.zeros((2 * LANES, 2 * LANES), BF16)
    spread_rows(sorted_rows, shifted_rows, sb, steps, tiles)
    for tile in range(2 * tiles):
        source = shifted_rows if tile % 2 else sorted_rows
        place = pl.ds(tile // 2 * LANES, LANES)
        lanes = pl.ds(tile * LANES, LANES)
        spots[0, :, lanes] = jnp.broadcast_to(source[pl.ds(steps, 1), place], (GROUP, LANES))
        spots[1, :, lanes] = jnp.broadcast_to(source[pl.ds(steps + 2, 1), place], (GROUP, LANES))
        at_col = source[pl.ds(steps + 1, 1), place].astype(jnp.int32)
        along_col = source[pl.ds(steps + 3, 1), place]
        col = iota((LANES, LANES), 0)
        across = jnp.where(
            col == at_col, 1.0 - along_col, jnp.where(col == at_col + 1, along_col, 0.0)
        )
        gv[tile] = doubled(across)
        if tile % 2 == 0:
            sv[tile] = doubled(jnp.transpose(across))
    for tile in range(1, 2 * tiles, 2):
        for start in (0, LANES):
            sv[tile, pl.ds(start, HALF), :] = sv[tile - 1, pl.ds(start + HALF, HALF), :]
            sv[tile, pl.ds(start + HALF, HALF), :] = sv[tile + 1, pl.ds(start, HALF), :]
    bounds_copy.wait()
    base_copy.wait()
    scatter_all(base, z, strips, sb, spots, sv, bounds)


def matrices_kernel(cov, mix, mat):
    steps = cov.shape[0]
    wide = steps * GROUP
    spread = (iota((wide, steps), 0) // GROUP == iota((wide, steps), 1)).astype(F32)
    spread_t = (iota((steps, wide), 1) // GROUP == iota((steps, wide), 0)).astype(F32)
    expanded = jnp.dot(
        jnp.dot(spread, cov[...], precision=HIGHEST, preferred_element_type=F32),
        spread_t,
        precision=HIGHEST,
        preferred_element_type=F32,
    )
    a = iota((wide, wide), 0)
    b = iota((wide, wide), 1)
    same = (a % GROUP) == (b % GROUP)
    high_part, low_part = split(jnp.where(same, expanded, 0.0))
    mix[...] = jnp.concatenate([high_part, high_part, low_part], axis=1)
    near = taper((b % GROUP) + REACH - (a % GROUP)) * expanded
    near = jnp.concatenate(
        [jnp.concatenate([x[GROUP:], x[:GROUP]], axis=0) for x in cut(near, 0)], axis=0
    )
    mat[0], mat[1] = split(near)
    far = taper(REACH + (a % GROUP) - (b % GROUP)) * expanded
    far = jnp.concatenate(
        [pltpu.roll(x, LANES - GROUP, 1) for x in cut(far, 1)], axis=1
    )
    mat[2], mat[3] = split(far)


def fixed_matrices(band_rows, band_cols, edge):
    rows = band_rows.shape[0]
    wide = edge.shape[1]
    a = iota((wide, wide), 0)
    b = iota((wide, wide), 1)
    ra = iota((rows, rows), 0)
    rb = iota((rows, rows), 1)
    high_part, low_part = split(0.25 * taper(ra - rb))
    band_rows[...] = jnp.concatenate([high_part, high_part, low_part], axis=1)
    ca = iota((LANES, LANES), 0)
    cb = iota((LANES, LANES), 1)
    band_cols[...] = doubled(taper(ca - cb))
    block_same = (a // GROUP) == (b // GROUP)
    above = 0.25 * taper((a % GROUP) + REACH - (b % GROUP))
    below = 0.25 * taper(REACH + (b % GROUP) - (a % GROUP))
    edge[0], edge[1] = split(jnp.where(block_same, above, 0.0))
    edge[2], edge[3] = split(jnp.where(block_same, below, 0.0))


def tile_lanes(index, count):
    return pl.ds(pl.multiple_of(index * LANES, LANES), count * LANES)


def row_weights(g, lanes, spots):
    row = (iota((GROUP, LANES), 0) + g * GROUP).astype(F32)
    offset = row - spots[0, :, lanes]
    along = spots[1, :, lanes]
    return jnp.where(offset == 0.0, 1.0 - along, jnp.where(offset == 1.0, along, 0.0))[None]


def spread_tile(g, index, sb, spots, sv):
    steps = sb.shape[0]
    lanes = tile_lanes(index, 1)
    weight = row_weights(g, lanes, spots)
    left = jnp.concatenate(
        [
            pair((sb[times, :, lanes] * weight).reshape(GROUP * GROUP, LANES))
            for times in chunks(steps)
        ],
        axis=0,
    )
    return halves(dot(left, sv[index])).reshape(steps, GROUP, LANES)


def scatter_all(base, z, strips, sb, spots, sv, bounds):
    groups = base.shape[1] // GROUP

    def run(g, carry):
        value = base[:, rows_of(g), :] + spread_tile(g, bounds[g, 0], sb, spots, sv)
        z[:, rows_of(g), :] = value
        pack_group(g, value, strips)
        return carry

    lax.fori_loop(0, groups, run, 0, unroll=32)

    @pl.when(bounds[0, 2] > 1)
    def _():
        def crowded(g, carry):
            def more(index, inner):
                z[:, rows_of(g), :] += spread_tile(g, bounds[g, 0] + 2 * index, sb, spots, sv)
                return inner

            lax.fori_loop(1, bounds[g, 1], more, 0)
            pack_group(g, z[:, rows_of(g), :], strips)
            return carry

        lax.fori_loop(0, groups, crowded, 0)


def pack_group(g, value, strips):
    steps = value.shape[0]
    per = LANES // GROUP
    slot = iota((GROUP, LANES), 1) // GROUP
    for half in range(steps // per):
        left = jnp.zeros((GROUP, LANES), F32)
        right = jnp.zeros((GROUP, LANES), F32)
        for local in range(per):
            moved = value[half * per + local]
            if local:
                moved = pltpu.roll(moved, local * GROUP, 1)
            left = jnp.where(slot == local, moved, left)
            right = jnp.where(slot == (local - 1) % per, moved, right)
        lanes = pl.ds(half * LANES, LANES)
        strips[slot_of("col", 0), rows_of(g), lanes] = left
        strips[slot_of("col", 1), rows_of(g), lanes] = right


def unpack(sides, where_rows, count, step):
    per = LANES // GROUP
    half, local = step // per, step % per
    lane = iota((count, LANES), 1)
    lanes = pl.ds(half * LANES, LANES) if isinstance(step, int) else tile_lanes(half, 1)
    both = jnp.where(lane // GROUP == local, sides[0, where_rows, lanes], sides[1, where_rows, lanes])
    both = pltpu.roll(both, (LANES - local * GROUP) % LANES, 1)
    return jnp.where((lane < GROUP) | (lane >= LANES - GROUP), both, 0.0)


def first_filter_kernel(z, mix, band_cols, u, u_edges, y):
    steps, rows, cols = z.shape
    groups = rows // GROUP
    flat = (steps * GROUP, LANES)

    def across(quad, carry):
        parts = [z[:, rows_of(4 * quad + i), :].reshape(flat) for i in range(4)]
        value = halves(dot(pair(jnp.concatenate(parts, axis=0)), band_cols[...]))
        both = split(value)
        for i in range(4):
            for part in range(2):
                y[2 * quad + i // 2, part, :, pl.ds((i % 2) * LANES, LANES)] = both[part][
                    i * flat[0] : (i + 1) * flat[0]
                ]
        return carry

    lax.fori_loop(0, groups // 4, across, 0, unroll=8)

    def mixing(two, carry):
        right = jnp.concatenate([y[two, 0], y[two, 1], y[two, 0]], axis=0)
        out = dot(mix[...], right)
        u[:, rows_of(2 * two), :] = out[:, :LANES].reshape(steps, GROUP, LANES)
        u[:, rows_of(2 * two + 1), :] = out[:, LANES:].reshape(steps, GROUP, LANES)
        return carry

    lax.fori_loop(0, groups // 2, mixing, 0, unroll=16)
    u_edges[0] = u[:, pl.ds(0, GROUP), :]
    u_edges[1] = u[:, pl.ds(rows - GROUP, GROUP), :]


def filter_unsort_kernel(z, mix, band_cols, flat_rows, rank, u, u_edges, unsorted, y):
    first_filter_kernel(z, mix, band_cols, u, u_edges, y)
    steps, slots = flat_rows.shape
    tiles = slots // LANES
    pieces = three(flat_rows[...])

    def unsort_block(block, carry):
        lanes = tile_lanes(block, 1)
        order = (iota((slots, LANES), 0) == rank[:, lanes]).astype(F32).astype(BF16)
        out = dot(pieces, order)
        unsorted[:, lanes] = out[:steps] + out[steps : 2 * steps] + out[2 * steps :]
        return carry

    lax.fori_loop(0, tiles, unsort_block, 0, unroll=8)


def second_filter_kernel(u, sides, band_rows, w):
    steps, rows, cols = u.shape

    def along(two, carry):
        one = split(u[2 * two])
        other = split(u[2 * two + 1])
        high = jnp.concatenate([one[0], other[0]], axis=1)
        low = jnp.concatenate([one[1], other[1]], axis=1)
        out = dot(band_rows[...], jnp.concatenate([high, low, high], axis=0))
        everything = pl.ds(0, rows)
        w[2 * two] = out[:, :LANES] + unpack(sides, everything, rows, 2 * two)
        w[2 * two + 1] = out[:, LANES:] + unpack(sides, everything, rows, 2 * two + 1)
        return carry

    lax.fori_loop(0, steps // 2, along, 0, unroll=16)


def edge_kernel(first, second, u_edges, mat, band_rows, sides, full_edges):
    steps = u_edges.shape[1]
    rows = first.shape[0]
    for place, source in ((0, first), (1, second)):
        side = slot_of("col", place)
        high, low = split(source[...])
        value = dot(high, mat[2 * side]) + dot(low, mat[2 * side])
        value = value + dot(high, mat[2 * side + 1])
        sides[side] = value
    for which, start in ((0, 0), (1, rows - GROUP)):
        slot = slot_of("row", which)
        for step in range(steps):
            full_edges[slot, step] = u_edges[which, step] + unpack(
                sides, pl.ds(start, GROUP), GROUP, step
            )
    for side in range(2):
        high, low = split(sides[side])
        sides[side] = dot(band_rows[...], jnp.concatenate([high, low, high], axis=0))


def fill_extra(extra, first, second, edge):
    steps = first.shape[0]
    flat = (steps * GROUP, LANES)
    for place, source in ((0, first), (1, second)):
        which = slot_of("row", place)
        both = pair(source[...].reshape(flat))
        value = halves(dot(edge[2 * which], both)) + dot(edge[2 * which + 1], both[:, :LANES])
        extra[which] = value.reshape(steps, GROUP, LANES)
    extra[2] = jnp.zeros((steps, GROUP, LANES), F32)


def which_extra(g, groups):
    return jnp.where(g == 0, 0, jnp.where(g == groups - 1, 1, 2))


def gather_tile(g, both, index, acc, spots, gv):
    steps = acc.shape[0]
    lanes = tile_lanes(index, 1)
    out = halves(dot(both, gv[index])).reshape(steps, GROUP, LANES)
    weight = row_weights(g, lanes, spots)
    for times in chunks(steps):
        acc[times, :, lanes] += out[times.start : times.start + times.size] * weight


def whole(x):
    return jnp.sum(jnp.sum(x, axis=1, keepdims=True), axis=0, keepdims=True)


def fold(x):
    return jnp.sum(x, axis=0)


def fold_flat(x):
    return fold(x.reshape(x.shape[0] // GROUP, GROUP, LANES))


def image_one_kernel(
    bounds, w, above, below, edge, noise, b, ordered, info, spots, gv, sv,
    p, z, strips, sums, flat_rows, acc, extra, ps, compact, shifted,
):
    steps, rows, _ = w.shape
    groups = rows // GROUP
    tiles = info.shape[1] // LANES
    fill_extra(extra, above, below, edge)
    acc[...] = jnp.zeros_like(acc)

    def run(g, carry):
        here = rows_of(g)
        which = which_extra(g, groups)
        spread = noise[here, :][None]
        first, second, third = carry
        left = []
        for times in chunks(steps):
            value = w[times, here, :] + extra[which, times]
            left.append(pair(value.reshape(GROUP * GROUP, LANES)))
            mine = b[times, here, :]
            image = value + spread * mine
            p[times, here, :] = image
            first = first + fold(mine * mine)
            second = second + fold(mine * image)
            third = third + fold(image * image)
        gather_tile(g, jnp.concatenate(left, axis=0), bounds[g, 0], acc, spots, gv)
        return first, second, third

    zero = jnp.zeros((GROUP, LANES), F32)
    carry = lax.fori_loop(0, groups, run, (zero,) * 3, unroll=16)

    @pl.when(bounds[0, 2] > 1)
    def _():
        def crowded(g, inner):
            value = w[:, rows_of(g), :] + extra[which_extra(g, groups)]
            both = pair(value.reshape(steps * GROUP, LANES))

            def more(index, innermost):
                gather_tile(g, both, bounds[g, 0] + 2 * index, acc, spots, gv)
                return innermost

            return lax.fori_loop(1, bounds[g, 1], more, inner)

        lax.fori_loop(0, groups, crowded, 0)

    wide = steps * GROUP
    adds = (iota((steps, 2 * wide), 1) % wide // GROUP == iota((steps, 2 * wide), 0)).astype(F32)
    adds = adds.astype(BF16)

    def fold_rows(index, inner):
        lanes = tile_lanes(2 * index, 2)
        high, low = split(acc[:, :, lanes].reshape(wide, 2 * LANES))
        compact[:, lanes] = dot(adds, jnp.concatenate([high, low], axis=0))
        return inner

    lax.fori_loop(0, tiles, fold_rows, 0)
    lane = iota((steps, LANES), 1)
    first, second, third = carry
    for block in range(tiles):
        place = pl.ds(block * LANES, LANES)
        before = jnp.zeros((steps, LANES), F32)
        if block:
            before = compact[:, pl.ds((2 * block - 1) * LANES, LANES)]
        after = compact[:, pl.ds((2 * block + 1) * LANES, LANES)]
        sampled = compact[:, pl.ds(2 * block * LANES, LANES)] + pltpu.roll(
            jnp.where(lane < HALF, after, before), HALF, 1
        )
        mine = ordered[:, place]
        image = info[pl.ds(1, 1), place] * sampled + info[pl.ds(0, 1), place] * mine
        flat_rows[:, place] = image
        first = first + fold_flat(mine * mine)
        second = second + fold_flat(mine * image)
        third = third + fold_flat(image * image)
    carry = first, second, third
    for block in range(tiles):
        shifted[:, pl.ds(block * LANES, LANES)] = shifted_block(flat_rows, block, tiles)
    ps[:, :, tile_lanes(2 * tiles, 1)] = jnp.zeros((steps, GROUP, LANES), F32)
    spread_rows(flat_rows, shifted, ps, steps, tiles)
    bb, bp, pp = (whole(x) for x in carry)
    lane = iota((GROUP, LANES), 1)
    value = jnp.where(lane == 0, bb / bp, 0.0)
    value = jnp.where(lane == 1, bb, value)
    value = jnp.where(lane == 2, bp, value)
    value = jnp.where(lane == 3, pp, value)
    sums[...] = value
    scatter_all(p, z, strips, ps, spots, sv, bounds)


def image_two_kernel(
    w, above, below, edge, noise, b, p, z_first, z, ordered, flat_rows, info, sums,
    q, message, extra,
):
    steps, rows, _ = w.shape
    groups = rows // GROUP
    tiles = info.shape[1] // LANES
    fill_extra(extra, above, below, edge)
    shift = jnp.broadcast_to(sums[0:1, 0:1], (GROUP, LANES))[None]

    def run(g, carry):
        here = rows_of(g)
        which = which_extra(g, groups)
        spread = noise[here, :][None]
        first, second, third = carry
        for times in chunks(steps, 4):
            value = w[times, here, :] + extra[which, times]
            mine = p[times, here, :]
            scaled = spread * mine
            q[times, here, :] = value + scaled
            residual = b[times, here, :] - shift * mine
            image = z[times, here, :]
            moved = z_first[times, here, :] - shift * image
            first = first + fold(residual * residual)
            second = second + fold(moved * value + residual * scaled)
            third = third + fold(image * value + mine * scaled)
        return first, second, third

    zero = jnp.zeros((GROUP, LANES), F32)
    carry = lax.fori_loop(0, groups, run, (zero,) * 3, unroll=8)

    first, second, third = carry
    own_shift = sums[0:1, 0:1]
    for block in range(tiles):
        place = pl.ds(block * LANES, LANES)
        mine = flat_rows[:, place]
        scaled = info[pl.ds(0, 1), place] * mine
        residual = ordered[:, place] - own_shift * mine
        first = first + fold_flat(residual * residual)
        second = second + fold_flat(residual * scaled)
        third = third + fold_flat(mine * scaled)
    carry = first, second, third
    lane = iota((1, LANES), 1)
    value = jnp.where(lane < 4, sums[0:1, :], 0.0)
    for place, x in enumerate(carry):
        value = jnp.where(lane == 4 + place, whole(x), value)
    message[...] = jnp.broadcast_to(value, message.shape)


def final_kernel(
    received, b, p, q, own, unsorted, solution_out, residual_out, station_out,
    solution_v, residual_v, station_v, sems, station_sem,
):
    everything = received[...]

    def column(index):
        return everything[:, index : index + 1]

    def total(x):
        return jnp.sum(x, axis=0, keepdims=True)

    shift, bb, bp, pp = (column(i) for i in range(4))
    rr, rq, pq = (column(i) for i in range(4, 7))
    norm = total(bb)
    alpha = norm / total(bp)
    delta = shift - alpha
    rp = bp - shift * pp
    ru = rp - shift * rq
    pu = pp - shift * pq
    norm_next = total(rr + 2.0 * delta * rp + delta * delta * pp)
    energy = total(ru + delta * (rq + pu) + delta * delta * pq)
    beta = norm_next / norm
    alpha_next = norm_next / (energy - beta * norm_next / alpha)
    along = alpha + alpha_next * (1.0 + beta)
    twice = alpha_next * alpha
    steps, rows, _ = b.shape
    chunk = 64
    tall = (chunk // GROUP, GROUP, LANES)
    wide_along = jnp.broadcast_to(along, (GROUP, LANES))[None]
    wide_twice = jnp.broadcast_to(twice, (GROUP, LANES))[None]

    def copies(place):
        here = pl.ds(place * 2, 2)
        return (
            pltpu.make_async_copy(solution_v.at[here], solution_out.at[here], sems.at[0, place]),
            pltpu.make_async_copy(residual_v.at[here], residual_out.at[here], sems.at[1, place]),
        )

    def run(place, carry):
        for inner in range(2):
            step = place * 2 + inner
            for piece in range(rows // chunk):
                here = pl.ds(piece * chunk, chunk)
                first = b[step, here, :].reshape(tall)
                second = p[step, here, :].reshape(tall)
                third = q[step, here, :].reshape(tall)
                solution_v[step, here, :] = (wide_along * first - wide_twice * second).reshape(
                    chunk, LANES
                )
                residual_v[step, here, :] = (
                    first - wide_along * second + wide_twice * third
                ).reshape(chunk, LANES)
        for copy in copies(place):
            copy.start()
        return carry

    lax.fori_loop(0, steps // 2, run, 0)
    stations = along * own[...] - twice * unsorted[...]
    for step in range(steps):
        station_v[step, 0] = stations[step : step + 1]
    station_copy = pltpu.make_async_copy(station_v, station_out, station_sem)
    station_copy.start()

    def finish(place, carry):
        for copy in copies(place):
            copy.wait()
        return carry

    lax.fori_loop(0, steps // 2, finish, 0)
    station_copy.wait()


VMEM = pl.BlockSpec(memory_space=pltpu.VMEM)
SMEM = pl.BlockSpec(memory_space=pltpu.SMEM)
ANY = pl.BlockSpec(memory_space=pltpu.HBM)


def call(kernel, outs, ins, operands, scratch=(), flops=10**9, moved=10**7, limit=8, **extra):
    return pl.pallas_call(
        kernel,
        out_shape=outs,
        in_specs=ins,
        out_specs=[VMEM] * len(outs),
        scratch_shapes=list(scratch),
        compiler_params=pltpu.CompilerParams(vmem_limit_bytes=limit * 2**20),
        cost_estimate=pl.CostEstimate(flops=flops, bytes_accessed=moved, transcendentals=0),
        **extra,
    )(*operands)


def exchange(both, axis):
    count = lax.axis_size(axis)
    pairs = [[(i, i + 1) for i in range(start, count - 1, 2)] for start in (0, 1)]
    return tuple(
        lax.ppermute(both[place], axis, found + [(b, a) for a, b in found])
        for place, found in enumerate(pairs)
    )


def body(
    grid_obs, grid_noise, station_obs, station_noise, station_offset, station_cell,
    station_count, time_cov,
):
    steps, rows, cols = grid_obs.shape
    slots = station_obs.shape[3]
    wide = steps * GROUP
    groups = rows // GROUP
    tiles = 2 * (slots // LANES) + 1
    lanes = tiles * LANES
    devices = lax.axis_size("row") * lax.axis_size("col")
    shape = jax.ShapeDtypeStruct
    field = shape((steps, rows, cols), F32)
    rim = shape((2, steps, GROUP, cols), F32)
    strips_shape = shape((2, rows, wide), F32)
    station_field = shape((steps, GROUP, lanes), F32)
    extra = pltpu.VMEM((3, steps, GROUP, LANES), F32)
    (
        b, z_first, strips, sb, ordered, info, rank, own, sv, gv, spots,
        band_rows, band_cols, edge, bounds,
    ) = pl.pallas_call(
        prepare_kernel,
        out_shape=[
            field,
            field,
            strips_shape,
            station_field,
            shape((steps, slots), F32),
            shape((2, slots), F32),
            shape((1, slots), jnp.int32),
            shape((steps, slots), F32),
            shape((tiles, 2 * LANES, 2 * LANES), BF16),
            shape((tiles, 2 * LANES, 2 * LANES), BF16),
            shape((2, GROUP, lanes), F32),
            shape((rows, 3 * rows), BF16),
            shape((2 * LANES, 2 * LANES), BF16),
            shape((4, wide, wide), BF16),
            shape((groups, LANES), jnp.int32),
        ],
        in_specs=[SMEM] + [ANY] * 5,
        out_specs=[VMEM] * 14 + [SMEM],
        scratch_shapes=[
            pltpu.VMEM((1, 1, slots), jnp.int32),
            pltpu.VMEM((2, 1, 1, slots), F32),
            pltpu.VMEM((1, 1, slots), F32),
            pltpu.VMEM((steps, 1, 1, slots), F32),
            pltpu.VMEM((groups, LANES), jnp.int32),
            pltpu.VMEM((steps + 8, slots), F32),
            pltpu.VMEM((steps + 8, slots), F32),
            pltpu.VMEM((steps + 8, slots), F32),
            pltpu.SemaphoreType.DMA((6,)),
        ],
        compiler_params=pltpu.CompilerParams(vmem_limit_bytes=8 * 2**20),
        cost_estimate=pl.CostEstimate(flops=10**9, bytes_accessed=10**7, transcendentals=0),
    )(
        station_count,
        *(
            pltpu.with_memory_space_constraint(x, pltpu.HBM)
            for x in (station_cell, station_offset, station_noise, station_obs, grid_obs)
        ),
    )
    mix, mat = call(
        matrices_kernel,
        [shape((wide, 3 * wide), BF16), shape((4, wide, wide), BF16)],
        [VMEM],
        (time_cov,),
    )

    def smooth(z, strips, *more):
        from_left, from_right = exchange(strips, "col")
        u, u_edges, *unsorted = call(
            filter_unsort_kernel if more else first_filter_kernel,
            [field, rim] + [shape((steps, slots), F32)] * bool(more),
            [VMEM] * (3 + len(more)),
            (z, mix, band_cols, *more),
            [pltpu.VMEM((groups // 2, 2, wide, 2 * LANES), BF16)],
        )
        sides, full_edges = call(
            edge_kernel,
            [strips_shape, rim],
            [VMEM] * 5,
            (from_left, from_right, u_edges, mat, band_rows),
            limit=4,
        )
        above, below = exchange(full_edges, "row")
        (w,) = call(
            second_filter_kernel, [field], [VMEM] * 3, (u, sides, band_rows), limit=4
        )
        return w, above, below, *unsorted

    w, above, below = smooth(z_first, strips)
    p, z, strips, sums, flat_rows = call(
        image_one_kernel,
        [field, field, strips_shape, shape((GROUP, LANES), F32), shape((steps, slots), F32)],
        [SMEM] + [VMEM] * 11,
        (bounds, w, above, below, edge, grid_noise, b, ordered, info, spots, gv, sv),
        [
            pltpu.VMEM((steps, GROUP, lanes), F32),
            extra,
            pltpu.VMEM((steps, GROUP, lanes), F32),
            pltpu.VMEM((steps, lanes), F32),
            pltpu.VMEM((steps, slots), F32),
        ],
        limit=12,
    )
    w, above, below, unsorted = smooth(z, strips, flat_rows, rank)
    q, message = call(
        image_two_kernel,
        [field, shape((devices, LANES), F32)],
        [VMEM] * 13,
        (w, above, below, edge, grid_noise, b, p, z_first, z, ordered, flat_rows, info, sums),
        [extra],
        limit=4,
    )
    received = lax.all_to_all(message, ("row", "col"), 0, 0, tiled=True)
    solution_grid, residual_grid, solution_stations = pl.pallas_call(
        final_kernel,
        out_shape=[field, field, shape((steps, 1, 1, slots), F32)],
        in_specs=[VMEM] * 6,
        out_specs=[ANY, ANY, ANY],
        scratch_shapes=[
            pltpu.VMEM((steps, rows, cols), F32),
            pltpu.VMEM((steps, rows, cols), F32),
            pltpu.VMEM((steps, 1, 1, slots), F32),
            pltpu.SemaphoreType.DMA((2, steps // 2)),
            pltpu.SemaphoreType.DMA(()),
        ],
        compiler_params=pltpu.CompilerParams(vmem_limit_bytes=10 * 2**20),
    )(received, b, p, q, own, unsorted)
    return solution_grid, solution_stations, residual_grid


def solution(mesh):
    placed = (
        P(None, "row", "col"),
        P("row", "col"),
        P(None, "row", "col", None),
        P("row", "col", None),
        P(None, "row", "col", None),
        P("row", "col", None),
        P("row", "col"),
        P(),
    )
    return jax.shard_map(
        body,
        mesh=mesh,
        in_specs=placed,
        out_specs=(P(None, "row", "col"), P(None, "row", "col", None), P(None, "row", "col")),
        check_vma=False,
    )
```
